32 devices in a mesh: seq: 4 (over y, x), ctx: 2 (over core), wsh: 4 (over z).
Axes of the slice: x: 2, y: 2, z: 4, core: 2. Of those that a mesh axis runs over, the one named last changes fastest.
Arguments:
- tokens: bfloat16 [4, 2048, 768], P('seq', ('ctx', 'wsh')), may hold values from -6 to 6
- segment_ids: int32 [4, 2048], P('seq', ('ctx', 'wsh')), may hold values from 0 to 15, never falling along the last dimension, each value on 1 to 1536 neighbouring positions
- w_query: bfloat16 [768, 768], P('wsh'), may hold values from -0.21875 to 0.21875
- b_query: bfloat16 [768], P('wsh'), may hold values from -3 to 3
- w_key: bfloat16 [768, 768], P('wsh'), may hold values from -0.21875 to 0.21875
- w_value: bfloat16 [768, 768], P('wsh'), may hold values from -0.21875 to 0.21875
- b_value: bfloat16 [768], P('wsh'), may hold values from -3 to 3
- w_out: bfloat16 [768, 768], P('wsh'), may hold values from -0.875 to 0.875
- b_out: bfloat16 [768], P('wsh'), may hold values from -3 to 3
- gain_attn: bfloat16 [768], P('wsh'), may hold values from 0.5 to 1.5
- shift_attn: bfloat16 [768], P('wsh'), may hold values from -3 to 3
- w_in: bfloat16 [768, 3072], P('wsh'), may hold values from -0.21875 to 0.21875
- b_in: bfloat16 [3072], P('wsh'), may hold values from -3 to 3
- w_down: bfloat16 [3072, 768], P('wsh'), may hold values from -0.109375 to 0.109375
- b_down: bfloat16 [768], P('wsh'), may hold values from -3 to 3
- gain_ffn: bfloat16 [768], P('wsh'), may hold values from 0.5 to 1.5
- shift_ffn: bfloat16 [768], P('wsh'), may hold values from -3 to 3
- cotangent: bfloat16 [4, 2048, 768], P('seq', ('ctx', 'wsh')), may hold values from -6 to 6
Outputs:
- output: bfloat16 [4, 2048, 768], P('seq', ('ctx', 'wsh'))
- grad_tokens: bfloat16 [4, 2048, 768], P('seq', ('ctx', 'wsh'))
- grad_w_query: float32 [768, 768], P('wsh')
- grad_b_query: float32 [768], P('wsh')
- grad_w_key: float32 [768, 768], P('wsh')
- grad_w_value: float32 [768, 768], P('wsh')
- grad_b_value: float32 [768], P('wsh')
- grad_w_out: float32 [768, 768], P('wsh')
- grad_b_out: float32 [768], P('wsh')
- grad_gain_attn: float32 [768], P('wsh')
- grad_shift_attn: float32 [768], P('wsh')
- grad_w_in: float32 [768, 3072], P('wsh')
- grad_b_in: float32 [3072], P('wsh')
- grad_w_down: float32 [3072, 768], P('wsh')
- grad_b_down: float32 [768], P('wsh')
- grad_gain_ffn: float32 [768], P('wsh')
- grad_shift_ffn: float32 [768], P('wsh')
The draws below stay inside these ranges and needn't reach their ends.
Inputs may be any that keep to these rules, and one draw needn't show every extreme that they name: `segment_ids`: within a sequence the ids never fall from one position to the next; each of the 16 documents holds 1 to 1536 positions and one holds exactly 1536.
All inputs are finite; a program needn't handle non-finite values.
Results may differ from the reference program's by a relative error of at most 0.02.
Values may be sent and summed in bfloat16 or wider, within the bound.
A program may use at most 320 MiB of HBM per device.

```python
import math
import jax
import jax.numpy as jnp
import numpy as np
from jax import lax

D = 768
HEADS = 12
FF = 3072
LENGTH = 2048
SEQS = 4
DOCS = 16
MOST = 1536


def steps_of(own_key, shape, cuts, least, high):
    def one(position, blocks):
        draws = jax.random.uniform(jax.random.fold_in(jax.random.fold_in(own_key, 6), position), (blocks,), jnp.float32, least / len(cuts), high / len(cuts))
        return jnp.repeat(jnp.exp(draws), shape[position] // blocks).reshape((-1,) + (1,) * (len(shape) - position - 1))

    factor_of = one(*cuts[0])
    for cut in cuts[1:]:
        factor_of = factor_of * one(*cut)
    return factor_of


def length_profile(amount, total, reach, skew):
    portions = [(1 << 20) // math.isqrt(rank ** skew) + 1 for rank in range(2, amount + 1)]
    rest, holding = total - reach - (amount - 1), [1] * (amount - 1)
    while rest > 0:
        free = [i for i in range(amount - 1) if holding[i] < reach]
        pool, left = sum([portions[i] for i in free]), rest
        for i in free:
            addition = min(reach - holding[i], max(1, left * portions[i] // pool), rest)
            holding[i] = holding[i] + addition
            rest = rest - addition
    return np.array([reach] + holding)


def uneven(own_key, count, total, limit, skew):
    if count == 2:
        one = jax.random.randint(own_key, (), max(1, total - limit), min(limit, total - 1) + 1)
        return jnp.stack([one, total - one])
    sizes = jnp.asarray(length_profile(count, total, limit, skew), jnp.int32)
    pairs = (count - 1) // 2
    giver, receiver = sizes[1:1 + 2 * pairs:2], sizes[2:2 + 2 * pairs:2]
    slack = jnp.minimum(giver - 1, limit - receiver)
    shifted = jax.random.randint(jax.random.fold_in(own_key, 1), (pairs,), 0, 1 << 20) % (slack + 1)
    sizes = sizes.at[1:1 + 2 * pairs:2].set(giver - shifted).at[2:2 + 2 * pairs:2].set(receiver + shifted)
    return sizes[jax.random.permutation(jax.random.fold_in(own_key, 2), count)]


def bell_draw(key, extent, width, limit, cuts=(), kind=jnp.bfloat16):
    level = steps_of(key, extent, cuts, -0.22, 0.18) if cuts else 1.0
    drawn = jax.random.normal(key, extent, jnp.float32) * width * level
    return jnp.minimum(jnp.maximum(drawn, -limit), limit).astype(kind)


def setup_inputs(seed: int = 0) -> dict:
    key_of = jax.random.split(jax.random.key(seed), 19)
    return {
        "tokens": bell_draw(key_of[0], (SEQS, LENGTH, D), 1.0, 6.0, ((0, 4), (1, 8))),
        "segment_ids": jax.vmap(lambda own: jnp.searchsorted(jnp.cumsum(uneven(own, DOCS, LENGTH, MOST, 2)), jnp.arange(LENGTH), side="right"))(jax.random.split(key_of[1], SEQS)).reshape((SEQS, LENGTH)).astype(jnp.int32),
        "w_query": bell_draw(key_of[2], (D, D), D ** -0.5, 0.21875, ((0, 4),)),
        "b_query": bell_draw(key_of[3], (D,), 0.5, 3.0, ((0, 4),)),
        "w_key": bell_draw(key_of[4], (D, D), D ** -0.5, 0.21875, ((0, 4),)),
        "w_value": bell_draw(key_of[5], (D, D), D ** -0.5, 0.21875, ((0, 4),)),
        "b_value": bell_draw(key_of[6], (D,), 0.5, 3.0, ((0, 4),)),
        "w_out": bell_draw(key_of[7], (D, D), (D // 16) ** -0.5, 0.875, ((0, 4),)),
        "b_out": bell_draw(key_of[8], (D,), 0.5, 3.0, ((0, 4),)),
        "gain_attn": jnp.clip(1.0 + 0.1 * jax.random.normal(key_of[9], (D,), jnp.float32), 0.5, 1.5).astype(jnp.bfloat16),
        "shift_attn": bell_draw(key_of[10], (D,), 0.5, 3.0, ((0, 4),)),
        "w_in": bell_draw(key_of[11], (D, FF), D ** -0.5, 0.21875, ((0, 4),)),
        "b_in": bell_draw(key_of[12], (FF,), 0.5, 3.0, ((0, 4),)),
        "w_down": bell_draw(key_of[13], (FF, D), FF ** -0.5, 0.109375, ((0, 4),)),
        "b_down": bell_draw(key_of[14], (D,), 0.5, 3.0, ((0, 4),)),
        "gain_ffn": jnp.clip(1.0 + 0.1 * jax.random.normal(key_of[15], (D,), jnp.float32), 0.5, 1.5).astype(jnp.bfloat16),
        "shift_ffn": bell_draw(key_of[16], (D,), 0.5, 3.0, ((0, 4),)),
        "cotangent": bell_draw(key_of[17], (SEQS, LENGTH, D), 1.0, 6.0, ((0, 4), (1, 8))),
    }


exact_mode = lax.Precision.HIGHEST
norm_eps = 1e-12
masked_fill = -1e+30

@jax.custom_vjp
def low(v):
    return lax.optimization_barrier(v.astype(jnp.bfloat16)).astype(jnp.float32)

@jax.custom_vjp
def low_back(v):
    return v

def low_keep(v):
    return (low(v), None)

def low_pass(kept, grad):
    return (grad,)

def back_keep(v):
    return (v, None)

def back_low(kept, grad):
    return (low(grad),)
low.defvjp(low_keep, low_pass)
low_back.defvjp(back_keep, back_low)

def product(left, right):
    return jnp.dot(left, right, precision=exact_mode)

def normalize(values, gain, shift):
    centre = lax.optimization_barrier(jnp.mean(values, axis=-1, keepdims=True))
    centred = values - centre
    spread = lax.optimization_barrier(jnp.mean(centred * centred, axis=-1, keepdims=True))
    return centred * lax.rsqrt(spread + norm_eps) * gain + shift

def layer(inputs, segments, params):
    w_query, b_query, w_key, w_value, b_value, w_out, b_out, gain_attn, shift_attn, w_in, b_in, w_down, b_down, gain_ffn, shift_ffn = params
    length = inputs.shape[0]
    head_dim = D // HEADS
    score_scale = 1.0 / math.sqrt(head_dim)
    queries = low(low_back(product(inputs, w_query) + b_query))
    key_rows = low(low_back(product(inputs, w_key)))
    values = low(low_back(product(inputs, w_value) + b_value))
    key_heads = key_rows.reshape(length, HEADS, head_dim)
    value_heads = values.reshape(length, HEADS, head_dim)
    block_rows = min(512, length)
    query_blocks = queries.reshape(length // block_rows, block_rows, HEADS, head_dim)
    seg_blocks = segments.reshape(length // block_rows, block_rows)

    def attend(paired):
        query_blk, seg_blk = paired
        scores = jnp.einsum('qhd,khd->hqk', query_blk, key_heads, precision=exact_mode) * score_scale
        scores = low_back(scores)
        same_doc = seg_blk[:, None] == segments[None, :]
        scores = jnp.where(same_doc[None], scores, masked_fill)
        highest = lax.optimization_barrier(jnp.max(scores, axis=2, keepdims=True))
        raised = jnp.exp(scores - highest)
        weights = raised / lax.optimization_barrier(jnp.sum(raised, axis=2, keepdims=True))
        mixture = jnp.einsum('hqk,khd->qhd', low(weights), value_heads, precision=exact_mode)
        return mixture.reshape(block_rows, HEADS * head_dim)
    attended = lax.map(jax.checkpoint(attend), (query_blocks, seg_blocks)).reshape(length, D)
    context = low(low_back(attended))
    attn_out = low_back(product(context, w_out) + b_out)
    hidden = normalize(inputs + attn_out, gain_attn, shift_attn)
    inner = low_back(product(low(hidden), w_in) + b_in)
    active = low(jax.nn.gelu(inner, approximate=False))
    branch = low_back(product(active, w_down) + b_down)
    return normalize(hidden + branch, gain_ffn, shift_ffn)

def reference(tokens, segment_ids, w_query, b_query, w_key, w_value, b_value, w_out, b_out, gain_attn, shift_attn, w_in, b_in, w_down, b_down, gain_ffn, shift_ffn, cotangent):
    params = tuple((weight.astype(jnp.float32) for weight in (w_query, b_query, w_key, w_value, b_value, w_out, b_out, gain_attn, shift_attn, w_in, b_in, w_down, b_down, gain_ffn, shift_ffn)))

    def one_sequence(totals, sequence_item):
        seq_tokens, seq_segments, seq_cotangent = sequence_item

        def forward(inputs, weights):
            return layer(inputs, seq_segments, weights)
        result, pullback = jax.vjp(forward, seq_tokens.astype(jnp.float32), params)
        grad_inputs, grad_params = pullback(seq_cotangent.astype(jnp.float32))
        totals = tuple((running + addend for running, addend in zip(totals, grad_params)))
        return (totals, (result.astype(jnp.bfloat16), grad_inputs.astype(jnp.bfloat16)))
    zeros = tuple((jnp.zeros_like(weight) for weight in params))
    totals, (outputs, grad_tokens) = lax.scan(one_sequence, zeros, (tokens, segment_ids, cotangent))
    return (outputs, grad_tokens, totals[0], totals[1], totals[2], totals[3], totals[4], totals[5], totals[6], totals[7], totals[8], totals[9], totals[10], totals[11], totals[12], totals[13], totals[14])
```

```python
from functools import partial
import math

import jax
import jax.numpy as jnp
from jax import lax
from jax.experimental import pallas as pl
from jax.experimental.pallas import tpu as pltpu
from jax.sharding import PartitionSpec as P

HEADS = 12


norm_eps = 1e-12
masked_fill = -1e30


def matmul(left, right):
    return jnp.dot(left, right, preferred_element_type=jnp.float32)


def matmul_left_t(left, right):
    return lax.dot_general(
        left, right, (((0,), (0,)), ((), ())), preferred_element_type=jnp.float32
    )


def matmul_right_t(left, right):
    return lax.dot_general(
        left, right, (((1,), (1,)), ((), ())), preferred_element_type=jnp.float32
    )


def normalize(values, gain, shift):
    centre = jnp.mean(values, axis=-1, keepdims=True)
    centred = values - centre
    inverse = lax.rsqrt(jnp.mean(centred * centred, axis=-1, keepdims=True) + norm_eps)
    normed = centred * inverse
    return (normed * gain + shift, normed, inverse)


def normalize_back(grad_out, normed, inverse, gain):
    grad_gain = jnp.sum(grad_out * normed, axis=0)
    grad_shift = jnp.sum(grad_out, axis=0)
    scaled = grad_out * gain
    grad_in = inverse * (
        scaled
        - jnp.mean(scaled, axis=-1, keepdims=True)
        - normed * jnp.mean(scaled * normed, axis=-1, keepdims=True)
    )
    return (grad_in, grad_gain, grad_shift)


def block_scores(query_blk, key_blk, seg_query, seg_key, score_scale):
    scores = (
        jnp.einsum("qhd,khd->hqk", query_blk, key_blk, preferred_element_type=jnp.float32)
        * score_scale
    )
    same_doc = seg_query[:, None] == seg_key[None, :]
    return (jnp.where(same_doc[None], scores, masked_fill), same_doc)


def block_grads(
    query_blk, dctx_blk, lse_blk, delta_blk, seg_query, key_blk, value_blk, seg_key, score_scale
):
    scores, same_doc = block_scores(query_blk, key_blk, seg_query, seg_key, score_scale)
    weights = jnp.where(same_doc[None], jnp.exp(scores - lse_blk.T[:, :, None]), 0.0)
    grad_weights = jnp.einsum(
        "qhd,khd->hqk", dctx_blk, value_blk, preferred_element_type=jnp.float32
    )
    grad_scores = (weights * (grad_weights - delta_blk.T[:, :, None])).astype(jnp.bfloat16)
    grad_query = None
    grad_key = None
    grad_value = None
    grad_query = (
        jnp.einsum("hqk,khd->qhd", grad_scores, key_blk, preferred_element_type=jnp.float32)
        * score_scale
    )
    grad_key = (
        jnp.einsum("hqk,qhd->khd", grad_scores, query_blk, preferred_element_type=jnp.float32)
        * score_scale
    )
    grad_value = jnp.einsum(
        "hqk,qhd->khd", weights.astype(jnp.bfloat16), dctx_blk, preferred_element_type=jnp.float32
    )
    return (grad_query, grad_key, grad_value)


def per_device(
    tokens,
    segment_ids,
    w_query,
    b_query,
    w_key,
    w_value,
    b_value,
    w_out,
    b_out,
    gain_attn,
    shift_attn,
    w_in,
    b_in,
    w_down,
    b_down,
    gain_ffn,
    shift_ffn,
    cotangent,
):
    (
        full_query,
        bias_query,
        full_key,
        full_value,
        bias_value,
        full_out,
        bias_out,
        gain_one,
        shift_one,
        full_in,
        bias_in,
        full_down,
        bias_down,
        gain_two,
        shift_two,
    ) = (
        lax.all_gather(w_query, "wsh", axis=0, tiled=True),
        lax.all_gather(b_query, "wsh", axis=0, tiled=True),
        lax.all_gather(w_key, "wsh", axis=0, tiled=True),
        lax.all_gather(w_value, "wsh", axis=0, tiled=True),
        lax.all_gather(b_value, "wsh", axis=0, tiled=True),
        lax.all_gather(w_out, "wsh", axis=0, tiled=True),
        lax.all_gather(b_out, "wsh", axis=0, tiled=True),
        lax.all_gather(gain_attn, "wsh", axis=0, tiled=True),
        lax.all_gather(shift_attn, "wsh", axis=0, tiled=True),
        lax.all_gather(w_in, "wsh", axis=0, tiled=True),
        lax.all_gather(b_in, "wsh", axis=0, tiled=True),
        lax.all_gather(w_down, "wsh", axis=0, tiled=True),
        lax.all_gather(b_down, "wsh", axis=0, tiled=True),
        lax.all_gather(gain_ffn, "wsh", axis=0, tiled=True),
        lax.all_gather(shift_ffn, "wsh", axis=0, tiled=True),
    )
    inputs = tokens[0]
    rows = inputs.shape[0]
    width = inputs.shape[1]
    head_dim = width // HEADS
    score_scale = 1.0 / math.sqrt(head_dim)
    seg_float = segment_ids[0].astype(jnp.bfloat16)
    queries = (matmul(inputs, full_query) + bias_query.astype(jnp.float32)).astype(jnp.bfloat16)
    key_rows = matmul(inputs, full_key).astype(jnp.bfloat16)
    values = (matmul(inputs, full_value) + bias_value.astype(jnp.float32)).astype(jnp.bfloat16)
    keys_all, values_all, segs_all = (
        lax.all_gather(key_rows, ("ctx", "wsh"), axis=0, tiled=True),
        lax.all_gather(values, ("ctx", "wsh"), axis=0, tiled=True),
        lax.all_gather(seg_float, ("ctx", "wsh"), axis=0, tiled=True),
    )
    total = keys_all.shape[0]
    key_block = min(512, total)
    block_count = total // key_block
    key_blocks = keys_all.reshape(block_count, key_block, HEADS, head_dim)
    value_blocks = values_all.reshape(block_count, key_block, HEADS, head_dim)
    seg_blocks = segs_all.reshape(block_count, key_block)
    query_heads = queries.reshape(rows, HEADS, head_dim)

    def forward_block(carry, block):
        run_max, run_sum, accum = carry
        key_blk, value_blk, seg_blk = block
        scores, same_doc = block_scores(query_heads, key_blk, seg_float, seg_blk, score_scale)
        new_max = jnp.maximum(run_max, jnp.max(scores, axis=2))
        raised = jnp.where(same_doc[None], jnp.exp(scores - new_max[:, :, None]), 0.0)
        factor = jnp.exp(run_max - new_max)
        run_sum = run_sum * factor + jnp.sum(raised, axis=2)
        accum = accum * factor.T[:, :, None] + jnp.einsum(
            "hqk,khd->qhd",
            raised.astype(jnp.bfloat16),
            value_blk,
            preferred_element_type=jnp.float32,
        )
        return ((new_max, run_sum, accum), None)

    start_state = (
        jnp.full((HEADS, rows), masked_fill, jnp.float32),
        jnp.zeros((HEADS, rows), jnp.float32),
        jnp.zeros((rows, HEADS, head_dim), jnp.float32),
    )
    (run_max, run_sum, accum), unused = lax.scan(
        forward_block, start_state, (key_blocks, value_blocks, seg_blocks)
    )
    attended = accum / run_sum.T[:, :, None]
    lse_rows = (run_max + jnp.log(run_sum)).T
    context = attended.reshape(rows, width).astype(jnp.bfloat16)
    attn_out = matmul(context, full_out) + bias_out.astype(jnp.float32)
    gain_first = gain_one.astype(jnp.float32)
    gain_second = gain_two.astype(jnp.float32)
    hidden, normed_one, inverse_one = normalize(
        inputs.astype(jnp.float32) + attn_out, gain_first, shift_one.astype(jnp.float32)
    )
    hidden_low = hidden.astype(jnp.bfloat16)
    inner = matmul(hidden_low, full_in) + bias_in.astype(jnp.float32)
    active_float, gelu_pull = jax.vjp(partial(jax.nn.gelu, approximate=False), inner)
    active = active_float.astype(jnp.bfloat16)
    branch = matmul(active, full_down) + bias_down.astype(jnp.float32)
    result, normed_two, inverse_two = normalize(
        hidden + branch, gain_second, shift_two.astype(jnp.float32)
    )
    grad_out = cotangent[0].astype(jnp.float32)
    grad_res_two, grad_gain_two, grad_shift_two = normalize_back(
        grad_out, normed_two, inverse_two, gain_second
    )
    grad_branch = grad_res_two.astype(jnp.bfloat16)
    grad_bias_down = jnp.sum(grad_branch.astype(jnp.float32), axis=0)
    grad_full_down = matmul_left_t(active, grad_branch)
    grad_inner = gelu_pull(matmul_right_t(grad_branch, full_down))[0].astype(jnp.bfloat16)
    grad_bias_in = jnp.sum(grad_inner.astype(jnp.float32), axis=0)
    grad_full_in = matmul_left_t(hidden_low, grad_inner)
    grad_hidden = grad_res_two + matmul_right_t(grad_inner, full_in)
    grad_res_one, grad_gain_one, grad_shift_one = normalize_back(
        grad_hidden, normed_one, inverse_one, gain_first
    )
    grad_attn = grad_res_one.astype(jnp.bfloat16)
    grad_bias_out = jnp.sum(grad_attn.astype(jnp.float32), axis=0)
    grad_full_out = matmul_left_t(context, grad_attn)
    grad_context = matmul_right_t(grad_attn, full_out).astype(jnp.bfloat16)
    dctx_heads = grad_context.reshape(rows, HEADS, head_dim)
    delta_rows = jnp.sum(dctx_heads.astype(jnp.float32) * attended, axis=2)
    zero_heads = jnp.zeros((rows, HEADS, head_dim), jnp.float32)

    def back_block(grad_acc, block):
        key_blk, value_blk, seg_blk = block
        part_query, part_key, part_value = block_grads(
            query_heads,
            dctx_heads,
            lse_rows,
            delta_rows,
            seg_float,
            key_blk,
            value_blk,
            seg_blk,
            score_scale,
        )
        return (grad_acc + part_query, (part_key, part_value))

    grad_q, (key_parts, value_parts) = lax.scan(
        back_block, zero_heads, (key_blocks, value_blocks, seg_blocks)
    )
    grad_key_own, grad_value_own = (
        lax.psum_scatter(
            key_parts.reshape(total, width), ("ctx", "wsh"), scatter_dimension=0, tiled=True
        ),
        lax.psum_scatter(
            value_parts.reshape(total, width), ("ctx", "wsh"), scatter_dimension=0, tiled=True
        ),
    )
    grad_queries = grad_q.reshape(rows, width).astype(jnp.bfloat16)
    grad_keys = grad_key_own.astype(jnp.bfloat16)
    grad_values = grad_value_own.astype(jnp.bfloat16)
    grad_full_query = matmul_left_t(inputs, grad_queries)
    grad_bias_query = jnp.sum(grad_queries.astype(jnp.float32), axis=0)
    grad_full_key = matmul_left_t(inputs, grad_keys)
    grad_full_value = matmul_left_t(inputs, grad_values)
    grad_bias_value = jnp.sum(grad_values.astype(jnp.float32), axis=0)
    grad_input = (
        grad_res_one
        + matmul_right_t(grad_queries, full_query)
        + matmul_right_t(grad_keys, full_key)
        + matmul_right_t(grad_values, full_value)
    )
    (
        share_query,
        share_bias_query,
        share_key,
        share_value,
        share_bias_value,
        share_out,
        share_bias_out,
        share_gain_one,
        share_shift_one,
        share_in,
        share_bias_in,
        share_down,
        share_bias_down,
        share_gain_two,
        share_shift_two,
    ) = (
        lax.psum_scatter(
            grad_full_query.astype(jnp.bfloat16), "wsh", scatter_dimension=0, tiled=True
        ).astype(jnp.float32),
        lax.psum_scatter(
            grad_bias_query.astype(jnp.bfloat16), "wsh", scatter_dimension=0, tiled=True
        ).astype(jnp.float32),
        lax.psum_scatter(
            grad_full_key.astype(jnp.bfloat16), "wsh", scatter_dimension=0, tiled=True
        ).astype(jnp.float32),
        lax.psum_scatter(
            grad_full_value.astype(jnp.bfloat16), "wsh", scatter_dimension=0, tiled=True
        ).astype(jnp.float32),
        lax.psum_scatter(
            grad_bias_value.astype(jnp.bfloat16), "wsh", scatter_dimension=0, tiled=True
        ).astype(jnp.float32),
        lax.psum_scatter(
            grad_full_out.astype(jnp.bfloat16), "wsh", scatter_dimension=0, tiled=True
        ).astype(jnp.float32),
        lax.psum_scatter(
            grad_bias_out.astype(jnp.bfloat16), "wsh", scatter_dimension=0, tiled=True
        ).astype(jnp.float32),
        lax.psum_scatter(
            grad_gain_one.astype(jnp.bfloat16), "wsh", scatter_dimension=0, tiled=True
        ).astype(jnp.float32),
        lax.psum_scatter(
            grad_shift_one.astype(jnp.bfloat16), "wsh", scatter_dimension=0, tiled=True
        ).astype(jnp.float32),
        lax.psum_scatter(
            grad_full_in.astype(jnp.bfloat16), "wsh", scatter_dimension=0, tiled=True
        ).astype(jnp.float32),
        lax.psum_scatter(
            grad_bias_in.astype(jnp.bfloat16), "wsh", scatter_dimension=0, tiled=True
        ).astype(jnp.float32),
        lax.psum_scatter(
            grad_full_down.astype(jnp.bfloat16), "wsh", scatter_dimension=0, tiled=True
        ).astype(jnp.float32),
        lax.psum_scatter(
            grad_bias_down.astype(jnp.bfloat16), "wsh", scatter_dimension=0, tiled=True
        ).astype(jnp.float32),
        lax.psum_scatter(
            grad_gain_two.astype(jnp.bfloat16), "wsh", scatter_dimension=0, tiled=True
        ).astype(jnp.float32),
        lax.psum_scatter(
            grad_shift_two.astype(jnp.bfloat16), "wsh", scatter_dimension=0, tiled=True
        ).astype(jnp.float32),
    )
    summed = lax.psum(
        (
            share_query,
            share_bias_query,
            share_key,
            share_value,
            share_bias_value,
            share_out,
            share_bias_out,
            share_gain_one,
            share_shift_one,
            share_in,
            share_bias_in,
            share_down,
            share_bias_down,
            share_gain_two,
            share_shift_two,
        ),
        ("seq", "ctx"),
    )
    return (
        result.astype(jnp.bfloat16)[None],
        grad_input.astype(jnp.bfloat16)[None],
        summed[0],
        summed[1],
        summed[2],
        summed[3],
        summed[4],
        summed[5],
        summed[6],
        summed[7],
        summed[8],
        summed[9],
        summed[10],
        summed[11],
        summed[12],
        summed[13],
        summed[14],
    )


MESH_ID = pl.DeviceIdType.MESH
LANES = 256
IDS = 16
BIG = float(2.0**99)
VMEM_LIMIT = 60 * 2**20


def remote(src, dst, send, recv, where):
    return pltpu.make_async_remote_copy(
        src_ref=src, dst_ref=dst, send_sem=send, recv_sem=recv, device_id=where, device_id_type=MESH_ID
    )


def nt(left, right):
    return lax.dot_general(left, right, (((1,), (1,)), ((), ())), preferred_element_type=jnp.float32)


def tn(left, right):
    return lax.dot_general(left, right, (((0,), (0,)), ((), ())), preferred_element_type=jnp.float32)


def nn(left, right):
    return jnp.dot(left, right, preferred_element_type=jnp.float32)


def greet(peers):
    barrier = pltpu.get_barrier_semaphore()
    for peer in peers:
        pl.semaphore_signal(barrier, inc=1, device_id=peer, device_id_type=MESH_ID)
    pl.semaphore_wait(barrier, len(peers))


def attend_kernel(
    dims,
    tokens, seg, w_q, w_k, w_v, b_q, b_v, vec, w_o, w_i, w_d,
    toks, wcol, qx, kx, vv, att_t, lse, ctx, full_o, full_i, full_d, vecs,
    segs, w_send, w_recv, vt, scores, ctx_send, ctx_recv,
    tok_s, tok_r, sv_s, sv_r, wz_s, wz_r, wp_s, wp_r, kv_s, kv_r, cx_s, cx_r,
    fz_s, fz_r, fx_s, fx_r, fc_s, fc_r, loc,
):
    S, W, heads = dims["S"], dims["W"], dims["heads"]
    rows, width = tokens.shape
    group = width // W
    head_dim = group // heads
    block = rows * W
    total = 2 * block
    s, c, z = lax.axis_index("seq"), lax.axis_index("ctx"), lax.axis_index("wsh")
    sib = (s, 1 - c, z)
    s1, s2, s3 = s ^ 1, s ^ 2, s ^ 3
    shifts = list(range(1, W))
    zz = [lax.rem(z + t, W) for t in shifts]
    greet([sib] + [(p, c, z) for p in (s1, s2, s3)] + [(s, c, q) for q in zz])

    toks[z] = tokens[...]
    segs[z] = seg[...]
    vecs[z] = vec[...]

    def tok_copy(slot, step, lane):
        return remote(toks.at[slot], toks.at[slot], tok_s.at[lane, slot], tok_r.at[slot], (s, c, z + step))

    @pl.when(z + 1 < W)
    def _():
        tok_copy(z, 1, 0).start()

    @pl.when(z > 0)
    def _():
        tok_copy(z, -1, 1).start()

    eighth = group // 8
    piece = c * S + s
    for j in range(W):
        for m, ref in enumerate((w_q, w_k, w_v)):
            part = ref[:, j * group : (j + 1) * group]
            part = jnp.concatenate([part, jnp.zeros((group, LANES - group), part.dtype)], axis=1)
            for e in range(8):
                w_send[j, e, :, m * LANES : (m + 1) * LANES] = part[e * eighth : (e + 1) * eighth]

    def wz(q):
        return remote(w_send.at[q, piece], w_recv.at[z, piece], wz_s.at[q], wz_r.at[z], (s, c, q))

    def wz_in(q):
        return remote(w_send.at[q, piece], w_recv.at[q, piece], wz_s.at[q], wz_r.at[q], (s, c, q))

    def seg_out(q):
        return remote(segs.at[z], segs.at[z], sv_s.at[0, q], sv_r.at[0, z], (s, c, q))

    def seg_in(q):
        return remote(segs.at[q], segs.at[q], sv_s.at[0, q], sv_r.at[0, q], (s, c, q))

    def vec_out(q):
        return remote(vecs.at[z], vecs.at[z], sv_s.at[1, q], sv_r.at[1, z], (s, c, q))

    def vec_in(q):
        return remote(vecs.at[q], vecs.at[q], sv_s.at[1, q], sv_r.at[1, q], (s, c, q))

    for q in zz:
        wz(q).start()
        seg_out(q).start()
        vec_out(q).start()

    parts = ((w_o, full_o), (w_i, full_i), (w_d, full_d))

    def spot_of(ref, base, part, cc, ss, half):
        n, m = parts[part][0].shape
        if part == 0:
            row, col, size, wide = (0 if ss is None else ss * (n // S)), cc * (m // 2), n // S, m // 2
            if ss is None:
                size = n
            if half is not None:
                col, wide = col + (0 if half == 0 else 128), (128 if half == 0 else m // 2 - 128)
        elif part == 1:
            wide = m // 2 if ss is None else m // 8
            row, col, size = 0, cc * (m // 2) + (0 if ss is None else ss * (m // 8)), n
            if half is not None:
                row, size = half * (n // 2), n // 2
        else:
            size = n // 2 if ss is None else n // 8
            row, col, wide = cc * (n // 2) + (0 if ss is None else ss * (n // 8)), 0, m
            if half is not None:
                col, wide = half * (m // 2), m // 2
        row = base + row
        if not isinstance(row, int):
            row = pl.multiple_of(row, 16)
        if not isinstance(col, int):
            col = pl.multiple_of(col, 128)
        return ref.at[pl.ds(row, size), pl.ds(col, wide)]

    def rows_of(part, q, cc, ss, half=None):
        return spot_of(parts[part][1], q * parts[part][0].shape[0], part, cc, ss, half)

    def own_copy(part):
        n = parts[part][0].shape[0]
        return pltpu.make_async_copy(
            parts[part][0], parts[part][1].at[pl.ds(pl.multiple_of(z * n, 16), n), :], loc.at[part]
        )

    def fz(part, q):
        src = spot_of(parts[part][0], 0, part, c, s, None)
        return remote(src, rows_of(part, z, c, s), fz_s.at[part, q], fz_r.at[part, z], (s, c, q))

    def fz_in(part, q):
        here = rows_of(part, q, c, s)
        return remote(here, here, fz_s.at[part, q], fz_r.at[part, q], (s, c, q))

    def fx(part, q, kind):
        if kind < 2:
            ref, to = rows_of(part, q, c, s), (s1, s2)[kind]
        else:
            ref, to = rows_of(part, q, c, (s1, s2)[kind - 2], kind - 2), (s2, s1)[kind - 2]
        return remote(ref, ref, fx_s.at[part, q, kind], fx_r.at[part, q, kind], (to, c, z))

    def fx_in(part, q, kind):
        if kind < 2:
            ref = rows_of(part, q, c, (s1, s2)[kind])
        else:
            ref = rows_of(part, q, c, s3, kind - 2)
        return remote(ref, ref, fx_s.at[part, q, kind], fx_r.at[part, q, kind], (s1, c, z))

    def fc(part, q):
        ref = rows_of(part, q, c, None)
        return remote(ref, ref, fc_s.at[part, q], fc_r.at[part, q], sib)

    def fc_in(part, q):
        ref = rows_of(part, q, 1 - c, None)
        return remote(ref, ref, fc_s.at[part, q], fc_r.at[part, q], sib)

    def w_start(part):
        own_copy(part).start()
        for q in zz:
            fz(part, q).start()

    def w_plane(part):
        for q in zz:
            fz_in(part, q).wait_recv()
            fx(part, q, 0).start()
            fx(part, q, 1).start()

    def w_cross(part):
        for q in zz:
            fx_in(part, q, 0).wait_recv()
            fx(part, q, 2).start()
            fx_in(part, q, 1).wait_recv()
            fx(part, q, 3).start()

    def w_core(part):
        for q in zz:
            fx_in(part, q, 2).wait_recv()
            fx_in(part, q, 3).wait_recv()
            fc(part, q).start()

    def w_finish(part):
        own_copy(part).wait()
        for q in zz:
            fc_in(part, q).wait_recv()
            fz(part, q).wait_send()
            for kind in range(4):
                fx(part, q, kind).wait_send()
            fc(part, q).wait_send()

    w_start(0)
    w_start(1)

    def wp(q, kind):
        at = piece if kind < 4 else c * S + (s ^ (kind - 3))
        where = (s ^ (kind + 1), c, z) if kind < 3 else sib
        ref = w_recv.at[q, at]
        return remote(ref, ref, wp_s.at[q, kind], wp_r.at[q, at], where)

    def wp_in(q, at):
        ref = w_recv.at[q, at]
        return remote(ref, ref, wp_s.at[q, 0], wp_r.at[q, at], sib)

    for q in zz:
        wz_in(q).wait_recv()
        for kind in range(4):
            wp(q, kind).start()
    for q in zz:
        for kind in range(4, 7):
            wp_in(q, c * S + (s ^ (kind - 3))).wait_recv()
            wp(q, kind).start()
    for e in range(8):
        w_recv[z, e] = w_send[z, e]
    for q in zz:
        for e in range(S):
            wp_in(q, (1 - c) * S + e).wait_recv()
    for j in range(W):
        for e in range(8):
            wcol[j * group + e * eighth : j * group + (e + 1) * eighth, :] = w_recv[j, e]
    for q in zz:
        seg_in(q).wait_recv()

    lane = lax.broadcasted_iota(jnp.int32, (1, LANES), 1)
    spot = lax.broadcasted_iota(jnp.int32, (IDS, LANES), 1) - lax.broadcasted_iota(jnp.int32, (IDS, LANES), 0)
    lanes_in = lax.broadcasted_iota(jnp.int32, (IDS, LANES), 1)
    in_ext = (lanes_in >= group) & (lanes_in < group + IDS)
    put_q = jnp.where(spot == group, 1.0, 0.0).astype(jnp.bfloat16)
    put_k = jnp.where(in_ext & (spot != group), -BIG, 0.0).astype(jnp.bfloat16)
    pad = jnp.zeros((1, LANES - group), jnp.float32)
    bias_q = jnp.concatenate([b_q[...], pad], axis=1)
    bias_v = jnp.concatenate([b_v[...], pad], axis=1)
    ids = lax.broadcasted_iota(jnp.int32, (IDS, rows), 0).astype(jnp.float32)

    def k_rows(owner, slot):
        return pl.ds(pl.multiple_of(owner * block + slot * rows, rows), rows)

    def kv(slot, which):
        ref = (kx, vv)[which].at[k_rows(c, slot), :]
        return remote(ref, ref, kv_s.at[which, slot], kv_r.at[which, slot], sib)

    def kv_in(slot, which):
        ref = (kx, vv)[which].at[k_rows(1 - c, slot), :]
        return remote(ref, ref, kv_s.at[which, slot], kv_r.at[which, slot], sib)

    def project(slot):
        made = nn(toks[slot], wcol[...])
        hot = jnp.where(jnp.broadcast_to(segs[slot], (IDS, rows)) == ids, 1.0, 0.0).astype(jnp.bfloat16)
        q_low = (made[:, :LANES] + bias_q).astype(jnp.bfloat16).astype(jnp.float32) * dims["scale"]
        ext_q = tn(hot, put_q)
        for h in range(heads):
            mine = (lane >= h * head_dim) & (lane < (h + 1) * head_dim)
            qx[pl.ds(pl.multiple_of(h * block + slot * rows, rows), rows), :] = (
                jnp.where(mine, q_low, 0.0) + ext_q
            ).astype(jnp.bfloat16)
        kx[k_rows(c, slot), :] = (made[:, LANES : 2 * LANES] + tn(hot, put_k)).astype(jnp.bfloat16)
        vv[k_rows(c, slot), :] = (made[:, 2 * LANES :] + bias_v).astype(jnp.bfloat16)
        kv(slot, 0).start()
        kv(slot, 1).start()

    def arrive(k, carry):
        far = lax.div(k + 1, 2)
        leftward = lax.rem(k, 2) == 1
        slot = jnp.where(leftward, z - far, z + far)
        there = (slot >= 0) & (slot < W)

        @pl.when(there)
        def _():
            @pl.when(k > 0)
            def _():
                tok_copy(slot, 1, 0).wait_recv()

            @pl.when((k > 0) & leftward & (z + 1 < W))
            def _():
                tok_copy(slot, 1, 0).start()

            @pl.when((k > 0) & jnp.logical_not(leftward) & (z > 0))
            def _():
                tok_copy(slot, -1, 1).start()

            project(slot)

        return carry

    lax.fori_loop(0, 2 * W - 1, arrive, 0)
    w_start(2)
    for j in range(W):
        kv_in(j, 0).wait_recv()
        kv_in(j, 1).wait_recv()
    vt[...] = vv[...].astype(jnp.float32).T.astype(jnp.bfloat16)

    chunk = dims["chunk"]
    n_chunks = total // chunk

    def cx(b):
        return remote(ctx_send.at[b], ctx_recv.at[z], cx_s.at[b], cx_r.at[z], (s, c, b))

    def cx_in(b):
        return remote(ctx_send.at[b], ctx_recv.at[b], cx_s.at[b], cx_r.at[b], (s, c, b))

    def attend(step, carry):
        i = lax.div(step, heads)
        h = lax.rem(step, heads)
        b = lax.rem(z + 1 + i, W)
        query = qx[pl.ds(pl.multiple_of(h * block + b * rows, rows), rows), :]
        top = None
        for n in range(n_chunks):
            got = nt(kx[n * chunk : (n + 1) * chunk, :], query)
            scores[n * chunk : (n + 1) * chunk, :] = got
            high = jnp.max(got, axis=0, keepdims=True)
            top = high if top is None else jnp.maximum(top, high)
        mass = None
        out = None
        here = pl.ds(pl.multiple_of(h * head_dim, head_dim), head_dim)
        for n in range(n_chunks):
            raised = jnp.exp(scores[n * chunk : (n + 1) * chunk, :] - top)
            add = jnp.sum(raised, axis=0, keepdims=True)
            mass = add if mass is None else mass + add
            piece_out = nn(vt[here, n * chunk : (n + 1) * chunk], raised.astype(jnp.bfloat16))
            out = piece_out if out is None else out + piece_out
        att_t[here, pl.ds(pl.multiple_of(b * rows, rows), rows)] = out / mass
        lse[h, :, pl.ds(pl.multiple_of(b * rows, rows), rows)] = top + jnp.log(mass)

        @pl.when(h == heads - 1)
        def _():
            done = att_t[:, pl.ds(pl.multiple_of(b * rows, rows), rows)]
            ctx_send[b] = done.T.astype(jnp.bfloat16)

            @pl.when(i < W - 1)
            def _():
                cx(b).start()

            @pl.when(i == W - 1)
            def _():
                ctx_recv[b] = ctx_send[b]

        for part, stage, when in dims["moves"]:
            @pl.when(step == when)
            def _():
                (w_plane, w_cross, w_core)[stage](part)

        return carry

    lax.fori_loop(0, W * heads, attend, 0)
    for part, stage in dims["late"]:
        (w_plane, w_cross, w_core)[stage](part)
    for q in zz:
        cx_in(q).wait_recv()
    for j in range(W):
        ctx[:, j * group : (j + 1) * group] = ctx_recv[j]

    for part in range(3):
        w_finish(part)

    @pl.when(z + 1 < W)
    def _():
        for j in range(W):
            @pl.when(j <= z)
            def _():
                tok_copy(j, 1, 0).wait_send()

    @pl.when(z > 0)
    def _():
        for j in range(W):
            @pl.when(j >= z)
            def _():
                tok_copy(j, -1, 1).wait_send()

    for q in zz:
        wz(q).wait_send()
        seg_out(q).wait_send()
        vec_out(q).wait_send()
        vec_in(q).wait_recv()
        for kind in range(7):
            wp(q, kind).wait_send()
        cx(q).wait_send()
    for j in range(W):
        kv(j, 0).wait_send()
        kv(j, 1).wait_send()


def attend_call(dims, tokens, seg, w_q, w_k, w_v, b_q, b_v, vec, w_o, w_i, w_d):
    W, heads = dims["W"], dims["heads"]
    rows, width = tokens.shape
    group = width // W
    block = rows * W
    total = 2 * block
    ff = w_i.shape[1]
    vm = pl.BlockSpec(memory_space=pltpu.VMEM)
    hb = pl.BlockSpec(memory_space=pl.ANY)
    f32, bf16 = jnp.float32, jnp.bfloat16
    dma = pltpu.SemaphoreType.DMA
    shape = jax.ShapeDtypeStruct
    return pl.pallas_call(
        partial(attend_kernel, dims),
        name="gather_attend",
        out_shape=(
            shape((W, rows, width), bf16),
            shape((width, 3 * LANES), bf16),
            shape((heads * block, LANES), bf16),
            shape((total, LANES), bf16),
            shape((total, LANES), bf16),
            shape((group, block), f32),
            shape((heads, 1, block), f32),
            shape((rows, width), bf16),
            shape((width, width), bf16),
            shape((width, ff), bf16),
            shape((ff, width), bf16),
            shape((W, 1, vec.shape[1]), f32),
        ),
        in_specs=[vm] * 8 + [hb] * 3,
        out_specs=tuple([vm] * 8 + [hb] * 3 + [vm]),
        scratch_shapes=[
            pltpu.VMEM((W, 1, rows), f32),
            pltpu.VMEM((W, 8, group // 8, 3 * LANES), bf16),
            pltpu.VMEM((W, 8, group // 8, 3 * LANES), bf16),
            pltpu.VMEM((LANES, total), bf16),
            pltpu.VMEM((total, rows), f32),
            pltpu.VMEM((W, rows, group), bf16),
            pltpu.VMEM((W, rows, group), bf16),
            dma((2, W)), dma((W,)), dma((2, W)), dma((2, W)), dma((W,)), dma((W,)),
            dma((W, 8)), dma((W, 8)), dma((2, W)), dma((2, W)), dma((W,)), dma((W,)),
            dma((3, W)), dma((3, W)), dma((3, W, 4)), dma((3, W, 4)), dma((3, W)), dma((3, W)),
            dma((3,)),
        ],
        compiler_params=pltpu.CompilerParams(
            collective_id=1, has_side_effects=True, vmem_limit_bytes=VMEM_LIMIT
        ),
    )(tokens, seg, w_q, w_k, w_v, b_q, b_v, vec, w_o, w_i, w_d)


def back_kernel(
    dims,
    toks, wcol, qx, kx, vv, att_t, lse, grad_ctx, res, active, grad_branch, hidden, grad_inner, context, grad_attn, vec,
    g_tok, gd, gi, go, gq, g_vec, g_b,
    d_send, d_recv, kt, dk, dv, dq_t, dqkv, kv_send, kv_recv, px, rx,
    pd, pi, po, pq, cd, ci, co, cq, xd, xi, xo, xq, yd, yi, yo, yq, zd, zi, zo, zq,
    vx, vc, vs, vz, bx, bc, bs,
    da_s, da_r, kv_s, kv_r, rx_s, rx_r, core_s, core_r, x1_s, x1_r, x2_s, x2_r, za_s, za_r, ga_s, ga_r, gc_s, gc_r,
    vp_s, vp_r, bp_s, bp_r,
):
    S, W, heads = dims["S"], dims["W"], dims["heads"]
    f32, bf16 = jnp.float32, jnp.bfloat16
    rows, width = grad_ctx.shape
    group = width // W
    head_dim = group // heads
    block = rows * W
    total = 2 * block
    half_width = width // 2
    s, c, z = lax.axis_index("seq"), lax.axis_index("ctx"), lax.axis_index("wsh")
    sib = (s, 1 - c, z)
    s1, s2, s3 = s ^ 1, s ^ 2, s ^ 3
    zz = [lax.rem(z + t, W) for t in range(1, W)]
    P, CR, X1, X2, Z, G = (pd, pi, po, pq), (cd, ci, co, cq), (xd, xi, xo, xq), (yd, yi, yo, yq), (zd, zi, zo, zq), (gd, gi, go, gq)
    mine = c * S + s

    for j in range(W):
        d_send[j] = grad_ctx[:, j * group : (j + 1) * group]
    greet([sib] + [(p, c, z) for p in (s1, s2, s3)] + [(s, c, q) for q in zz])

    def da(q):
        return remote(d_send.at[q], d_recv.at[z], da_s.at[q], da_r.at[z], (s, c, q))

    def da_in(q):
        return remote(d_send.at[q], d_recv.at[q], da_s.at[q], da_r.at[q], (s, c, q))

    for q in zz:
        da(q).start()
    d_recv[z] = d_send[z]

    def vcore():
        return remote(vc.at[c], vc.at[c], vp_s.at[0], vp_r.at[0], sib)

    def vplane(k):
        return remote(vs.at[s], vs.at[s], vp_s.at[k], vp_r.at[k], (s ^ k, c, z))

    def vz_out(q, t):
        return remote(vx.at[q], vz.at[z], vp_s.at[4 + t], vp_r.at[4 + z], (s, c, q))

    def vz_in(q, t):
        return remote(vx.at[q], vz.at[q], vp_s.at[4 + t], vp_r.at[4 + q], (s, c, q))

    def vec_core():
        vc[c] = vec[...]
        vcore().start()

    def vec_plane():
        vcore().wait_recv()
        vs[s] = vc[0] + vc[1]
        for k in (1, 2, 3):
            vplane(k).start()

    def vec_z():
        for k in (1, 2, 3):
            vplane(k).wait_recv()
        vx[...] = (vs[0] + vs[1]) + (vs[2] + vs[3])
        vz[z] = vx[z]
        for t, q in enumerate(zz):
            vz_out(q, t).start()

    def vec_end():
        for t, q in enumerate(zz):
            vz_in(q, t).wait_recv()
        acc = vz[0]
        for j in range(1, W):
            acc = acc + vz[j]
        g_vec[...] = acc
        vcore().wait_send()
        for k in (1, 2, 3):
            vplane(k).wait_send()
        for t, q in enumerate(zz):
            vz_out(q, t).wait_send()

    def core_move(a):
        return remote(P[a].at[:, pl.ds((1 - c) * S, S)], CR[a], core_s.at[a], core_r.at[a], sib)

    def add_into(a, at, half, ref):
        P[a][:, at, half] = (P[a][:, at, half].astype(f32) + ref.astype(f32)).astype(bf16)

    def core_add(a):
        core_move(a).wait_recv()
        for j in range(S):
            for half in range(2):
                add_into(a, c * S + j, half, CR[a][:, j, half])

    def x1(a, half, slot):
        to = (s1, s2)[half]
        at = c * S + ((s1, s3) if half == 0 else (s2, s3))[slot]
        k = half * 2 + slot
        return remote(P[a].at[:, at, half], X1[a].at[half, slot], x1_s.at[a, k], x1_r.at[a, k], (to, c, z))

    def x1_send(a):
        for half in range(2):
            for slot in range(2):
                x1(a, half, slot).start()

    def x1_add(a):
        for half in range(2):
            for slot in (1, 0):
                x1(a, half, slot).wait_recv()
                at = c * S + (s if slot == 0 else (s2, s1)[half])
                add_into(a, at, half, X1[a][half, slot])

    def x2(a, half):
        to = (s2, s1)[half]
        return remote(P[a].at[:, c * S + to, half], X2[a].at[half], x2_s.at[a, half], x2_r.at[a, half], (to, c, z))

    def x2_send(a):
        for half in range(2):
            x2(a, half).start()

    def x2_add(a):
        for half in range(2):
            x2(a, half).wait_recv()
            add_into(a, mine, half, X2[a][half])

    def za(a, q, t):
        return remote(P[a].at[q, mine], Z[a].at[z], za_s.at[a, t], za_r.at[a, z], (s, c, q))

    def za_in(a, q, t):
        return remote(P[a].at[q, mine], Z[a].at[q], za_s.at[a, t], za_r.at[a, q], (s, c, q))

    def z_send(a):
        for t, q in enumerate(zz):
            za(a, q, t).start()
        Z[a][z] = P[a][z, mine]

    def z_add(a):
        for t, q in enumerate(zz):
            za_in(a, q, t).wait_recv()
        if a == 3:
            G[a][mine] = Z[a][...]
        else:
            acc = Z[a][0].astype(f32)
            for j in range(1, W):
                acc = acc + Z[a][j].astype(f32)
            G[a][mine] = acc.astype(bf16)

    def half_of(a, at, half):
        return G[a].at[at, :, half] if a == 3 else G[a].at[at, half]

    def ga(a, kind):
        if kind < 2:
            return remote(G[a].at[mine], G[a].at[mine], ga_s.at[a, kind], ga_r.at[a, kind], ((s1, s2)[kind], c, z))
        ref = half_of(a, c * S + (s1, s2)[kind - 2], kind - 2)
        return remote(ref, ref, ga_s.at[a, kind], ga_r.at[a, kind], ((s2, s1)[kind - 2], c, z))

    def ga_in(a, kind):
        if kind < 2:
            ref = G[a].at[c * S + (s1, s2)[kind]]
        else:
            ref = half_of(a, c * S + s3, kind - 2)
        return remote(ref, ref, ga_s.at[a, kind], ga_r.at[a, kind], (s1, c, z))

    def gc(a):
        ref = G[a].at[pl.ds(c * S, S)]
        return remote(ref, ref, gc_s.at[a], gc_r.at[a], sib)

    def gc_in(a):
        ref = G[a].at[pl.ds((1 - c) * S, S)]
        return remote(ref, ref, gc_s.at[a], gc_r.at[a], sib)

    def g_send(a):
        ga(a, 0).start()
        ga(a, 1).start()

    def g_forward(a):
        for kind in range(2):
            ga_in(a, kind).wait_recv()
            ga(a, 2 + kind).start()

    def g_core(a):
        for kind in range(2):
            ga_in(a, 2 + kind).wait_recv()
        gc(a).start()

    def g_end(a):
        gc_in(a).wait_recv()

    def drain(a):
        core_move(a).wait_send()
        for half in range(2):
            x1(a, half, 0).wait_send()
            x1(a, half, 1).wait_send()
            x2(a, half).wait_send()
        for t, q in enumerate(zz):
            za(a, q, t).wait_send()
        for kind in range(4):
            ga(a, kind).wait_send()
        gc(a).wait_send()

    stages = dict(core_add=core_add, x1_send=x1_send, x1_add=x1_add, x2_send=x2_send, x2_add=x2_add, z_send=z_send,
                  z_add=z_add, g_send=g_send, g_forward=g_forward, g_core=g_core,
                  vec_plane=lambda a: vec_plane(), vec_z=lambda a: vec_z(), vec_end=lambda a: vec_end())

    vec_core()
    eighth = pd.shape[3]
    down_rows = 8 * eighth
    for j in range(W):
        made = tn(active[:, j * down_rows : (j + 1) * down_rows], grad_branch[...]).astype(bf16)
        for e in range(8):
            for half in range(2):
                pd[j, e, half] = made[e * eighth : (e + 1) * eighth, half * half_width : (half + 1) * half_width]
    core_move(0).start()
    part = grad_inner.shape[1] // 8
    half_rows = group // 2
    for e in range(8):
        made = tn(hidden[...], grad_inner[:, e * part : (e + 1) * part]).astype(bf16)
        for j in range(W):
            for half in range(2):
                lo = j * group + half * half_rows
                pi[j, e, half] = made[lo : lo + half_rows]
    core_move(1).start()

    def store_eighths(ref, made):
        size = group // 8
        for j in range(W):
            for e in range(8):
                for half in range(2):
                    lo = j * group + e * size
                    ref[j, e, half] = made[lo : lo + size, half * half_width : (half + 1) * half_width]

    store_eighths(po, tn(context[...], grad_attn[...]).astype(bf16))
    core_move(2).start()
    kt[...] = kx[:, :group].astype(f32).T.astype(bf16)
    dk[...] = jnp.zeros_like(dk)
    dv[...] = jnp.zeros_like(dv)
    core_add(0)
    x1_send(0)
    core_add(1)
    x1_send(1)

    chunk = dims["chunk"]
    n_chunks = total // chunk
    lane = lax.broadcasted_iota(jnp.int32, (1, LANES), 1)

    def attend(step, carry):
        i = lax.div(step, heads)
        h = lax.rem(step, heads)
        b = lax.rem(z + i, W)

        @pl.when((h == 0) & (i > 0))
        def _():
            da_in(b).wait_recv()

        at = pl.ds(pl.multiple_of(b * rows, rows), rows)
        here = pl.ds(pl.multiple_of(h * head_dim, head_dim), head_dim)
        got = d_recv[b].astype(f32)
        got = jnp.concatenate([got, jnp.zeros((rows, LANES - group), f32)], axis=1)
        mask = (lane >= h * head_dim) & (lane < (h + 1) * head_dim)
        grad = jnp.where(mask, got, 0.0)
        delta = jnp.sum(grad.T[:group] * att_t[:, at], axis=0, keepdims=True)
        grad = grad.astype(bf16)
        query = qx[pl.ds(pl.multiple_of(h * block + b * rows, rows), rows), :]
        log_mass = lse[h, :, at]
        acc = None
        for n in range(n_chunks):
            span = slice(n * chunk, (n + 1) * chunk)
            weights = jnp.exp(nt(kx[span, :], query) - log_mass)
            grad_weights = nt(vv[span, :], grad)
            grad_scores = (weights * (grad_weights - delta)).astype(bf16)
            dv[span, :] += nn(weights.astype(bf16), grad)
            dk[span, :] += nn(grad_scores, query)
            add = nn(kt[here, span], grad_scores)
            acc = add if acc is None else acc + add
        dq_t[here, at] = acc * dims["scale"]

        for when, name, a in dims["back_moves"]:
            @pl.when(step == when)
            def _():
                stages[name](a)

        return carry

    lax.fori_loop(0, W * heads, attend, 0)

    def kv_move():
        return remote(kv_send, kv_recv, kv_s.at[0], kv_r.at[0], sib)

    other = pl.ds(pl.multiple_of((1 - c) * block, block), block)
    own = pl.ds(pl.multiple_of(c * block, block), block)
    kv_send[0] = dk[other, :].astype(bf16)
    kv_send[1] = dv[other, :].astype(bf16)
    kv_move().start()
    pad = jnp.zeros((block, LANES - group), bf16)
    dqkv[:, :LANES] = jnp.concatenate([dq_t[...].T.astype(bf16), pad], axis=1)
    kv_move().wait_recv()
    keep = lane < group
    for m, ref in ((0, dk), (1, dv)):
        whole = ref[own, :] + kv_recv[m].astype(f32)
        dqkv[:, (m + 1) * LANES : (m + 2) * LANES] = jnp.where(keep, whole, 0.0).astype(bf16)

    def rx_out(d, step, lane_):
        return remote(px.at[d], rx.at[lane_, d], rx_s.at[d], rx_r.at[lane_, d], (s, c, z + step))

    def make(d):
        at = pl.ds(pl.multiple_of(d * rows, rows), rows)
        return nt(dqkv[at, :], wcol[...])

    def line(k, carry):
        far = W - 1 - lax.div(k, 2)
        right = lax.rem(k, 2) == 0
        d = jnp.where(right, far, W - 1 - far)

        @pl.when(right & (d > z))
        def _():
            px[d] = make(d).astype(bf16)

            @pl.when(z > 0)
            def _():
                rx_out(d, 1, 0).wait_recv()
                px[d] = (px[d].astype(f32) + rx[0, d].astype(f32)).astype(bf16)

            rx_out(d, 1, 0).start()

        @pl.when(jnp.logical_not(right) & (d < z))
        def _():
            px[d] = make(d).astype(bf16)

            @pl.when(z < W - 1)
            def _():
                rx_out(d, -1, 1).wait_recv()
                px[d] = (px[d].astype(f32) + rx[1, d].astype(f32)).astype(bf16)

            rx_out(d, -1, 1).start()

        return carry

    lax.fori_loop(0, 2 * (W - 1), line, 0)
    made = None
    for j in range(W):
        add = tn(toks[j], dqkv[j * rows : (j + 1) * rows, :])
        made = add if made is None else made + add
    store_eighths(pq, made.astype(bf16))
    core_move(3).start()
    ones = jnp.ones((8, block), bf16)
    sums = nn(ones, dqkv[...])[0:1]
    bc[c] = jnp.concatenate([sums[:, :LANES], sums[:, 2 * LANES :]], axis=1)

    def bcore():
        return remote(bc.at[c], bc.at[c], bp_s.at[0], bp_r.at[0], sib)

    def bplane(k):
        return remote(bs.at[s], bs.at[s], bp_s.at[k], bp_r.at[k], (s ^ k, c, z))

    bcore().start()
    g_tok[...] = make(z) + res[...]
    for name, a in dims["back_late"]:
        stages[name](a)
    bcore().wait_recv()
    bs[s] = bc[0] + bc[1]
    for k in (1, 2, 3):
        bplane(k).start()
    for name, a in dims["back_last"]:
        stages[name](a)

    @pl.when(z > 0)
    def _():
        rx_out(z, 1, 0).wait_recv()
        g_tok[...] += rx[0, z].astype(f32)

    @pl.when(z < W - 1)
    def _():
        rx_out(z, -1, 1).wait_recv()
        g_tok[...] += rx[1, z].astype(f32)

    for k in (1, 2, 3):
        bplane(k).wait_recv()
    tot = (bs[0] + bs[1]) + (bs[2] + bs[3])
    g_b[...] = tot
    bcore().wait_send()
    for k in (1, 2, 3):
        bplane(k).wait_send()
    kv_move().wait_send()
    for q in zz:
        da(q).wait_send()
    for j in range(W):
        @pl.when(j > z)
        def _():
            rx_out(j, 1, 0).wait_send()

        @pl.when(j < z)
        def _():
            rx_out(j, -1, 1).wait_send()

    for a in range(4):
        g_end(a)
    for a in range(4):
        drain(a)


def back_call(dims, *operands):
    toks, wcol, qx, kx, vv, att_t, lse, grad_ctx, res, active, grad_branch, hidden, grad_inner, context, grad_attn, vec = operands
    S, W, heads = dims["S"], dims["W"], dims["heads"]
    rows, width = grad_ctx.shape
    ff = active.shape[1]
    group = width // W
    block = rows * W
    total = 2 * block
    f32, bf16 = jnp.float32, jnp.bfloat16
    vm = pl.BlockSpec(memory_space=pltpu.VMEM)
    dma = pltpu.SemaphoreType.DMA
    shape = jax.ShapeDtypeStruct
    half = width // 2
    sizes = (ff // W // 8, group // 2, group // 8, group // 8)
    assert ff // 8 == half
    n_vec = vec.shape[2]
    pieces = [pltpu.VMEM((W, 8, 2, r, half), bf16) for r in sizes]
    cores = [pltpu.VMEM((W, S, 2, r, half), bf16) for r in sizes]
    x1s = [pltpu.VMEM((2, 2, W, r, half), bf16) for r in sizes]
    x2s = [pltpu.VMEM((2, W, r, half), bf16) for r in sizes]
    zs = [pltpu.VMEM((W, 2, r, half), bf16) for r in sizes]
    return pl.pallas_call(
        partial(back_kernel, dims),
        name="attend_back_sum",
        out_shape=(
            shape((rows, width), f32),
            *[shape((8, 2, r, half), bf16) for r in sizes[:3]],
            shape((8, W, 2, sizes[3], half), bf16),
            shape((1, n_vec), f32),
            shape((1, 2 * LANES), f32),
        ),
        in_specs=[vm] * 16,
        out_specs=tuple([vm] * 7),
        scratch_shapes=[
            pltpu.VMEM((W, rows, group), bf16),
            pltpu.VMEM((W, rows, group), bf16),
            pltpu.VMEM((group, total), bf16),
            pltpu.VMEM((total, LANES), f32),
            pltpu.VMEM((total, LANES), f32),
            pltpu.VMEM((group, block), f32),
            pltpu.VMEM((block, 3 * LANES), bf16),
            pltpu.VMEM((2, block, LANES), bf16),
            pltpu.VMEM((2, block, LANES), bf16),
            pltpu.VMEM((W, rows, width), bf16),
            pltpu.VMEM((2, W, rows, width), bf16),
            *pieces, *cores, *x1s, *x2s, *zs,
            pltpu.VMEM((W, 1, n_vec), f32),
            pltpu.VMEM((2, W, 1, n_vec), f32),
            pltpu.VMEM((S, W, 1, n_vec), f32),
            pltpu.VMEM((W, 1, n_vec), f32),
            pltpu.VMEM((1, 2 * LANES), f32),
            pltpu.VMEM((2, 1, 2 * LANES), f32),
            pltpu.VMEM((S, 1, 2 * LANES), f32),
            dma((W,)), dma((W,)), dma((1,)), dma((1,)), dma((W,)), dma((2, W)),
            dma((4,)), dma((4,)), dma((4, 4)), dma((4, 4)), dma((4, 2)), dma((4, 2)),
            dma((4, W)), dma((4, W)), dma((4, 4)), dma((4, 4)), dma((4,)), dma((4,)),
            dma((4 + W,)), dma((4 + W,)), dma((4,)), dma((4,)),
        ],
        compiler_params=pltpu.CompilerParams(
            collective_id=2, has_side_effects=True, vmem_limit_bytes=VMEM_LIMIT
        ),
    )(*operands)


def finish_kernel(dims, result, g_tok, gd, gi, go, gq, vec, g_b,
                  o_res, o_tok, o_q, o_bq, o_k, o_v, o_bv, o_o, o_s0, o_s1, o_s2, o_i, o_s3, o_d, o_s4, o_s5, o_s6):
    f32 = jnp.float32
    W = dims["W"]
    group = o_q.shape[0]
    eighth, half_width = gd.shape[2:]
    half_rows = gi.shape[2]
    o_res[0] = result[...].astype(jnp.bfloat16)
    o_tok[0] = g_tok[...].astype(jnp.bfloat16)
    for e in range(8):
        for half in range(2):
            lanes = slice(half * half_width, (half + 1) * half_width)
            o_d[e * eighth : (e + 1) * eighth, lanes] = gd[e, half].astype(f32)
            o_i[half * half_rows : (half + 1) * half_rows, e * half_width : (e + 1) * half_width] = gi[e, half].astype(f32)
            size = group // 8
            o_o[e * size : (e + 1) * size, lanes] = go[e, half].astype(f32)
    size = group // 8
    for e in range(8):
        for j in range(W):
            both = jnp.concatenate([gq[e, j, 0].astype(f32), gq[e, j, 1].astype(f32)], axis=1)
            for m, ref in enumerate((o_q, o_k, o_v)):
                ref[e * size : (e + 1) * size, j * group : (j + 1) * group] = both[:, m * LANES : m * LANES + group]
    o_bq[...] = g_b[0, :group]
    o_bv[...] = g_b[0, LANES : LANES + group]
    for ref, (lo, hi) in zip((o_s0, o_s1, o_s2, o_s3, o_s4, o_s5, o_s6), shift_cuts(group, o_s3.shape[0])):
        ref[...] = vec[0, lo:hi]


def finish_call(dims, result, g_tok, gd, gi, go, gq, vec, g_b):
    f32, bf16 = jnp.float32, jnp.bfloat16
    W = dims["W"]
    rows, width = result.shape
    group = width // W
    ff = width * W
    vm = pl.BlockSpec(memory_space=pltpu.VMEM)
    shape = jax.ShapeDtypeStruct
    small, mat = shape((group,), f32), shape((group, width), f32)
    return pl.pallas_call(
        partial(finish_kernel, dims),
        name="finish",
        out_shape=(shape((1, rows, width), bf16), shape((1, rows, width), bf16), mat, small, mat, mat, small, mat,
                   small, small, small, shape((group, ff), f32), shape((ff // W,), f32), shape((ff // W, width), f32),
                   small, small, small),
        in_specs=[vm] * 8,
        out_specs=tuple([vm] * 17),
        compiler_params=pltpu.CompilerParams(vmem_limit_bytes=VMEM_LIMIT),
    )(result, g_tok, gd, gi, go, gq, vec, g_b)


def shift_cuts(small, large):
    edges = [0]
    for n in (small, small, small, large, small, small, small):
        edges.append(edges[-1] + n)
    return list(zip(edges[:-1], edges[1:]))


def fast_device(dims, tokens, segment_ids, w_query, b_query, w_key, w_value, b_value, w_out, b_out, gain_attn,
                shift_attn, w_in, b_in, w_down, b_down, gain_ffn, shift_ffn, cotangent):
    f32, bf16 = jnp.float32, jnp.bfloat16
    W = dims["W"]
    inputs = tokens[0]
    vec = jnp.concatenate([b_out, gain_attn, shift_attn, b_in, b_down, gain_ffn, shift_ffn]).astype(f32)[None]
    got = attend_call(dims, inputs, segment_ids.astype(f32), w_query, w_key, w_value, b_query.astype(f32)[None],
                      b_value.astype(f32)[None], vec, w_out, w_in, w_down)
    toks, wcol, qx, kx, vv, att_t, lse, context, full_out, full_in, full_down, vecs = got
    cuts = shift_cuts(b_out.shape[0], b_in.shape[0])
    bias_out, gain_one, shift_one, bias_in, bias_down, gain_two, shift_two = [
        vecs[:, 0, lo:hi].reshape(-1) for lo, hi in cuts
    ]
    attn_out = matmul(context, full_out) + bias_out
    hidden, normed_one, inverse_one = normalize(inputs.astype(f32) + attn_out, gain_one, shift_one)
    hidden_low = hidden.astype(bf16)
    inner = matmul(hidden_low, full_in) + bias_in
    active_float, gelu_pull = jax.vjp(partial(jax.nn.gelu, approximate=False), inner)
    active = active_float.astype(bf16)
    branch = matmul(active, full_down) + bias_down
    result, normed_two, inverse_two = normalize(hidden + branch, gain_two, shift_two)
    grad_res_two, grad_gain_two, grad_shift_two = normalize_back(
        cotangent[0].astype(f32), normed_two, inverse_two, gain_two
    )
    grad_branch = grad_res_two.astype(bf16)
    grad_bias_down = jnp.sum(grad_branch.astype(f32), axis=0)
    grad_inner = gelu_pull(matmul_right_t(grad_branch, full_down))[0].astype(bf16)
    grad_bias_in = jnp.sum(grad_inner.astype(f32), axis=0)
    grad_hidden = grad_res_two + matmul_right_t(grad_inner, full_in)
    grad_res_one, grad_gain_one, grad_shift_one = normalize_back(grad_hidden, normed_one, inverse_one, gain_one)
    grad_attn = grad_res_one.astype(bf16)
    grad_bias_out = jnp.sum(grad_attn.astype(f32), axis=0)
    grad_context = matmul_right_t(grad_attn, full_out).astype(bf16)
    grad_vec = jnp.concatenate(
        [v.reshape(W, -1) for v in (grad_bias_out, grad_gain_one, grad_shift_one, grad_bias_in, grad_bias_down,
                                    grad_gain_two, grad_shift_two)], axis=1)[:, None]
    back = back_call(
        dims, toks, wcol, qx, kx, vv, att_t, lse, grad_context, grad_res_one, active, grad_branch, hidden_low, grad_inner,
        context, grad_attn, grad_vec)
    return finish_call(dims, result, *back)


def plan(mesh):
    return dict(
        S=mesh.shape["seq"], W=mesh.shape["wsh"], heads=HEADS // mesh.shape["wsh"], scale=0.125, chunk=512,
        moves=[(0, 0, 0), (1, 0, 2), (0, 1, 2), (0, 2, 4), (1, 1, 5), (2, 0, 8), (1, 2, 9)],
        late=[(2, 1), (2, 2)],
        back_moves=[(0, "vec_plane", 0), (1, "core_add", 2), (1, "x1_send", 2), (3, "vec_z", 0), (4, "x1_add", 0), (4, "x2_send", 0),
                    (7, "x2_add", 0), (7, "z_send", 0), (9, "x1_add", 1), (9, "x2_send", 1), (11, "vec_end", 0)],
        back_late=[("z_add", 0), ("g_send", 0), ("x2_add", 1), ("z_send", 1), ("x1_add", 2), ("x2_send", 2),
                   ("core_add", 3), ("x1_send", 3), ("x2_add", 2), ("z_send", 2), ("g_forward", 0), ("x1_add", 3), ("x2_send", 3),
                   ("z_add", 1), ("g_send", 1)],
        back_last=[("x2_add", 3), ("z_send", 3), ("g_core", 0), ("z_add", 2), ("g_send", 2), ("g_forward", 1),
                   ("z_add", 3), ("g_send", 3), ("g_core", 1), ("g_forward", 2), ("g_forward", 3), ("g_core", 2), ("g_core", 3)],
    )


def solution(mesh):
    fast = mesh.shape["seq"] == 4 and mesh.shape["ctx"] == 2 and HEADS % mesh.shape["wsh"] == 0
    return jax.shard_map(
        partial(fast_device, plan(mesh)) if fast else per_device,
        mesh=mesh,
        in_specs=(
            P("seq", ("ctx", "wsh"), None),
            P("seq", ("ctx", "wsh")),
            P("wsh", None),
            P("wsh"),
            P("wsh", None),
            P("wsh", None),
            P("wsh"),
            P("wsh", None),
            P("wsh"),
            P("wsh"),
            P("wsh"),
            P("wsh", None),
            P("wsh"),
            P("wsh", None),
            P("wsh"),
            P("wsh"),
            P("wsh"),
            P("seq", ("ctx", "wsh"), None),
        ),
        out_specs=(
            P("seq", ("ctx", "wsh"), None),
            P("seq", ("ctx", "wsh"), None),
            P("wsh", None),
            P("wsh"),
            P("wsh", None),
            P("wsh", None),
            P("wsh"),
            P("wsh", None),
            P("wsh"),
            P("wsh"),
            P("wsh"),
            P("wsh", None),
            P("wsh"),
            P("wsh", None),
            P("wsh"),
            P("wsh"),
            P("wsh"),
        ),
        check_vma=False,
    )
```

```python
from functools import partial
import math

import jax
import jax.numpy as jnp
from jax import lax
from jax.experimental import pallas as pl
from jax.experimental.pallas import tpu as pltpu
from jax.sharding import PartitionSpec as P

HEADS = 12


norm_eps = 1e-12
masked_fill = -1e30


def matmul(left, right):
    return jnp.dot(left, right, preferred_element_type=jnp.float32)


def matmul_left_t(left, right):
    return lax.dot_general(
        left, right, (((0,), (0,)), ((), ())), preferred_element_type=jnp.float32
    )


def matmul_right_t(left, right):
    return lax.dot_general(
        left, right, (((1,), (1,)), ((), ())), preferred_element_type=jnp.float32
    )


def normalize(values, gain, shift):
    centre = jnp.mean(values, axis=-1, keepdims=True)
    centred = values - centre
    inverse = lax.rsqrt(jnp.mean(centred * centred, axis=-1, keepdims=True) + norm_eps)
    normed = centred * inverse
    return (normed * gain + shift, normed, inverse)


def normalize_back(grad_out, normed, inverse, gain):
    grad_gain = jnp.sum(grad_out * normed, axis=0)
    grad_shift = jnp.sum(grad_out, axis=0)
    scaled = grad_out * gain
    grad_in = inverse * (
        scaled
        - jnp.mean(scaled, axis=-1, keepdims=True)
        - normed * jnp.mean(scaled * normed, axis=-1, keepdims=True)
    )
    return (grad_in, grad_gain, grad_shift)


def block_scores(query_blk, key_blk, seg_query, seg_key, score_scale):
    scores = (
        jnp.einsum("qhd,khd->hqk", query_blk, key_blk, preferred_element_type=jnp.float32)
        * score_scale
    )
    same_doc = seg_query[:, None] == seg_key[None, :]
    return (jnp.where(same_doc[None], scores, masked_fill), same_doc)


def block_grads(
    query_blk, dctx_blk, lse_blk, delta_blk, seg_query, key_blk, value_blk, seg_key, score_scale
):
    scores, same_doc = block_scores(query_blk, key_blk, seg_query, seg_key, score_scale)
    weights = jnp.where(same_doc[None], jnp.exp(scores - lse_blk.T[:, :, None]), 0.0)
    grad_weights = jnp.einsum(
        "qhd,khd->hqk", dctx_blk, value_blk, preferred_element_type=jnp.float32
    )
    grad_scores = (weights * (grad_weights - delta_blk.T[:, :, None])).astype(jnp.bfloat16)
    grad_query = None
    grad_key = None
    grad_value = None
    grad_query = (
        jnp.einsum("hqk,khd->qhd", grad_scores, key_blk, preferred_element_type=jnp.float32)
        * score_scale
    )
    grad_key = (
        jnp.einsum("hqk,qhd->khd", grad_scores, query_blk, preferred_element_type=jnp.float32)
        * score_scale
    )
    grad_value = jnp.einsum(
        "hqk,qhd->khd", weights.astype(jnp.bfloat16), dctx_blk, preferred_element_type=jnp.float32
    )
    return (grad_query, grad_key, grad_value)


def per_device(
    tokens,
    segment_ids,
    w_query,
    b_query,
    w_key,
    w_value,
    b_value,
    w_out,
    b_out,
    gain_attn,
    shift_attn,
    w_in,
    b_in,
    w_down,
    b_down,
    gain_ffn,
    shift_ffn,
    cotangent,
):
    (
        full_query,
        bias_query,
        full_key,
        full_value,
        bias_value,
        full_out,
        bias_out,
        gain_one,
        shift_one,
        full_in,
        bias_in,
        full_down,
        bias_down,
        gain_two,
        shift_two,
    ) = (
        lax.all_gather(w_query, "wsh", axis=0, tiled=True),
        lax.all_gather(b_query, "wsh", axis=0, tiled=True),
        lax.all_gather(w_key, "wsh", axis=0, tiled=True),
        lax.all_gather(w_value, "wsh", axis=0, tiled=True),
        lax.all_gather(b_value, "wsh", axis=0, tiled=True),
        lax.all_gather(w_out, "wsh", axis=0, tiled=True),
        lax.all_gather(b_out, "wsh", axis=0, tiled=True),
        lax.all_gather(gain_attn, "wsh", axis=0, tiled=True),
        lax.all_gather(shift_attn, "wsh", axis=0, tiled=True),
        lax.all_gather(w_in, "wsh", axis=0, tiled=True),
        lax.all_gather(b_in, "wsh", axis=0, tiled=True),
        lax.all_gather(w_down, "wsh", axis=0, tiled=True),
        lax.all_gather(b_down, "wsh", axis=0, tiled=True),
        lax.all_gather(gain_ffn, "wsh", axis=0, tiled=True),
        lax.all_gather(shift_ffn, "wsh", axis=0, tiled=True),
    )
    inputs = tokens[0]
    rows = inputs.shape[0]
    width = inputs.shape[1]
    head_dim = width // HEADS
    score_scale = 1.0 / math.sqrt(head_dim)
    seg_float = segment_ids[0].astype(jnp.bfloat16)
    queries = (matmul(inputs, full_query) + bias_query.astype(jnp.float32)).astype(jnp.bfloat16)
    key_rows = matmul(inputs, full_key).astype(jnp.bfloat16)
    values = (matmul(inputs, full_value) + bias_value.astype(jnp.float32)).astype(jnp.bfloat16)
    keys_all, values_all, segs_all = (
        lax.all_gather(key_rows, ("ctx", "wsh"), axis=0, tiled=True),
        lax.all_gather(values, ("ctx", "wsh"), axis=0, tiled=True),
        lax.all_gather(seg_float, ("ctx", "wsh"), axis=0, tiled=True),
    )
    total = keys_all.shape[0]
    key_block = min(512, total)
    block_count = total // key_block
    key_blocks = keys_all.reshape(block_count, key_block, HEADS, head_dim)
    value_blocks = values_all.reshape(block_count, key_block, HEADS, head_dim)
    seg_blocks = segs_all.reshape(block_count, key_block)
    query_heads = queries.reshape(rows, HEADS, head_dim)

    def forward_block(carry, block):
        run_max, run_sum, accum = carry
        key_blk, value_blk, seg_blk = block
        scores, same_doc = block_scores(query_heads, key_blk, seg_float, seg_blk, score_scale)
        new_max = jnp.maximum(run_max, jnp.max(scores, axis=2))
        raised = jnp.where(same_doc[None], jnp.exp(scores - new_max[:, :, None]), 0.0)
        factor = jnp.exp(run_max - new_max)
        run_sum = run_sum * factor + jnp.sum(raised, axis=2)
        accum = accum * factor.T[:, :, None] + jnp.einsum(
            "hqk,khd->qhd",
            raised.astype(jnp.bfloat16),
            value_blk,
            preferred_element_type=jnp.float32,
        )
        return ((new_max, run_sum, accum), None)

    start_state = (
        jnp.full((HEADS, rows), masked_fill, jnp.float32),
        jnp.zeros((HEADS, rows), jnp.float32),
        jnp.zeros((rows, HEADS, head_dim), jnp.float32),
    )
    (run_max, run_sum, accum), unused = lax.scan(
        forward_block, start_state, (key_blocks, value_blocks, seg_blocks)
    )
    attended = accum / run_sum.T[:, :, None]
    lse_rows = (run_max + jnp.log(run_sum)).T
    context = attended.reshape(rows, width).astype(jnp.bfloat16)
    attn_out = matmul(context, full_out) + bias_out.astype(jnp.float32)
    gain_first = gain_one.astype(jnp.float32)
    gain_second = gain_two.astype(jnp.float32)
    hidden, normed_one, inverse_one = normalize(
        inputs.astype(jnp.float32) + attn_out, gain_first, shift_one.astype(jnp.float32)
    )
    hidden_low = hidden.astype(jnp.bfloat16)
    inner = matmul(hidden_low, full_in) + bias_in.astype(jnp.float32)
    active_float, gelu_pull = jax.vjp(partial(jax.nn.gelu, approximate=False), inner)
    active = active_float.astype(jnp.bfloat16)
    branch = matmul(active, full_down) + bias_down.astype(jnp.float32)
    result, normed_two, inverse_two = normalize(
        hidden + branch, gain_second, shift_two.astype(jnp.float32)
    )
    grad_out = cotangent[0].astype(jnp.float32)
    grad_res_two, grad_gain_two, grad_shift_two = normalize_back(
        grad_out, normed_two, inverse_two, gain_second
    )
    grad_branch = grad_res_two.astype(jnp.bfloat16)
    grad_bias_down = jnp.sum(grad_branch.astype(jnp.float32), axis=0)
    grad_full_down = matmul_left_t(active, grad_branch)
    grad_inner = gelu_pull(matmul_right_t(grad_branch, full_down))[0].astype(jnp.bfloat16)
    grad_bias_in = jnp.sum(grad_inner.astype(jnp.float32), axis=0)
    grad_full_in = matmul_left_t(hidden_low, grad_inner)
    grad_hidden = grad_res_two + matmul_right_t(grad_inner, full_in)
    grad_res_one, grad_gain_one, grad_shift_one = normalize_back(
        grad_hidden, normed_one, inverse_one, gain_first
    )
    grad_attn = grad_res_one.astype(jnp.bfloat16)
    grad_bias_out = jnp.sum(grad_attn.astype(jnp.float32), axis=0)
    grad_full_out = matmul_left_t(context, grad_attn)
    grad_context = matmul_right_t(grad_attn, full_out).astype(jnp.bfloat16)
    dctx_heads = grad_context.reshape(rows, HEADS, head_dim)
    delta_rows = jnp.sum(dctx_heads.astype(jnp.float32) * attended, axis=2)
    zero_heads = jnp.zeros((rows, HEADS, head_dim), jnp.float32)

    def back_block(grad_acc, block):
        key_blk, value_blk, seg_blk = block
        part_query, part_key, part_value = block_grads(
            query_heads,
            dctx_heads,
            lse_rows,
            delta_rows,
            seg_float,
            key_blk,
            value_blk,
            seg_blk,
            score_scale,
        )
        return (grad_acc + part_query, (part_key, part_value))

    grad_q, (key_parts, value_parts) = lax.scan(
        back_block, zero_heads, (key_blocks, value_blocks, seg_blocks)
    )
    grad_key_own, grad_value_own = (
        lax.psum_scatter(
            key_parts.reshape(total, width), ("ctx", "wsh"), scatter_dimension=0, tiled=True
        ),
        lax.psum_scatter(
            value_parts.reshape(total, width), ("ctx", "wsh"), scatter_dimension=0, tiled=True
        ),
    )
    grad_queries = grad_q.reshape(rows, width).astype(jnp.bfloat16)
    grad_keys = grad_key_own.astype(jnp.bfloat16)
    grad_values = grad_value_own.astype(jnp.bfloat16)
    grad_full_query = matmul_left_t(inputs, grad_queries)
    grad_bias_query = jnp.sum(grad_queries.astype(jnp.float32), axis=0)
    grad_full_key = matmul_left_t(inputs, grad_keys)
    grad_full_value = matmul_left_t(inputs, grad_values)
    grad_bias_value = jnp.sum(grad_values.astype(jnp.float32), axis=0)
    grad_input = (
        grad_res_one
        + matmul_right_t(grad_queries, full_query)
        + matmul_right_t(grad_keys, full_key)
        + matmul_right_t(grad_values, full_value)
    )
    (
        share_query,
        share_bias_query,
        share_key,
        share_value,
        share_bias_value,
        share_out,
        share_bias_out,
        share_gain_one,
        share_shift_one,
        share_in,
        share_bias_in,
        share_down,
        share_bias_down,
        share_gain_two,
        share_shift_two,
    ) = (
        lax.psum_scatter(
            grad_full_query.astype(jnp.bfloat16), "wsh", scatter_dimension=0, tiled=True
        ).astype(jnp.float32),
        lax.psum_scatter(
            grad_bias_query.astype(jnp.bfloat16), "wsh", scatter_dimension=0, tiled=True
        ).astype(jnp.float32),
        lax.psum_scatter(
            grad_full_key.astype(jnp.bfloat16), "wsh", scatter_dimension=0, tiled=True
        ).astype(jnp.float32),
        lax.psum_scatter(
            grad_full_value.astype(jnp.bfloat16), "wsh", scatter_dimension=0, tiled=True
        ).astype(jnp.float32),
        lax.psum_scatter(
            grad_bias_value.astype(jnp.bfloat16), "wsh", scatter_dimension=0, tiled=True
        ).astype(jnp.float32),
        lax.psum_scatter(
            grad_full_out.astype(jnp.bfloat16), "wsh", scatter_dimension=0, tiled=True
        ).astype(jnp.float32),
        lax.psum_scatter(
            grad_bias_out.astype(jnp.bfloat16), "wsh", scatter_dimension=0, tiled=True
        ).astype(jnp.float32),
        lax.psum_scatter(
            grad_gain_one.astype(jnp.bfloat16), "wsh", scatter_dimension=0, tiled=True
        ).astype(jnp.float32),
        lax.psum_scatter(
            grad_shift_one.astype(jnp.bfloat16), "wsh", scatter_dimension=0, tiled=True
        ).astype(jnp.float32),
        lax.psum_scatter(
            grad_full_in.astype(jnp.bfloat16), "wsh", scatter_dimension=0, tiled=True
        ).astype(jnp.float32),
        lax.psum_scatter(
            grad_bias_in.astype(jnp.bfloat16), "wsh", scatter_dimension=0, tiled=True
        ).astype(jnp.float32),
        lax.psum_scatter(
            grad_full_down.astype(jnp.bfloat16), "wsh", scatter_dimension=0, tiled=True
        ).astype(jnp.float32),
        lax.psum_scatter(
            grad_bias_down.astype(jnp.bfloat16), "wsh", scatter_dimension=0, tiled=True
        ).astype(jnp.float32),
        lax.psum_scatter(
            grad_gain_two.astype(jnp.bfloat16), "wsh", scatter_dimension=0, tiled=True
        ).astype(jnp.float32),
        lax.psum_scatter(
            grad_shift_two.astype(jnp.bfloat16), "wsh", scatter_dimension=0, tiled=True
        ).astype(jnp.float32),
    )
    summed = lax.psum(
        (
            share_query,
            share_bias_query,
            share_key,
            share_value,
            share_bias_value,
            share_out,
            share_bias_out,
            share_gain_one,
            share_shift_one,
            share_in,
            share_bias_in,
            share_down,
            share_bias_down,
            share_gain_two,
            share_shift_two,
        ),
        ("seq", "ctx"),
    )
    return (
        result.astype(jnp.bfloat16)[None],
        grad_input.astype(jnp.bfloat16)[None],
        summed[0],
        summed[1],
        summed[2],
        summed[3],
        summed[4],
        summed[5],
        summed[6],
        summed[7],
        summed[8],
        summed[9],
        summed[10],
        summed[11],
        summed[12],
        summed[13],
        summed[14],
    )


MESH_ID = pl.DeviceIdType.MESH
LANES = 256
IDS = 16
BIG = float(2.0**99)
VMEM_LIMIT = 60 * 2**20


def remote(src, dst, send, recv, where):
    return pltpu.make_async_remote_copy(
        src_ref=src, dst_ref=dst, send_sem=send, recv_sem=recv, device_id=where, device_id_type=MESH_ID
    )


def nt(left, right):
    return lax.dot_general(left, right, (((1,), (1,)), ((), ())), preferred_element_type=jnp.float32)


def tn(left, right):
    return lax.dot_general(left, right, (((0,), (0,)), ((), ())), preferred_element_type=jnp.float32)


def nn(left, right):
    return jnp.dot(left, right, preferred_element_type=jnp.float32)


def greet(peers):
    barrier = pltpu.get_barrier_semaphore()
    for peer in peers:
        pl.semaphore_signal(barrier, inc=1, device_id=peer, device_id_type=MESH_ID)
    pl.semaphore_wait(barrier, len(peers))


def attend_kernel(
    dims,
    tokens, seg, w_q, w_k, w_v, b_q, b_v, b_o, gain_1, shift_1, b_i, b_d, gain_2, shift_2, cot, w_o, w_i, w_d,
    toks, wcol, qx, kx, vv, att_t, lse, ctx, grad_ctx, res, active, grad_branch, hidden_low, grad_inner, grad_attn,
    grad_vec, result,
    full_o, full_i, full_d, vecs, slope,
    segs, w_send, w_recv, vt, scores, ctx_send, ctx_recv,
    tok_s, tok_r, sv_s, sv_r, wz_s, wz_r, wp_s, wp_r, kv_s, kv_r, cx_s, cx_r,
    fz_s, fz_r, fx_s, fx_r, fc_s, fc_r, loc,
):
    S, W, heads = dims["S"], dims["W"], dims["heads"]
    rows, width = tokens.shape
    group = width // W
    head_dim = group // heads
    block = rows * W
    total = 2 * block
    s, c, z = lax.axis_index("seq"), lax.axis_index("ctx"), lax.axis_index("wsh")
    sib = (s, 1 - c, z)
    s1, s2, s3 = s ^ 1, s ^ 2, s ^ 3
    shifts = list(range(1, W))
    zz = [lax.rem(z + t, W) for t in shifts]
    barrier = pltpu.get_barrier_semaphore()
    peers = [sib] + [(p, c, z) for p in (s1, s2, s3)] + [(s, c, q) for q in zz]
    for peer in peers:
        pl.semaphore_signal(barrier, inc=1, device_id=peer, device_id_type=MESH_ID)
    toks[z] = tokens[...]
    segs[z] = seg[...].astype(jnp.float32)
    for ref, lo in zip((b_o, gain_1, shift_1, b_d, gain_2, shift_2, b_i), dims["cuts"]):
        vecs[z, :, lo : lo + ref.shape[0]] = ref[...].astype(jnp.float32).reshape(1, -1)

    eighth = group // 8
    piece = c * S + s
    for j in range(W):
        for m, ref in enumerate((w_q, w_k, w_v)):
            part = ref[:, j * group : (j + 1) * group]
            part = jnp.concatenate([part, jnp.zeros((group, LANES - group), part.dtype)], axis=1)
            for e in range(8):
                w_send[j, e, :, m * LANES : (m + 1) * LANES] = part[e * eighth : (e + 1) * eighth]

    pl.semaphore_wait(barrier, len(peers))

    def wz(q):
        return remote(w_send.at[q, piece], w_recv.at[z, piece], wz_s.at[q], wz_r.at[z], (s, c, q))

    def wz_in(q):
        return remote(w_send.at[q, piece], w_recv.at[q, piece], wz_s.at[q], wz_r.at[q], (s, c, q))

    def seg_out(q):
        return remote(segs.at[z], segs.at[z], sv_s.at[0, q], sv_r.at[0, z], (s, c, q))

    def seg_in(q):
        return remote(segs.at[q], segs.at[q], sv_s.at[0, q], sv_r.at[0, q], (s, c, q))

    def vec_out(q):
        return remote(vecs.at[z], vecs.at[z], sv_s.at[1, q], sv_r.at[1, z], (s, c, q))

    def vec_in(q):
        return remote(vecs.at[q], vecs.at[q], sv_s.at[1, q], sv_r.at[1, q], (s, c, q))

    def tok_copy(slot, step, lane):
        return remote(toks.at[slot], toks.at[slot], tok_s.at[lane, slot], tok_r.at[slot], (s, c, z + step))

    for q in zz:
        wz(q).start()
        seg_out(q).start()

    @pl.when(z + 1 < W)
    def _():
        tok_copy(z, 1, 0).start()

    @pl.when(z > 0)
    def _():
        tok_copy(z, -1, 1).start()

    for q in zz:
        vec_out(q).start()

    parts = ((w_o, full_o), (w_i, full_i), (w_d, full_d))

    def spot_of(ref, base, part, cc, ss, half):
        n, m = parts[part][0].shape
        if part == 0:
            row, col, size, wide = (0 if ss is None else ss * (n // S)), cc * (m // 2), n // S, m // 2
            if ss is None:
                size = n
            if half is not None:
                col, wide = col + (0 if half == 0 else 128), (128 if half == 0 else m // 2 - 128)
        elif part == 1:
            wide = m // 2 if ss is None else m // 8
            row, col, size = 0, cc * (m // 2) + (0 if ss is None else ss * (m // 8)), n
            if half is not None:
                row, size = half * (n // 2), n // 2
        else:
            size = n // 2 if ss is None else n // 8
            row, col, wide = cc * (n // 2) + (0 if ss is None else ss * (n // 8)), 0, m
            if half is not None:
                col, wide = half * (m // 2), m // 2
        row = base + row
        if not isinstance(row, int):
            row = pl.multiple_of(row, 16)
        if not isinstance(col, int):
            col = pl.multiple_of(col, 128)
        return ref.at[pl.ds(row, size), pl.ds(col, wide)]

    def rows_of(part, q, cc, ss, half=None):
        return spot_of(parts[part][1], q * parts[part][0].shape[0], part, cc, ss, half)

    def own_copy(part):
        n = parts[part][0].shape[0]
        return pltpu.make_async_copy(
            parts[part][0], parts[part][1].at[pl.ds(pl.multiple_of(z * n, 16), n), :], loc.at[part]
        )

    def fz(part, q):
        src = spot_of(parts[part][0], 0, part, c, s, None)
        return remote(src, rows_of(part, z, c, s), fz_s.at[part, q], fz_r.at[part, z], (s, c, q))

    def fz_in(part, q):
        here = rows_of(part, q, c, s)
        return remote(here, here, fz_s.at[part, q], fz_r.at[part, q], (s, c, q))

    def fx(part, q, kind):
        if kind < 2:
            ref, to = rows_of(part, q, c, s), (s1, s2)[kind]
        else:
            ref, to = rows_of(part, q, c, (s1, s2)[kind - 2], kind - 2), (s2, s1)[kind - 2]
        return remote(ref, ref, fx_s.at[part, q, kind], fx_r.at[part, q, kind], (to, c, z))

    def fx_in(part, q, kind):
        if kind < 2:
            ref = rows_of(part, q, c, (s1, s2)[kind])
        else:
            ref = rows_of(part, q, c, s3, kind - 2)
        return remote(ref, ref, fx_s.at[part, q, kind], fx_r.at[part, q, kind], (s1, c, z))

    def fc(part, q):
        ref = rows_of(part, q, c, None)
        return remote(ref, ref, fc_s.at[part, q], fc_r.at[part, q], sib)

    def fc_in(part, q):
        ref = rows_of(part, q, 1 - c, None)
        return remote(ref, ref, fc_s.at[part, q], fc_r.at[part, q], sib)

    def w_start(part):
        own_copy(part).start()
        for q in zz:
            fz(part, q).start()

    def w_plane(part):
        for q in zz:
            fz_in(part, q).wait_recv()
            fx(part, q, 0).start()
            fx(part, q, 1).start()

    def w_cross(part):
        for q in zz:
            fx_in(part, q, 0).wait_recv()
            fx(part, q, 2).start()
            fx_in(part, q, 1).wait_recv()
            fx(part, q, 3).start()

    def w_core(part):
        for q in zz:
            fx_in(part, q, 2).wait_recv()
            fx_in(part, q, 3).wait_recv()
            fc(part, q).start()

    def w_ready(part):
        own_copy(part).wait()
        for q in zz:
            fc_in(part, q).wait_recv()

    stages = dict(plane=w_plane, cross=w_cross, core=w_core, start=w_start)

    def w_finish(part):
        for q in zz:
            fz(part, q).wait_send()
            for kind in range(4):
                fx(part, q, kind).wait_send()
            fc(part, q).wait_send()


    def wp(q, kind):
        at = piece if kind < 4 else c * S + (s ^ (kind - 3))
        where = (s ^ (kind + 1), c, z) if kind < 3 else sib
        ref = w_recv.at[q, at]
        return remote(ref, ref, wp_s.at[q, kind], wp_r.at[q, at], where)

    def wp_in(q, at):
        ref = w_recv.at[q, at]
        return remote(ref, ref, wp_s.at[q, 0], wp_r.at[q, at], sib)

    for q in zz:
        wz_in(q).wait_recv()
        for kind in range(4):
            wp(q, kind).start()
    for q in zz:
        for kind in range(4, 7):
            wp_in(q, c * S + (s ^ (kind - 3))).wait_recv()
            wp(q, kind).start()
    for e in range(8):
        w_recv[z, e] = w_send[z, e]
    for q in zz:
        for e in range(S):
            wp_in(q, (1 - c) * S + e).wait_recv()
    for j in range(W):
        for e in range(8):
            wcol[j * group + e * eighth : j * group + (e + 1) * eighth, :] = w_recv[j, e]
    for q in zz:
        seg_in(q).wait_recv()

    lane = lax.broadcasted_iota(jnp.int32, (1, LANES), 1)
    spot = lax.broadcasted_iota(jnp.int32, (IDS, LANES), 1) - lax.broadcasted_iota(jnp.int32, (IDS, LANES), 0)
    lanes_in = lax.broadcasted_iota(jnp.int32, (IDS, LANES), 1)
    in_ext = (lanes_in >= group) & (lanes_in < group + IDS)
    put_q = jnp.where(spot == group, 1.0, 0.0).astype(jnp.bfloat16)
    put_k = jnp.where(in_ext & (spot != group), -BIG, 0.0).astype(jnp.bfloat16)
    pad = jnp.zeros((1, LANES - group), jnp.float32)
    bias_q = jnp.concatenate([b_q[...].astype(jnp.float32).reshape(1, -1), pad], axis=1)
    bias_v = jnp.concatenate([b_v[...].astype(jnp.float32).reshape(1, -1), pad], axis=1)
    ids = lax.broadcasted_iota(jnp.int32, (IDS, rows), 0).astype(jnp.float32)

    def k_rows(owner, slot):
        return pl.ds(pl.multiple_of(owner * block + slot * rows, rows), rows)

    def kv(slot, which):
        ref = (kx, vv)[which].at[k_rows(c, slot), :]
        return remote(ref, ref, kv_s.at[which, slot], kv_r.at[which, slot], sib)

    def kv_in(slot, which):
        ref = (kx, vv)[which].at[k_rows(1 - c, slot), :]
        return remote(ref, ref, kv_s.at[which, slot], kv_r.at[which, slot], sib)

    def project(slot):
        made = nn(toks[slot], wcol[...])
        hot = jnp.where(jnp.broadcast_to(segs[slot], (IDS, rows)) == ids, 1.0, 0.0).astype(jnp.bfloat16)
        q_low = (made[:, :LANES] + bias_q).astype(jnp.bfloat16).astype(jnp.float32) * dims["scale"]
        ext_q = tn(hot, put_q)
        for h in range(heads):
            mine = (lane >= h * head_dim) & (lane < (h + 1) * head_dim)
            qx[pl.ds(pl.multiple_of(h * block + slot * rows, rows), rows), :] = (
                jnp.where(mine, q_low, 0.0) + ext_q
            ).astype(jnp.bfloat16)
        kx[k_rows(c, slot), :] = (made[:, LANES : 2 * LANES] + tn(hot, put_k)).astype(jnp.bfloat16)
        vv[k_rows(c, slot), :] = (made[:, 2 * LANES :] + bias_v).astype(jnp.bfloat16)
        kv(slot, 0).start()
        kv(slot, 1).start()

    def arrive(k, carry):
        far = lax.div(k + 1, 2)
        leftward = lax.rem(k, 2) == 1
        slot = jnp.where(leftward, z - far, z + far)
        there = (slot >= 0) & (slot < W)

        @pl.when(there)
        def _():
            @pl.when(k > 0)
            def _():
                tok_copy(slot, 1, 0).wait_recv()

            @pl.when((k > 0) & leftward & (z + 1 < W))
            def _():
                tok_copy(slot, 1, 0).start()

            @pl.when((k > 0) & jnp.logical_not(leftward) & (z > 0))
            def _():
                tok_copy(slot, -1, 1).start()

            project(slot)

        for part, when in dims["starts"]:
            @pl.when(k == when)
            def _():
                w_start(part)

        return carry

    lax.fori_loop(0, 2 * W - 1, arrive, 0)
    for name, part in dims["mid"]:
        stages[name](part)
    for j in range(W):
        kv_in(j, 0).wait_recv()
        kv_in(j, 1).wait_recv()
    vt[...] = vv[...].astype(jnp.float32).T.astype(jnp.bfloat16)

    chunk = dims["chunk"]
    n_chunks = total // chunk

    def cx(b):
        return remote(ctx_send.at[b], ctx_recv.at[z], cx_s.at[b], cx_r.at[z], (s, c, b))

    def cx_in(b):
        return remote(ctx_send.at[b], ctx_recv.at[b], cx_s.at[b], cx_r.at[b], (s, c, b))

    def attend(step, carry):
        i = lax.div(step, heads)
        h = lax.rem(step, heads)
        b = lax.rem(z + 1 + i, W)
        query = qx[pl.ds(pl.multiple_of(h * block + b * rows, rows), rows), :]
        top = None
        for n in range(n_chunks):
            got = nt(kx[n * chunk : (n + 1) * chunk, :], query)
            scores[n * chunk : (n + 1) * chunk, :] = got
            high = jnp.max(got, axis=0, keepdims=True)
            top = high if top is None else jnp.maximum(top, high)
        mass = None
        out = None
        here = pl.ds(pl.multiple_of(h * head_dim, head_dim), head_dim)
        for n in range(n_chunks):
            raised = jnp.exp(scores[n * chunk : (n + 1) * chunk, :] - top)
            add = jnp.sum(raised, axis=0, keepdims=True)
            mass = add if mass is None else mass + add
            piece_out = nn(vt[here, n * chunk : (n + 1) * chunk], raised.astype(jnp.bfloat16))
            out = piece_out if out is None else out + piece_out
        att_t[here, pl.ds(pl.multiple_of(b * rows, rows), rows)] = out / mass
        lse[h, :, pl.ds(pl.multiple_of(b * rows, rows), rows)] = top + jnp.log(mass)

        @pl.when(h == heads - 1)
        def _():
            done = att_t[:, pl.ds(pl.multiple_of(b * rows, rows), rows)]
            ctx_send[b] = done.T.astype(jnp.bfloat16)

            @pl.when(i < W - 1)
            def _():
                cx(b).start()

            @pl.when(i == W - 1)
            def _():
                ctx_recv[b] = ctx_send[b]

        for when, name, part in dims["moves"]:
            @pl.when(step == when)
            def _():
                stages[name](part)

        return carry

    lax.fori_loop(0, W * heads, attend, 0)
    for name, part in dims["late"]:
        stages[name](part)
    for q in zz:
        cx_in(q).wait_recv()
    for j in range(W):
        ctx[:, j * group : (j + 1) * group] = ctx_recv[j]
    for q in zz:
        vec_in(q).wait_recv()

    f32, bf16 = jnp.float32, jnp.bfloat16
    cuts = dims["cuts"]

    def vec_of(k):
        n = (b_o, gain_1, shift_1, b_d, gain_2, shift_2, b_i)[k].shape[0]
        return jnp.concatenate([vecs[j, :, cuts[k] : cuts[k] + n] for j in range(W)], axis=1)

    def norm(values, gain, shift):
        centred = values - jnp.mean(values, axis=-1, keepdims=True)
        inverse = lax.rsqrt(jnp.mean(centred * centred, axis=-1, keepdims=True) + norm_eps)
        normed = centred * inverse
        return normed * gain + shift, normed, inverse

    def norm_back(grad, normed, inverse, gain):
        scaled = grad * gain
        return inverse * (
            scaled
            - jnp.mean(scaled, axis=-1, keepdims=True)
            - normed * jnp.mean(scaled * normed, axis=-1, keepdims=True)
        )

    def put_vec(k, values):
        n = values.shape[1] // W
        for j in range(W):
            grad_vec[j, :, cuts[k] : cuts[k] + n] = values[:, j * n : (j + 1) * n]

    def total_of(values):
        return jnp.sum(values, axis=0, keepdims=True)

    gain_a, gain_b = vec_of(1), vec_of(4)
    w_ready(0)
    summed = tokens[...].astype(f32) + (nn(ctx[...], full_o[...]) + vec_of(0))
    hidden, normed_1, inverse_1 = norm(summed, gain_a, vec_of(2))
    hidden_low[...] = hidden.astype(bf16)
    for name, part in dims["ffn0"]:
        stages[name](part)
    w_ready(1)
    n_ff = dims["ff_chunk"]
    spans = [slice(k * n_ff, (k + 1) * n_ff) for k in range(w_i.shape[1] // n_ff)]
    bias_in = vec_of(6)
    for span in spans:
        inner = nn(hidden_low[...], full_i[:, span]) + bias_in[:, span]
        cdf = 0.5 * (1.0 + lax.erf(inner * (0.5**0.5)))
        active[:, span] = (inner * cdf).astype(bf16)
        slope[:, span] = cdf + inner * (jnp.exp(-0.5 * inner * inner) * dims["density"])
    for name, part in dims["ffn1"]:
        stages[name](part)
    w_ready(2)
    branch = nn(active[...], full_d[...]) + vec_of(3)
    out, normed_2, inverse_2 = norm(hidden + branch, gain_b, vec_of(5))
    result[...] = out.astype(bf16)
    grad_out = cot[0].astype(f32)
    put_vec(4, total_of(grad_out * normed_2))
    put_vec(5, total_of(grad_out))
    grad_res = norm_back(grad_out, normed_2, inverse_2, gain_b)
    grad_branch[...] = grad_res.astype(bf16)
    put_vec(3, total_of(grad_branch[...].astype(f32)))
    grad_hidden = grad_res
    for k, span in enumerate(spans):
        low = (nt(grad_branch[...], full_d[span, :]) * slope[:, span]).astype(bf16)
        grad_inner[:, span] = low
        sums = total_of(low.astype(f32))
        n = b_i.shape[0]
        for j in range(W):
            lo, hi = max(j * n, span.start), min((j + 1) * n, span.stop)
            if lo < hi:
                grad_vec[j, :, cuts[6] + lo - j * n : cuts[6] + hi - j * n] = sums[:, lo - span.start : hi - span.start]
        grad_hidden = grad_hidden + nt(low, full_i[:, span])
    put_vec(1, total_of(grad_hidden * normed_1))
    put_vec(2, total_of(grad_hidden))
    grad_first = norm_back(grad_hidden, normed_1, inverse_1, gain_a)
    res[...] = grad_first
    grad_attn[...] = grad_first.astype(bf16)
    put_vec(0, total_of(grad_attn[...].astype(f32)))
    grad_ctx[...] = nt(grad_attn[...], full_o[...]).astype(bf16)

    for part in range(3):
        w_finish(part)

    @pl.when(z + 1 < W)
    def _():
        for j in range(W):
            @pl.when(j <= z)
            def _():
                tok_copy(j, 1, 0).wait_send()

    @pl.when(z > 0)
    def _():
        for j in range(W):
            @pl.when(j >= z)
            def _():
                tok_copy(j, -1, 1).wait_send()

    for q in zz:
        wz(q).wait_send()
        seg_out(q).wait_send()
        vec_out(q).wait_send()
        for kind in range(7):
            wp(q, kind).wait_send()
        cx(q).wait_send()
    for j in range(W):
        kv(j, 0).wait_send()
        kv(j, 1).wait_send()


def attend_call(dims, *operands):
    tokens, w_i = operands[0], operands[-2]
    W, heads = dims["W"], dims["heads"]
    rows, width = tokens.shape
    group = width // W
    block = rows * W
    total = 2 * block
    ff = w_i.shape[1]
    vm = pl.BlockSpec(memory_space=pltpu.VMEM)
    hb = pl.BlockSpec(memory_space=pl.ANY)
    f32, bf16 = jnp.float32, jnp.bfloat16
    dma = pltpu.SemaphoreType.DMA
    shape = jax.ShapeDtypeStruct
    return pl.pallas_call(
        partial(attend_kernel, dims),
        name="gather_attend",
        out_shape=(
            shape((W, rows, width), bf16),
            shape((width, 3 * LANES), bf16),
            shape((heads * block, LANES), bf16),
            shape((total, LANES), bf16),
            shape((total, LANES), bf16),
            shape((group, block), f32),
            shape((heads, 1, block), f32),
            shape((rows, width), bf16),
            shape((rows, width), bf16),
            shape((rows, width), f32),
            shape((rows, ff), bf16),
            shape((rows, width), bf16),
            shape((rows, width), bf16),
            shape((rows, ff), bf16),
            shape((rows, width), bf16),
            shape((W, 1, dims["n_vec"]), f32),
            shape((rows, width), bf16),
        ),
        in_specs=[vm] * 15 + [hb] * 3,
        out_specs=tuple([vm] * 17),
        scratch_shapes=[
            pltpu.VMEM((width, width), bf16),
            pltpu.VMEM((width, ff), bf16),
            pltpu.VMEM((ff, width), bf16),
            pltpu.VMEM((W, 1, dims["n_vec"]), f32),
            pltpu.VMEM((rows, ff), f32),
            pltpu.VMEM((W, 1, rows), f32),
            pltpu.VMEM((W, 8, group // 8, 3 * LANES), bf16),
            pltpu.VMEM((W, 8, group // 8, 3 * LANES), bf16),
            pltpu.VMEM((LANES, total), bf16),
            pltpu.VMEM((total, rows), f32),
            pltpu.VMEM((W, rows, group), bf16),
            pltpu.VMEM((W, rows, group), bf16),
            dma((2, W)), dma((W,)), dma((2, W)), dma((2, W)), dma((W,)), dma((W,)),
            dma((W, 8)), dma((W, 8)), dma((2, W)), dma((2, W)), dma((W,)), dma((W,)),
            dma((3, W)), dma((3, W)), dma((3, W, 4)), dma((3, W, 4)), dma((3, W)), dma((3, W)),
            dma((3,)),
        ],
        compiler_params=pltpu.CompilerParams(
            collective_id=1, has_side_effects=True, vmem_limit_bytes=VMEM_LIMIT
        ),
    )(*operands)


def back_kernel(
    dims,
    toks, wcol, qx, kx, vv, att_t, lse, grad_ctx, res, active, grad_branch, hidden, grad_inner, context, grad_attn, vec,
    g_tok, gd, gi, go, gq, g_vec, g_b,
    d_send, d_recv, kt, dk, dv, dq_t, dqkv, kv_send, kv_recv, px, rx,
    pd, pi, po, pq, cd, ci, co, cq, xd, xi, xo, xq, yd, yi, yo, yq, zd, zi, zo, zq,
    vx, vc, vs, vz, bx, bc, bs,
    da_s, da_r, kv_s, kv_r, rx_s, rx_r, core_s, core_r, x1_s, x1_r, x2_s, x2_r, za_s, za_r, ga_s, ga_r, gc_s, gc_r,
    vp_s, vp_r, bp_s, bp_r,
):
    S, W, heads = dims["S"], dims["W"], dims["heads"]
    f32, bf16 = jnp.float32, jnp.bfloat16
    rows, width = grad_ctx.shape
    group = width // W
    head_dim = group // heads
    block = rows * W
    total = 2 * block
    half_width = width // 2
    s, c, z = lax.axis_index("seq"), lax.axis_index("ctx"), lax.axis_index("wsh")
    sib = (s, 1 - c, z)
    s1, s2, s3 = s ^ 1, s ^ 2, s ^ 3
    zz = [lax.rem(z + t, W) for t in range(1, W)]
    P, CR, X1, X2, Z, G = (pd, pi, po, pq), (cd, ci, co, cq), (xd, xi, xo, xq), (yd, yi, yo, yq), (zd, zi, zo, zq), (gd, gi, go, gq)
    mine = c * S + s

    for j in range(W):
        d_send[j] = grad_ctx[:, j * group : (j + 1) * group]
    greet([sib] + [(p, c, z) for p in (s1, s2, s3)] + [(s, c, q) for q in zz])

    def da(q):
        return remote(d_send.at[q], d_recv.at[z], da_s.at[q], da_r.at[z], (s, c, q))

    def da_in(q):
        return remote(d_send.at[q], d_recv.at[q], da_s.at[q], da_r.at[q], (s, c, q))

    for q in zz:
        da(q).start()
    d_recv[z] = d_send[z]

    def vcore():
        return remote(vc.at[c], vc.at[c], vp_s.at[0], vp_r.at[0], sib)

    def vplane(k):
        return remote(vs.at[s], vs.at[s], vp_s.at[k], vp_r.at[k], (s ^ k, c, z))

    def vz_out(q, t):
        return remote(vx.at[q], vz.at[z], vp_s.at[4 + t], vp_r.at[4 + z], (s, c, q))

    def vz_in(q, t):
        return remote(vx.at[q], vz.at[q], vp_s.at[4 + t], vp_r.at[4 + q], (s, c, q))

    def vec_core():
        vc[c] = vec[...]
        vcore().start()

    def vec_plane():
        vcore().wait_recv()
        vs[s] = vc[0] + vc[1]
        for k in (1, 2, 3):
            vplane(k).start()

    def vec_z():
        for k in (1, 2, 3):
            vplane(k).wait_recv()
        vx[...] = (vs[0] + vs[1]) + (vs[2] + vs[3])
        vz[z] = vx[z]
        for t, q in enumerate(zz):
            vz_out(q, t).start()

    def vec_end():
        for t, q in enumerate(zz):
            vz_in(q, t).wait_recv()
        acc = vz[0]
        for j in range(1, W):
            acc = acc + vz[j]
        g_vec[...] = acc
        vcore().wait_send()
        for k in (1, 2, 3):
            vplane(k).wait_send()
        for t, q in enumerate(zz):
            vz_out(q, t).wait_send()

    def core_move(a):
        return remote(P[a].at[:, pl.ds((1 - c) * S, S)], CR[a], core_s.at[a], core_r.at[a], sib)

    def add_into(a, at, half, ref):
        P[a][:, at, half] = (P[a][:, at, half].astype(f32) + ref.astype(f32)).astype(bf16)

    def core_add(a):
        core_move(a).wait_recv()
        for j in range(S):
            for half in range(2):
                add_into(a, c * S + j, half, CR[a][:, j, half])

    def x1(a, half, slot):
        to = (s1, s2)[half]
        at = c * S + ((s1, s3) if half == 0 else (s2, s3))[slot]
        k = half * 2 + slot
        return remote(P[a].at[:, at, half], X1[a].at[half, slot], x1_s.at[a, k], x1_r.at[a, k], (to, c, z))

    def x1_send(a):
        for half in range(2):
            for slot in range(2):
                x1(a, half, slot).start()

    def x1_add(a):
        for half in range(2):
            for slot in (1, 0):
                x1(a, half, slot).wait_recv()
                at = c * S + (s if slot == 0 else (s2, s1)[half])
                add_into(a, at, half, X1[a][half, slot])

    def x2(a, half):
        to = (s2, s1)[half]
        return remote(P[a].at[:, c * S + to, half], X2[a].at[half], x2_s.at[a, half], x2_r.at[a, half], (to, c, z))

    def x2_send(a):
        for half in range(2):
            x2(a, half).start()

    def x2_add(a):
        for half in range(2):
            x2(a, half).wait_recv()
            add_into(a, mine, half, X2[a][half])

    def za(a, q, t):
        return remote(P[a].at[q, mine], Z[a].at[z], za_s.at[a, t], za_r.at[a, z], (s, c, q))

    def za_in(a, q, t):
        return remote(P[a].at[q, mine], Z[a].at[q], za_s.at[a, t], za_r.at[a, q], (s, c, q))

    def z_send(a):
        for t, q in enumerate(zz):
            za(a, q, t).start()
        Z[a][z] = P[a][z, mine]

    def z_add(a):
        for t, q in enumerate(zz):
            za_in(a, q, t).wait_recv()
        if a == 3:
            G[a][mine] = Z[a][...]
        else:
            acc = Z[a][0].astype(f32)
            for j in range(1, W):
                acc = acc + Z[a][j].astype(f32)
            G[a][mine] = acc.astype(bf16)

    def half_of(a, at, half):
        return G[a].at[at, :, half] if a == 3 else G[a].at[at, half]

    def ga(a, kind):
        if kind < 2:
            return remote(G[a].at[mine], G[a].at[mine], ga_s.at[a, kind], ga_r.at[a, kind], ((s1, s2)[kind], c, z))
        ref = half_of(a, c * S + (s1, s2)[kind - 2], kind - 2)
        return remote(ref, ref, ga_s.at[a, kind], ga_r.at[a, kind], ((s2, s1)[kind - 2], c, z))

    def ga_in(a, kind):
        if kind < 2:
            ref = G[a].at[c * S + (s1, s2)[kind]]
        else:
            ref = half_of(a, c * S + s3, kind - 2)
        return remote(ref, ref, ga_s.at[a, kind], ga_r.at[a, kind], (s1, c, z))

    def gc(a):
        ref = G[a].at[pl.ds(c * S, S)]
        return remote(ref, ref, gc_s.at[a], gc_r.at[a], sib)

    def gc_in(a):
        ref = G[a].at[pl.ds((1 - c) * S, S)]
        return remote(ref, ref, gc_s.at[a], gc_r.at[a], sib)

    def g_send(a):
        ga(a, 0).start()
        ga(a, 1).start()

    def g_forward(a):
        for kind in range(2):
            ga_in(a, kind).wait_recv()
            ga(a, 2 + kind).start()

    def g_core(a):
        for kind in range(2):
            ga_in(a, 2 + kind).wait_recv()
        gc(a).start()

    def g_end(a):
        gc_in(a).wait_recv()

    def drain(a):
        core_move(a).wait_send()
        for half in range(2):
            x1(a, half, 0).wait_send()
            x1(a, half, 1).wait_send()
            x2(a, half).wait_send()
        for t, q in enumerate(zz):
            za(a, q, t).wait_send()
        for kind in range(4):
            ga(a, kind).wait_send()
        gc(a).wait_send()

    stages = dict(core_add=core_add, x1_send=x1_send, x1_add=x1_add, x2_send=x2_send, x2_add=x2_add, z_send=z_send,
                  z_add=z_add, g_send=g_send, g_forward=g_forward, g_core=g_core,
                  vec_plane=lambda a: vec_plane(), vec_z=lambda a: vec_z(), vec_end=lambda a: vec_end())

    vec_core()
    eighth = pd.shape[3]
    down_rows = 8 * eighth
    for j in range(W):
        made = tn(active[:, j * down_rows : (j + 1) * down_rows], grad_branch[...]).astype(bf16)
        for e in range(8):
            for half in range(2):
                pd[j, e, half] = made[e * eighth : (e + 1) * eighth, half * half_width : (half + 1) * half_width]
    core_move(0).start()
    part = grad_inner.shape[1] // 8
    half_rows = group // 2
    for e in range(8):
        made = tn(hidden[...], grad_inner[:, e * part : (e + 1) * part]).astype(bf16)
        for j in range(W):
            for half in range(2):
                lo = j * group + half * half_rows
                pi[j, e, half] = made[lo : lo + half_rows]
    core_move(1).start()

    def store_eighths(ref, made):
        size = group // 8
        for j in range(W):
            for e in range(8):
                for half in range(2):
                    lo = j * group + e * size
                    ref[j, e, half] = made[lo : lo + size, half * half_width : (half + 1) * half_width]

    store_eighths(po, tn(context[...], grad_attn[...]).astype(bf16))
    core_move(2).start()
    kt[...] = kx[:, :group].astype(f32).T.astype(bf16)
    dk[...] = jnp.zeros_like(dk)
    dv[...] = jnp.zeros_like(dv)
    core_add(0)
    x1_send(0)
    core_add(1)
    x1_send(1)

    chunk = dims["chunk"]
    n_chunks = total // chunk
    lane = lax.broadcasted_iota(jnp.int32, (1, LANES), 1)

    def attend(step, carry):
        i = lax.div(step, heads)
        h = lax.rem(step, heads)
        b = lax.rem(z + i, W)

        @pl.when((h == 0) & (i > 0))
        def _():
            da_in(b).wait_recv()

        at = pl.ds(pl.multiple_of(b * rows, rows), rows)
        here = pl.ds(pl.multiple_of(h * head_dim, head_dim), head_dim)
        got = d_recv[b].astype(f32)
        got = jnp.concatenate([got, jnp.zeros((rows, LANES - group), f32)], axis=1)
        mask = (lane >= h * head_dim) & (lane < (h + 1) * head_dim)
        grad = jnp.where(mask, got, 0.0)
        delta = jnp.sum(grad.T[:group] * att_t[:, at], axis=0, keepdims=True)
        grad = grad.astype(bf16)
        query = qx[pl.ds(pl.multiple_of(h * block + b * rows, rows), rows), :]
        log_mass = lse[h, :, at]
        acc = None
        for n in range(n_chunks):
            span = slice(n * chunk, (n + 1) * chunk)
            weights = jnp.exp(nt(kx[span, :], query) - log_mass)
            grad_weights = nt(vv[span, :], grad)
            grad_scores = (weights * (grad_weights - delta)).astype(bf16)
            dv[span, :] += nn(weights.astype(bf16), grad)
            dk[span, :] += nn(grad_scores, query)
            add = nn(kt[here, span], grad_scores)
            acc = add if acc is None else acc + add
        dq_t[here, at] = acc * dims["scale"]

        for when, name, a in dims["back_moves"]:
            @pl.when(step == when)
            def _():
                stages[name](a)

        return carry

    lax.fori_loop(0, W * heads, attend, 0)

    def kv_move():
        return remote(kv_send, kv_recv, kv_s.at[0], kv_r.at[0], sib)

    other = pl.ds(pl.multiple_of((1 - c) * block, block), block)
    own = pl.ds(pl.multiple_of(c * block, block), block)
    kv_send[0] = dk[other, :].astype(bf16)
    kv_send[1] = dv[other, :].astype(bf16)
    kv_move().start()
    pad = jnp.zeros((block, LANES - group), bf16)
    dqkv[:, :LANES] = jnp.concatenate([dq_t[...].T.astype(bf16), pad], axis=1)
    kv_move().wait_recv()
    keep = lane < group
    for m, ref in ((0, dk), (1, dv)):
        whole = ref[own, :] + kv_recv[m].astype(f32)
        dqkv[:, (m + 1) * LANES : (m + 2) * LANES] = jnp.where(keep, whole, 0.0).astype(bf16)

    def rx_out(d, step, lane_):
        return remote(px.at[d], rx.at[lane_, d], rx_s.at[d], rx_r.at[lane_, d], (s, c, z + step))

    def make(d):
        at = pl.ds(pl.multiple_of(d * rows, rows), rows)
        return nt(dqkv[at, :], wcol[...])

    def line(k, carry):
        far = W - 1 - lax.div(k, 2)
        right = lax.rem(k, 2) == 0
        d = jnp.where(right, far, W - 1 - far)

        @pl.when(right & (d > z))
        def _():
            px[d] = make(d).astype(bf16)

            @pl.when(z > 0)
            def _():
                rx_out(d, 1, 0).wait_recv()
                px[d] = (px[d].astype(f32) + rx[0, d].astype(f32)).astype(bf16)

            rx_out(d, 1, 0).start()

        @pl.when(jnp.logical_not(right) & (d < z))
        def _():
            px[d] = make(d).astype(bf16)

            @pl.when(z < W - 1)
            def _():
                rx_out(d, -1, 1).wait_recv()
                px[d] = (px[d].astype(f32) + rx[1, d].astype(f32)).astype(bf16)

            rx_out(d, -1, 1).start()

        return carry

    lax.fori_loop(0, 2 * (W - 1), line, 0)
    made = None
    for j in range(W):
        add = tn(toks[j], dqkv[j * rows : (j + 1) * rows, :])
        made = add if made is None else made + add
    store_eighths(pq, made.astype(bf16))
    core_move(3).start()
    ones = jnp.ones((8, block), bf16)
    sums = nn(ones, dqkv[...])[0:1]
    bc[c] = jnp.concatenate([sums[:, :LANES], sums[:, 2 * LANES :]], axis=1)

    def bcore():
        return remote(bc.at[c], bc.at[c], bp_s.at[0], bp_r.at[0], sib)

    def bplane(k):
        return remote(bs.at[s], bs.at[s], bp_s.at[k], bp_r.at[k], (s ^ k, c, z))

    bcore().start()
    g_tok[...] = make(z) + res[...]
    for name, a in dims["back_late"]:
        stages[name](a)
    bcore().wait_recv()
    bs[s] = bc[0] + bc[1]
    for k in (1, 2, 3):
        bplane(k).start()
    for name, a in dims["back_last"]:
        stages[name](a)

    @pl.when(z > 0)
    def _():
        rx_out(z, 1, 0).wait_recv()
        g_tok[...] += rx[0, z].astype(f32)

    @pl.when(z < W - 1)
    def _():
        rx_out(z, -1, 1).wait_recv()
        g_tok[...] += rx[1, z].astype(f32)

    for k in (1, 2, 3):
        bplane(k).wait_recv()
    tot = (bs[0] + bs[1]) + (bs[2] + bs[3])
    g_b[...] = tot
    bcore().wait_send()
    for k in (1, 2, 3):
        bplane(k).wait_send()
    kv_move().wait_send()
    for q in zz:
        da(q).wait_send()
    for j in range(W):
        @pl.when(j > z)
        def _():
            rx_out(j, 1, 0).wait_send()

        @pl.when(j < z)
        def _():
            rx_out(j, -1, 1).wait_send()

    for a in range(4):
        g_end(a)
    for a in range(4):
        drain(a)


def back_call(dims, *operands):
    toks, wcol, qx, kx, vv, att_t, lse, grad_ctx, res, active, grad_branch, hidden, grad_inner, context, grad_attn, vec = operands
    S, W, heads = dims["S"], dims["W"], dims["heads"]
    rows, width = grad_ctx.shape
    ff = active.shape[1]
    group = width // W
    block = rows * W
    total = 2 * block
    f32, bf16 = jnp.float32, jnp.bfloat16
    vm = pl.BlockSpec(memory_space=pltpu.VMEM)
    dma = pltpu.SemaphoreType.DMA
    shape = jax.ShapeDtypeStruct
    half = width // 2
    sizes = (ff // W // 8, group // 2, group // 8, group // 8)
    assert ff // 8 == half
    n_vec = vec.shape[2]
    pieces = [pltpu.VMEM((W, 8, 2, r, half), bf16) for r in sizes]
    cores = [pltpu.VMEM((W, S, 2, r, half), bf16) for r in sizes]
    x1s = [pltpu.VMEM((2, 2, W, r, half), bf16) for r in sizes]
    x2s = [pltpu.VMEM((2, W, r, half), bf16) for r in sizes]
    zs = [pltpu.VMEM((W, 2, r, half), bf16) for r in sizes]
    return pl.pallas_call(
        partial(back_kernel, dims),
        name="attend_back_sum",
        out_shape=(
            shape((rows, width), f32),
            *[shape((8, 2, r, half), bf16) for r in sizes[:3]],
            shape((8, W, 2, sizes[3], half), bf16),
            shape((1, n_vec), f32),
            shape((1, 2 * LANES), f32),
        ),
        in_specs=[vm] * 16,
        out_specs=tuple([vm] * 7),
        scratch_shapes=[
            pltpu.VMEM((W, rows, group), bf16),
            pltpu.VMEM((W, rows, group), bf16),
            pltpu.VMEM((group, total), bf16),
            pltpu.VMEM((total, LANES), f32),
            pltpu.VMEM((total, LANES), f32),
            pltpu.VMEM((group, block), f32),
            pltpu.VMEM((block, 3 * LANES), bf16),
            pltpu.VMEM((2, block, LANES), bf16),
            pltpu.VMEM((2, block, LANES), bf16),
            pltpu.VMEM((W, rows, width), bf16),
            pltpu.VMEM((2, W, rows, width), bf16),
            *pieces, *cores, *x1s, *x2s, *zs,
            pltpu.VMEM((W, 1, n_vec), f32),
            pltpu.VMEM((2, W, 1, n_vec), f32),
            pltpu.VMEM((S, W, 1, n_vec), f32),
            pltpu.VMEM((W, 1, n_vec), f32),
            pltpu.VMEM((1, 2 * LANES), f32),
            pltpu.VMEM((2, 1, 2 * LANES), f32),
            pltpu.VMEM((S, 1, 2 * LANES), f32),
            dma((W,)), dma((W,)), dma((1,)), dma((1,)), dma((W,)), dma((2, W)),
            dma((4,)), dma((4,)), dma((4, 4)), dma((4, 4)), dma((4, 2)), dma((4, 2)),
            dma((4, W)), dma((4, W)), dma((4, 4)), dma((4, 4)), dma((4,)), dma((4,)),
            dma((4 + W,)), dma((4 + W,)), dma((4,)), dma((4,)),
        ],
        compiler_params=pltpu.CompilerParams(
            collective_id=2, has_side_effects=True, vmem_limit_bytes=VMEM_LIMIT
        ),
    )(*operands)


def finish_kernel(dims, result, g_tok, gd, gi, go, gq, vec, g_b,
                  o_res, o_tok, o_q, o_bq, o_k, o_v, o_bv, o_o, o_s0, o_s1, o_s2, o_i, o_s3, o_d, o_s4, o_s5, o_s6):
    f32 = jnp.float32
    W = dims["W"]
    group = o_q.shape[0]
    eighth, half_width = gd.shape[2:]
    half_rows = gi.shape[2]
    o_res[0] = result[...].astype(jnp.bfloat16)
    o_tok[0] = g_tok[...].astype(jnp.bfloat16)
    for e in range(8):
        for half in range(2):
            lanes = slice(half * half_width, (half + 1) * half_width)
            o_d[e * eighth : (e + 1) * eighth, lanes] = gd[e, half].astype(f32)
            o_i[half * half_rows : (half + 1) * half_rows, e * half_width : (e + 1) * half_width] = gi[e, half].astype(f32)
            size = group // 8
            o_o[e * size : (e + 1) * size, lanes] = go[e, half].astype(f32)
    size = group // 8
    for e in range(8):
        for j in range(W):
            both = jnp.concatenate([gq[e, j, 0].astype(f32), gq[e, j, 1].astype(f32)], axis=1)
            for m, ref in enumerate((o_q, o_k, o_v)):
                ref[e * size : (e + 1) * size, j * group : (j + 1) * group] = both[:, m * LANES : m * LANES + group]
    o_bq[...] = g_b[0, :group]
    o_bv[...] = g_b[0, LANES : LANES + group]
    for ref, lo in zip((o_s0, o_s1, o_s2, o_s4, o_s5, o_s6, o_s3), dims["cuts"]):
        ref[...] = vec[0, lo : lo + ref.shape[0]]


def finish_call(dims, result, g_tok, gd, gi, go, gq, vec, g_b):
    f32, bf16 = jnp.float32, jnp.bfloat16
    W = dims["W"]
    rows, width = result.shape
    group = width // W
    ff = width * W
    vm = pl.BlockSpec(memory_space=pltpu.VMEM)
    shape = jax.ShapeDtypeStruct
    small, mat = shape((group,), f32), shape((group, width), f32)
    return pl.pallas_call(
        partial(finish_kernel, dims),
        name="finish",
        out_shape=(shape((1, rows, width), bf16), shape((1, rows, width), bf16), mat, small, mat, mat, small, mat,
                   small, small, small, shape((group, ff), f32), shape((ff // W,), f32), shape((ff // W, width), f32),
                   small, small, small),
        in_specs=[vm] * 8,
        out_specs=tuple([vm] * 17),
        compiler_params=pltpu.CompilerParams(vmem_limit_bytes=VMEM_LIMIT),
    )(result, g_tok, gd, gi, go, gq, vec, g_b)


def fast_device(dims, tokens, segment_ids, w_query, b_query, w_key, w_value, b_value, w_out, b_out, gain_attn,
                shift_attn, w_in, b_in, w_down, b_down, gain_ffn, shift_ffn, cotangent):
    got = attend_call(dims, tokens[0], segment_ids, w_query, w_key, w_value, b_query, b_value, b_out, gain_attn, shift_attn,
                      b_in, b_down, gain_ffn, shift_ffn, cotangent, w_out, w_in, w_down)
    (toks, wcol, qx, kx, vv, att_t, lse, context, grad_ctx, res, active, grad_branch, hidden, grad_inner, grad_attn,
     grad_vec, result) = got
    back = back_call(dims, toks, wcol, qx, kx, vv, att_t, lse, grad_ctx, res, active, grad_branch, hidden, grad_inner,
                     context, grad_attn, grad_vec)
    return finish_call(dims, result, *back)


def plan(mesh):
    return dict(
        S=mesh.shape["seq"], W=mesh.shape["wsh"], heads=HEADS // mesh.shape["wsh"], scale=0.125, chunk=512,
        cuts=(0, 256, 512, 768, 1024, 1280, 1536), n_vec=2304, ff_chunk=768, density=1.0 / math.sqrt(2.0 * math.pi),
        starts=[(0, 1), (1, 2)],
        mid=[("start", 2), ("plane", 0), ("plane", 1)],
        moves=[(2, "cross", 0), (4, "core", 0), (6, "cross", 1), (8, "plane", 2), (9, "core", 1)],
        late=[], ffn0=[], ffn1=[("cross", 2), ("core", 2)],
        back_moves=[(0, "vec_plane", 0), (1, "core_add", 2), (1, "x1_send", 2), (3, "vec_z", 0), (4, "x1_add", 0), (4, "x2_send", 0),
                    (7, "x2_add", 0), (7, "z_send", 0), (9, "x1_add", 1), (9, "x2_send", 1), (11, "vec_end", 0)],
        back_late=[("z_add", 0), ("g_send", 0), ("x2_add", 1), ("z_send", 1), ("x1_add", 2), ("x2_send", 2),
                   ("core_add", 3), ("x1_send", 3), ("x2_add", 2), ("z_send", 2), ("g_forward", 0), ("x1_add", 3), ("x2_send", 3),
                   ("z_add", 1), ("g_send", 1)],
        back_last=[("x2_add", 3), ("z_send", 3), ("g_core", 0), ("z_add", 2), ("g_send", 2), ("g_forward", 1),
                   ("z_add", 3), ("g_send", 3), ("g_core", 1), ("g_forward", 2), ("g_forward", 3), ("g_core", 2), ("g_core", 3)],
    )


def solution(mesh):
    fast = mesh.shape["seq"] == 4 and mesh.shape["ctx"] == 2 and HEADS % mesh.shape["wsh"] == 0
    return jax.shard_map(
        partial(fast_device, plan(mesh)) if fast else per_device,
        mesh=mesh,
        in_specs=(
            P("seq", ("ctx", "wsh"), None),
            P("seq", ("ctx", "wsh")),
            P("wsh", None),
            P("wsh"),
            P("wsh", None),
            P("wsh", None),
            P("wsh"),
            P("wsh", None),
            P("wsh"),
            P("wsh"),
            P("wsh"),
            P("wsh", None),
            P("wsh"),
            P("wsh", None),
            P("wsh"),
            P("wsh"),
            P("wsh"),
            P("seq", ("ctx", "wsh"), None),
        ),
        out_specs=(
            P("seq", ("ctx", "wsh"), None),
            P("seq", ("ctx", "wsh"), None),
            P("wsh", None),
            P("wsh"),
            P("wsh", None),
            P("wsh", None),
            P("wsh"),
            P("wsh", None),
            P("wsh"),
            P("wsh"),
            P("wsh"),
            P("wsh", None),
            P("wsh"),
            P("wsh", None),
            P("wsh"),
            P("wsh"),
            P("wsh"),
        ),
        check_vma=False,
    )
```

```python
from functools import partial
import math

import jax
import jax.numpy as jnp
from jax import lax
from jax.experimental import pallas as pl
from jax.experimental.pallas import tpu as pltpu
from jax.sharding import PartitionSpec as P

HEADS = 12


norm_eps = 1e-12
masked_fill = -1e30


def matmul(left, right):
    return jnp.dot(left, right, preferred_element_type=jnp.float32)


def matmul_left_t(left, right):
    return lax.dot_general(
        left, right, (((0,), (0,)), ((), ())), preferred_element_type=jnp.float32
    )


def matmul_right_t(left, right):
    return lax.dot_general(
        left, right, (((1,), (1,)), ((), ())), preferred_element_type=jnp.float32
    )


def normalize(values, gain, shift):
    centre = jnp.mean(values, axis=-1, keepdims=True)
    centred = values - centre
    inverse = lax.rsqrt(jnp.mean(centred * centred, axis=-1, keepdims=True) + norm_eps)
    normed = centred * inverse
    return (normed * gain + shift, normed, inverse)


def normalize_back(grad_out, normed, inverse, gain):
    grad_gain = jnp.sum(grad_out * normed, axis=0)
    grad_shift = jnp.sum(grad_out, axis=0)
    scaled = grad_out * gain
    grad_in = inverse * (
        scaled
        - jnp.mean(scaled, axis=-1, keepdims=True)
        - normed * jnp.mean(scaled * normed, axis=-1, keepdims=True)
    )
    return (grad_in, grad_gain, grad_shift)


def block_scores(query_blk, key_blk, seg_query, seg_key, score_scale):
    scores = (
        jnp.einsum("qhd,khd->hqk", query_blk, key_blk, preferred_element_type=jnp.float32)
        * score_scale
    )
    same_doc = seg_query[:, None] == seg_key[None, :]
    return (jnp.where(same_doc[None], scores, masked_fill), same_doc)


def block_grads(
    query_blk, dctx_blk, lse_blk, delta_blk, seg_query, key_blk, value_blk, seg_key, score_scale
):
    scores, same_doc = block_scores(query_blk, key_blk, seg_query, seg_key, score_scale)
    weights = jnp.where(same_doc[None], jnp.exp(scores - lse_blk.T[:, :, None]), 0.0)
    grad_weights = jnp.einsum(
        "qhd,khd->hqk", dctx_blk, value_blk, preferred_element_type=jnp.float32
    )
    grad_scores = (weights * (grad_weights - delta_blk.T[:, :, None])).astype(jnp.bfloat16)
    grad_query = None
    grad_key = None
    grad_value = None
    grad_query = (
        jnp.einsum("hqk,khd->qhd", grad_scores, key_blk, preferred_element_type=jnp.float32)
        * score_scale
    )
    grad_key = (
        jnp.einsum("hqk,qhd->khd", grad_scores, query_blk, preferred_element_type=jnp.float32)
        * score_scale
    )
    grad_value = jnp.einsum(
        "hqk,qhd->khd", weights.astype(jnp.bfloat16), dctx_blk, preferred_element_type=jnp.float32
    )
    return (grad_query, grad_key, grad_value)


def per_device(
    tokens,
    segment_ids,
    w_query,
    b_query,
    w_key,
    w_value,
    b_value,
    w_out,
    b_out,
    gain_attn,
    shift_attn,
    w_in,
    b_in,
    w_down,
    b_down,
    gain_ffn,
    shift_ffn,
    cotangent,
):
    (
        full_query,
        bias_query,
        full_key,
        full_value,
        bias_value,
        full_out,
        bias_out,
        gain_one,
        shift_one,
        full_in,
        bias_in,
        full_down,
        bias_down,
        gain_two,
        shift_two,
    ) = (
        lax.all_gather(w_query, "wsh", axis=0, tiled=True),
        lax.all_gather(b_query, "wsh", axis=0, tiled=True),
        lax.all_gather(w_key, "wsh", axis=0, tiled=True),
        lax.all_gather(w_value, "wsh", axis=0, tiled=True),
        lax.all_gather(b_value, "wsh", axis=0, tiled=True),
        lax.all_gather(w_out, "wsh", axis=0, tiled=True),
        lax.all_gather(b_out, "wsh", axis=0, tiled=True),
        lax.all_gather(gain_attn, "wsh", axis=0, tiled=True),
        lax.all_gather(shift_attn, "wsh", axis=0, tiled=True),
        lax.all_gather(w_in, "wsh", axis=0, tiled=True),
        lax.all_gather(b_in, "wsh", axis=0, tiled=True),
        lax.all_gather(w_down, "wsh", axis=0, tiled=True),
        lax.all_gather(b_down, "wsh", axis=0, tiled=True),
        lax.all_gather(gain_ffn, "wsh", axis=0, tiled=True),
        lax.all_gather(shift_ffn, "wsh", axis=0, tiled=True),
    )
    inputs = tokens[0]
    rows = inputs.shape[0]
    width = inputs.shape[1]
    head_dim = width // HEADS
    score_scale = 1.0 / math.sqrt(head_dim)
    seg_float = segment_ids[0].astype(jnp.bfloat16)
    queries = (matmul(inputs, full_query) + bias_query.astype(jnp.float32)).astype(jnp.bfloat16)
    key_rows = matmul(inputs, full_key).astype(jnp.bfloat16)
    values = (matmul(inputs, full_value) + bias_value.astype(jnp.float32)).astype(jnp.bfloat16)
    keys_all, values_all, segs_all = (
        lax.all_gather(key_rows, ("ctx", "wsh"), axis=0, tiled=True),
        lax.all_gather(values, ("ctx", "wsh"), axis=0, tiled=True),
        lax.all_gather(seg_float, ("ctx", "wsh"), axis=0, tiled=True),
    )
    total = keys_all.shape[0]
    key_block = min(512, total)
    block_count = total // key_block
    key_blocks = keys_all.reshape(block_count, key_block, HEADS, head_dim)
    value_blocks = values_all.reshape(block_count, key_block, HEADS, head_dim)
    seg_blocks = segs_all.reshape(block_count, key_block)
    query_heads = queries.reshape(rows, HEADS, head_dim)

    def forward_block(carry, block):
        run_max, run_sum, accum = carry
        key_blk, value_blk, seg_blk = block
        scores, same_doc = block_scores(query_heads, key_blk, seg_float, seg_blk, score_scale)
        new_max = jnp.maximum(run_max, jnp.max(scores, axis=2))
        raised = jnp.where(same_doc[None], jnp.exp(scores - new_max[:, :, None]), 0.0)
        factor = jnp.exp(run_max - new_max)
        run_sum = run_sum * factor + jnp.sum(raised, axis=2)
        accum = accum * factor.T[:, :, None] + jnp.einsum(
            "hqk,khd->qhd",
            raised.astype(jnp.bfloat16),
            value_blk,
            preferred_element_type=jnp.float32,
        )
        return ((new_max, run_sum, accum), None)

    start_state = (
        jnp.full((HEADS, rows), masked_fill, jnp.float32),
        jnp.zeros((HEADS, rows), jnp.float32),
        jnp.zeros((rows, HEADS, head_dim), jnp.float32),
    )
    (run_max, run_sum, accum), unused = lax.scan(
        forward_block, start_state, (key_blocks, value_blocks, seg_blocks)
    )
    attended = accum / run_sum.T[:, :, None]
    lse_rows = (run_max + jnp.log(run_sum)).T
    context = attended.reshape(rows, width).astype(jnp.bfloat16)
    attn_out = matmul(context, full_out) + bias_out.astype(jnp.float32)
    gain_first = gain_one.astype(jnp.float32)
    gain_second = gain_two.astype(jnp.float32)
    hidden, normed_one, inverse_one = normalize(
        inputs.astype(jnp.float32) + attn_out, gain_first, shift_one.astype(jnp.float32)
    )
    hidden_low = hidden.astype(jnp.bfloat16)
    inner = matmul(hidden_low, full_in) + bias_in.astype(jnp.float32)
    active_float, gelu_pull = jax.vjp(partial(jax.nn.gelu, approximate=False), inner)
    active = active_float.astype(jnp.bfloat16)
    branch = matmul(active, full_down) + bias_down.astype(jnp.float32)
    result, normed_two, inverse_two = normalize(
        hidden + branch, gain_second, shift_two.astype(jnp.float32)
    )
    grad_out = cotangent[0].astype(jnp.float32)
    grad_res_two, grad_gain_two, grad_shift_two = normalize_back(
        grad_out, normed_two, inverse_two, gain_second
    )
    grad_branch = grad_res_two.astype(jnp.bfloat16)
    grad_bias_down = jnp.sum(grad_branch.astype(jnp.float32), axis=0)
    grad_full_down = matmul_left_t(active, grad_branch)
    grad_inner = gelu_pull(matmul_right_t(grad_branch, full_down))[0].astype(jnp.bfloat16)
    grad_bias_in = jnp.sum(grad_inner.astype(jnp.float32), axis=0)
    grad_full_in = matmul_left_t(hidden_low, grad_inner)
    grad_hidden = grad_res_two + matmul_right_t(grad_inner, full_in)
    grad_res_one, grad_gain_one, grad_shift_one = normalize_back(
        grad_hidden, normed_one, inverse_one, gain_first
    )
    grad_attn = grad_res_one.astype(jnp.bfloat16)
    grad_bias_out = jnp.sum(grad_attn.astype(jnp.float32), axis=0)
    grad_full_out = matmul_left_t(context, grad_attn)
    grad_context = matmul_right_t(grad_attn, full_out).astype(jnp.bfloat16)
    dctx_heads = grad_context.reshape(rows, HEADS, head_dim)
    delta_rows = jnp.sum(dctx_heads.astype(jnp.float32) * attended, axis=2)
    zero_heads = jnp.zeros((rows, HEADS, head_dim), jnp.float32)

    def back_block(grad_acc, block):
        key_blk, value_blk, seg_blk = block
        part_query, part_key, part_value = block_grads(
            query_heads,
            dctx_heads,
            lse_rows,
            delta_rows,
            seg_float,
            key_blk,
            value_blk,
            seg_blk,
            score_scale,
        )
        return (grad_acc + part_query, (part_key, part_value))

    grad_q, (key_parts, value_parts) = lax.scan(
        back_block, zero_heads, (key_blocks, value_blocks, seg_blocks)
    )
    grad_key_own, grad_value_own = (
        lax.psum_scatter(
            key_parts.reshape(total, width), ("ctx", "wsh"), scatter_dimension=0, tiled=True
        ),
        lax.psum_scatter(
            value_parts.reshape(total, width), ("ctx", "wsh"), scatter_dimension=0, tiled=True
        ),
    )
    grad_queries = grad_q.reshape(rows, width).astype(jnp.bfloat16)
    grad_keys = grad_key_own.astype(jnp.bfloat16)
    grad_values = grad_value_own.astype(jnp.bfloat16)
    grad_full_query = matmul_left_t(inputs, grad_queries)
    grad_bias_query = jnp.sum(grad_queries.astype(jnp.float32), axis=0)
    grad_full_key = matmul_left_t(inputs, grad_keys)
    grad_full_value = matmul_left_t(inputs, grad_values)
    grad_bias_value = jnp.sum(grad_values.astype(jnp.float32), axis=0)
    grad_input = (
        grad_res_one
        + matmul_right_t(grad_queries, full_query)
        + matmul_right_t(grad_keys, full_key)
        + matmul_right_t(grad_values, full_value)
    )
    (
        share_query,
        share_bias_query,
        share_key,
        share_value,
        share_bias_value,
        share_out,
        share_bias_out,
        share_gain_one,
        share_shift_one,
        share_in,
        share_bias_in,
        share_down,
        share_bias_down,
        share_gain_two,
        share_shift_two,
    ) = (
        lax.psum_scatter(
            grad_full_query.astype(jnp.bfloat16), "wsh", scatter_dimension=0, tiled=True
        ).astype(jnp.float32),
        lax.psum_scatter(
            grad_bias_query.astype(jnp.bfloat16), "wsh", scatter_dimension=0, tiled=True
        ).astype(jnp.float32),
        lax.psum_scatter(
            grad_full_key.astype(jnp.bfloat16), "wsh", scatter_dimension=0, tiled=True
        ).astype(jnp.float32),
        lax.psum_scatter(
            grad_full_value.astype(jnp.bfloat16), "wsh", scatter_dimension=0, tiled=True
        ).astype(jnp.float32),
        lax.psum_scatter(
            grad_bias_value.astype(jnp.bfloat16), "wsh", scatter_dimension=0, tiled=True
        ).astype(jnp.float32),
        lax.psum_scatter(
            grad_full_out.astype(jnp.bfloat16), "wsh", scatter_dimension=0, tiled=True
        ).astype(jnp.float32),
        lax.psum_scatter(
            grad_bias_out.astype(jnp.bfloat16), "wsh", scatter_dimension=0, tiled=True
        ).astype(jnp.float32),
        lax.psum_scatter(
            grad_gain_one.astype(jnp.bfloat16), "wsh", scatter_dimension=0, tiled=True
        ).astype(jnp.float32),
        lax.psum_scatter(
            grad_shift_one.astype(jnp.bfloat16), "wsh", scatter_dimension=0, tiled=True
        ).astype(jnp.float32),
        lax.psum_scatter(
            grad_full_in.astype(jnp.bfloat16), "wsh", scatter_dimension=0, tiled=True
        ).astype(jnp.float32),
        lax.psum_scatter(
            grad_bias_in.astype(jnp.bfloat16), "wsh", scatter_dimension=0, tiled=True
        ).astype(jnp.float32),
        lax.psum_scatter(
            grad_full_down.astype(jnp.bfloat16), "wsh", scatter_dimension=0, tiled=True
        ).astype(jnp.float32),
        lax.psum_scatter(
            grad_bias_down.astype(jnp.bfloat16), "wsh", scatter_dimension=0, tiled=True
        ).astype(jnp.float32),
        lax.psum_scatter(
            grad_gain_two.astype(jnp.bfloat16), "wsh", scatter_dimension=0, tiled=True
        ).astype(jnp.float32),
        lax.psum_scatter(
            grad_shift_two.astype(jnp.bfloat16), "wsh", scatter_dimension=0, tiled=True
        ).astype(jnp.float32),
    )
    summed = lax.psum(
        (
            share_query,
            share_bias_query,
            share_key,
            share_value,
            share_bias_value,
            share_out,
            share_bias_out,
            share_gain_one,
            share_shift_one,
            share_in,
            share_bias_in,
            share_down,
            share_bias_down,
            share_gain_two,
            share_shift_two,
        ),
        ("seq", "ctx"),
    )
    return (
        result.astype(jnp.bfloat16)[None],
        grad_input.astype(jnp.bfloat16)[None],
        summed[0],
        summed[1],
        summed[2],
        summed[3],
        summed[4],
        summed[5],
        summed[6],
        summed[7],
        summed[8],
        summed[9],
        summed[10],
        summed[11],
        summed[12],
        summed[13],
        summed[14],
    )


MESH_ID = pl.DeviceIdType.MESH
LANES = 256
IDS = 16
BIG = float(2.0**99)
VMEM_LIMIT = 60 * 2**20


def remote(src, dst, send, recv, where):
    return pltpu.make_async_remote_copy(
        src_ref=src, dst_ref=dst, send_sem=send, recv_sem=recv, device_id=where, device_id_type=MESH_ID
    )


def nt(left, right):
    return lax.dot_general(left, right, (((1,), (1,)), ((), ())), preferred_element_type=jnp.float32)


def tn(left, right):
    return lax.dot_general(left, right, (((0,), (0,)), ((), ())), preferred_element_type=jnp.float32)


def nn(left, right):
    return jnp.dot(left, right, preferred_element_type=jnp.float32)


def greet(peers):
    barrier = pltpu.get_barrier_semaphore()
    for peer in peers:
        pl.semaphore_signal(barrier, inc=1, device_id=peer, device_id_type=MESH_ID)
    pl.semaphore_wait(barrier, len(peers))


def layer_kernel(
    dims,
    tokens, seg, w_q, w_k, w_v, b_q, b_v, b_o, gain_1, shift_1, b_i, b_d, gain_2, shift_2, cot, w_o, w_i, w_d,
    result, g_tok, gd, gi, go, gq, g_vec, g_b,
    toks, wcol, qx, kx, vv, att_t, lse, ctx, res, active, grad_branch, hidden_low, grad_inner, grad_attn, grad_vec,
    full_o, full_i, full_d, vecs, slope, segs, w_send, vt, scores, dv, ctx_send, ctx_recv, d_recv, dqkv, kv_recv, rx,
    cd, ci, co, cq, xd, xi, xo, xq, yd, yi, yo, yq, zd, zi, zo, zq, vx, vc, vs, vz, bc, bs,
    tok_s, tok_r, sv_s, sv_r, wz_s, wz_r, wp_s, wp_r, kv_s, kv_r, cx_s, cx_r,
    fz_s, fz_r, fx_s, fx_r, fc_s, fc_r, loc,
    da_s, da_r, kb_s, kb_r, rx_s, rx_r, core_s, core_r, x1_s, x1_r, x2_s, x2_r, za_s, za_r, ga_s, ga_r, gc_s, gc_r,
    vp_s, vp_r, bp_s, bp_r,
):
    S, W, heads = dims["S"], dims["W"], dims["heads"]
    rows, width = tokens.shape
    f32, bf16 = jnp.float32, jnp.bfloat16
    group = width // W
    head_dim = group // heads
    block = rows * W
    total = 2 * block
    ff = w_i.shape[1]
    P, CR, X1, X2, Z, G = (full_d, full_i, full_o, w_send), (cd, ci, co, cq), (xd, xi, xo, xq), (yd, yi, yo, yq), (zd, zi, zo, zq), (gd, gi, go, gq)
    kt, dk, kv_send, px, dq_t = vt, scores, kx, active, att_t

    def run(name):
        for stage, part in dims[name]:
            stages[stage](part)

    s, c, z = lax.axis_index("seq"), lax.axis_index("ctx"), lax.axis_index("wsh")
    sib = (s, 1 - c, z)
    s1, s2, s3 = s ^ 1, s ^ 2, s ^ 3
    shifts = list(range(1, W))
    zz = [lax.rem(z + t, W) for t in shifts]
    barrier = pltpu.get_barrier_semaphore()
    peers = [sib] + [(p, c, z) for p in (s1, s2, s3)] + [(s, c, q) for q in zz]
    for peer in peers:
        pl.semaphore_signal(barrier, inc=1, device_id=peer, device_id_type=MESH_ID)
    toks[z] = tokens[...]
    segs[z] = seg[...].astype(jnp.float32)
    for ref, lo in zip((b_o, gain_1, shift_1, b_d, gain_2, shift_2, b_i), dims["cuts"]):
        vecs[z, :, lo : lo + ref.shape[0]] = ref[...].astype(jnp.float32).reshape(1, -1)

    for j in range(W):
        for m, ref in enumerate((w_q, w_k, w_v)):
            part = ref[:, j * group : (j + 1) * group]
            part = jnp.concatenate([part, jnp.zeros((group, LANES - group), part.dtype)], axis=1)
            w_send[j, :, m * LANES : (m + 1) * LANES] = part

    pl.semaphore_wait(barrier, len(peers))

    slab, wide = group // S, 3 * LANES // 2

    def col_at(ref, base, cc, ss):
        rows_at = pl.ds(pl.multiple_of(base + (0 if ss is None else ss * slab), 16), group if ss is None else slab)
        return ref.at[rows_at, pl.ds(pl.multiple_of(cc * wide, 128), wide)]

    def wz(q):
        return remote(col_at(w_send.at[q], 0, c, s), col_at(wcol, z * group, c, s), wz_s.at[q], wz_r.at[z], (s, c, q))

    def wz_in(q):
        here = col_at(wcol, q * group, c, s)
        return remote(here, here, wz_s.at[q], wz_r.at[q], (s, c, q))

    def wp(q, k):
        ref = col_at(wcol, q * group, c, s if k else None)
        return remote(ref, ref, wp_s.at[q, k], wp_r.at[q, k], (s ^ k, c, z) if k else sib)

    def wp_in(q, k):
        ref = col_at(wcol, q * group, c, s ^ k) if k else col_at(wcol, q * group, 1 - c, None)
        return remote(ref, ref, wp_s.at[q, k], wp_r.at[q, k], sib)

    def seg_out(q):
        return remote(segs.at[z], segs.at[z], sv_s.at[0, q], sv_r.at[0, z], (s, c, q))

    def seg_in(q):
        return remote(segs.at[q], segs.at[q], sv_s.at[0, q], sv_r.at[0, q], (s, c, q))

    def vec_out(q):
        return remote(vecs.at[z], vecs.at[z], sv_s.at[1, q], sv_r.at[1, z], (s, c, q))

    def vec_in(q):
        return remote(vecs.at[q], vecs.at[q], sv_s.at[1, q], sv_r.at[1, q], (s, c, q))

    def tok_copy(slot, step, lane):
        return remote(toks.at[slot], toks.at[slot], tok_s.at[lane, slot], tok_r.at[slot], (s, c, z + step))

    parts = ((w_o, full_o), (w_i, full_i), (w_d, full_d))

    def place(kind, cc, ss, half=None):
        n, m = ((group, width), (group, ff), (ff // W, width))[kind]
        if kind == 0:
            row, size, col, wide = (0, n) if ss is None else (ss * (n // S), n // S), None, cc * (m // 2), m // 2
            row, size = row
            if half is not None:
                col, wide = col + (0 if half == 0 else 128), (128 if half == 0 else m // 2 - 128)
        elif kind == 1:
            row, size = 0, n
            col, wide = cc * (m // 2) + (0 if ss is None else ss * (m // 8)), m // 2 if ss is None else m // 8
            if half is not None:
                row, size = half * (n // 2), n // 2
        else:
            row, size = cc * (n // 2) + (0 if ss is None else ss * (n // 8)), n // 2 if ss is None else n // 8
            col, wide = 0, m
            if half is not None:
                col, wide = half * (m // 2), m // 2
        if not isinstance(row, int):
            row = pl.multiple_of(row, 16)
        if not isinstance(col, int):
            col = pl.multiple_of(col, 128)
        return pl.ds(row, size), pl.ds(col, wide)

    def rows_of(part, q, cc, ss, half=None):
        return parts[part][1].at[q].at[place(part, cc, ss, half)]

    def own_copy(part):
        return pltpu.make_async_copy(parts[part][0], parts[part][1].at[z], loc.at[part])

    def fz(part, q):
        src = parts[part][0].at[place(part, c, s)]
        return remote(src, rows_of(part, z, c, s), fz_s.at[part, q], fz_r.at[part, z], (s, c, q))

    def fz_in(part, q):
        here = rows_of(part, q, c, s)
        return remote(here, here, fz_s.at[part, q], fz_r.at[part, q], (s, c, q))

    def fx(part, q, kind):
        if kind < 2:
            ref, to = rows_of(part, q, c, s), (s1, s2)[kind]
        else:
            ref, to = rows_of(part, q, c, (s1, s2)[kind - 2], kind - 2), (s2, s1)[kind - 2]
        return remote(ref, ref, fx_s.at[part, q, kind], fx_r.at[part, q, kind], (to, c, z))

    def fx_in(part, q, kind):
        if kind < 2:
            ref = rows_of(part, q, c, (s1, s2)[kind])
        else:
            ref = rows_of(part, q, c, s3, kind - 2)
        return remote(ref, ref, fx_s.at[part, q, kind], fx_r.at[part, q, kind], (s1, c, z))

    def fc(part, q):
        ref = rows_of(part, q, c, None)
        return remote(ref, ref, fc_s.at[part, q], fc_r.at[part, q], sib)

    def fc_in(part, q):
        ref = rows_of(part, q, 1 - c, None)
        return remote(ref, ref, fc_s.at[part, q], fc_r.at[part, q], sib)

    def w_start(part):
        own_copy(part).start()
        for q in zz:
            fz(part, q).start()

    def w_plane(part):
        for q in zz:
            fz_in(part, q).wait_recv()
            fx(part, q, 0).start()
            fx(part, q, 1).start()

    def w_cross(part):
        for q in zz:
            fx_in(part, q, 0).wait_recv()
            fx(part, q, 2).start()
            fx_in(part, q, 1).wait_recv()
            fx(part, q, 3).start()

    def w_core(part):
        for q in zz:
            fx_in(part, q, 2).wait_recv()
            fx_in(part, q, 3).wait_recv()
            fc(part, q).start()

    def w_ready(part):
        own_copy(part).wait()
        for q in zz:
            fc_in(part, q).wait_recv()

    stages = dict(plane=w_plane, cross=w_cross, core=w_core, start=w_start)

    def w_finish(part):
        for q in zz:
            fz(part, q).wait_send()
            for kind in range(4):
                fx(part, q, kind).wait_send()
            fc(part, q).wait_send()


    for q in zz:
        wz(q).start()
        seg_out(q).start()
    for part in dims["first"]:
        w_start(part)
    @pl.when(z + 1 < W)
    def _():
        tok_copy(z, 1, 0).start()

    @pl.when(z > 0)
    def _():
        tok_copy(z, -1, 1).start()

    for q in zz:
        vec_out(q).start()

    lane = lax.broadcasted_iota(jnp.int32, (1, LANES), 1)
    spot = lax.broadcasted_iota(jnp.int32, (IDS, LANES), 1) - lax.broadcasted_iota(jnp.int32, (IDS, LANES), 0)
    lanes_in = lax.broadcasted_iota(jnp.int32, (IDS, LANES), 1)
    in_ext = (lanes_in >= group) & (lanes_in < group + IDS)
    put_q = jnp.where(spot == group, 1.0, 0.0).astype(jnp.bfloat16)
    put_k = jnp.where(in_ext & (spot != group), -BIG, 0.0).astype(jnp.bfloat16)
    pad = jnp.zeros((1, LANES - group), jnp.float32)
    bias_q = jnp.concatenate([b_q[...].astype(jnp.float32).reshape(1, -1), pad], axis=1)
    bias_v = jnp.concatenate([b_v[...].astype(jnp.float32).reshape(1, -1), pad], axis=1)
    ids = lax.broadcasted_iota(jnp.int32, (IDS, rows), 0).astype(jnp.float32)

    def k_rows(owner, slot):
        return pl.ds(pl.multiple_of(owner * block + slot * rows, rows), rows)

    def kv(slot, which):
        ref = (kx, vv)[which].at[k_rows(c, slot), :]
        return remote(ref, ref, kv_s.at[which, slot], kv_r.at[which, slot], sib)

    def kv_in(slot, which):
        ref = (kx, vv)[which].at[k_rows(1 - c, slot), :]
        return remote(ref, ref, kv_s.at[which, slot], kv_r.at[which, slot], sib)

    def project(slot):
        made = nn(toks[slot], wcol[...])
        hot = jnp.where(jnp.broadcast_to(segs[slot], (IDS, rows)) == ids, 1.0, 0.0).astype(jnp.bfloat16)
        q_low = (made[:, :LANES] + bias_q).astype(jnp.bfloat16).astype(jnp.float32) * dims["scale"]
        ext_q = tn(hot, put_q)
        for h in range(heads):
            mine = (lane >= h * head_dim) & (lane < (h + 1) * head_dim)
            qx[pl.ds(pl.multiple_of(h * block + slot * rows, rows), rows), :] = (
                jnp.where(mine, q_low, 0.0) + ext_q
            ).astype(jnp.bfloat16)
        kx[k_rows(c, slot), :] = (made[:, LANES : 2 * LANES] + tn(hot, put_k)).astype(jnp.bfloat16)
        vv[k_rows(c, slot), :] = (made[:, 2 * LANES :] + bias_v).astype(jnp.bfloat16)
        kv(slot, 0).start()
        kv(slot, 1).start()

    def qkv_z(part):
        for q in zz:
            wz_in(q).wait_recv()
            for k in (1, 2, 3):
                wp(q, k).start()

    def qkv_plane(part):
        for q in zz:
            for k in (1, 2, 3):
                wp_in(q, k).wait_recv()
            wp(q, 0).start()
        wcol[pl.ds(pl.multiple_of(z * group, 16), group), :] = w_send[z]

    def qkv_core(part):
        for q in zz:
            wp_in(q, 0).wait_recv()
            seg_in(q).wait_recv()

    def forward(far):
        @pl.when(z >= far)
        def _():
            tok_copy(z - far, 1, 0).wait_recv()

            @pl.when(z + 1 < W)
            def _():
                tok_copy(z - far, 1, 0).start()

        @pl.when(z + far < W)
        def _():
            tok_copy(z + far, 1, 0).wait_recv()

            @pl.when(z > 0)
            def _():
                tok_copy(z + far, -1, 1).start()

    def near(far):
        def side(k, carry):
            slot = jnp.where(k == 0, z - far, z + far)

            @pl.when((slot >= 0) & (slot < W))
            def _():
                project(slot)

            return carry

        if far == 0:
            project(z)
        else:
            lax.fori_loop(0, 2, side, 0)

    stages.update(qkv_z=qkv_z, qkv_plane=qkv_plane, qkv_core=qkv_core, forward=forward, near=near)
    for name, part in dims["seq_t"]:
        stages[name](part)
    for j in range(W):
        kv_in(j, 0).wait_recv()
        kv_in(j, 1).wait_recv()
    vt[...] = vv[...].astype(jnp.float32).T.astype(jnp.bfloat16)

    chunk = dims["chunk"]
    n_chunks = total // chunk

    def cx(b):
        return remote(ctx_send.at[b], ctx_recv.at[z], cx_s.at[b], cx_r.at[z], (s, c, b))

    def cx_in(b):
        return remote(ctx_send.at[b], ctx_recv.at[b], cx_s.at[b], cx_r.at[b], (s, c, b))

    def attend(step, carry):
        i = lax.div(step, heads)
        h = lax.rem(step, heads)
        b = lax.rem(z + 1 + i, W)
        query = qx[pl.ds(pl.multiple_of(h * block + b * rows, rows), rows), :]
        top = None
        for n in range(n_chunks):
            got = nt(kx[n * chunk : (n + 1) * chunk, :], query)
            scores[n * chunk : (n + 1) * chunk, :] = got
            high = jnp.max(got, axis=0, keepdims=True)
            top = high if top is None else jnp.maximum(top, high)
        mass = None
        out = None
        here = pl.ds(pl.multiple_of(h * head_dim, head_dim), head_dim)
        for n in range(n_chunks):
            raised = jnp.exp(scores[n * chunk : (n + 1) * chunk, :] - top)
            add = jnp.sum(raised, axis=0, keepdims=True)
            mass = add if mass is None else mass + add
            piece_out = nn(vt[here, n * chunk : (n + 1) * chunk], raised.astype(jnp.bfloat16))
            out = piece_out if out is None else out + piece_out
        att_t[here, pl.ds(pl.multiple_of(b * rows, rows), rows)] = out / mass
        lse[h, :, pl.ds(pl.multiple_of(b * rows, rows), rows)] = top + jnp.log(mass)

        @pl.when(h == heads - 1)
        def _():
            done = att_t[:, pl.ds(pl.multiple_of(b * rows, rows), rows)]
            ctx_send[b] = done.T.astype(jnp.bfloat16)

            @pl.when(i < W - 1)
            def _():
                cx(b).start()

            @pl.when(i == W - 1)
            def _():
                ctx_recv[b] = ctx_send[b]

        for when, name, part in dims["moves_a"]:
            @pl.when(step == when)
            def _():
                stages[name](part)

        return carry

    lax.fori_loop(0, W * heads, attend, 0)
    for q in zz:
        wz(q).wait_send()
    for j in range(W):
        kv(j, 0).wait_send()
        kv(j, 1).wait_send()
    for q in zz:
        cx_in(q).wait_recv()
    for j in range(W):
        ctx[:, j * group : (j + 1) * group] = ctx_recv[j]
    for q in zz:
        vec_in(q).wait_recv()

    def vcore():
        return remote(vc.at[c], vc.at[c], vp_s.at[0], vp_r.at[0], sib)

    def vplane(k):
        return remote(vs.at[s], vs.at[s], vp_s.at[k], vp_r.at[k], (s ^ k, c, z))

    def vz_out(q, t):
        return remote(vx.at[q], vz.at[z], vp_s.at[4 + t], vp_r.at[4 + z], (s, c, q))

    def vz_in(q, t):
        return remote(vx.at[q], vz.at[q], vp_s.at[4 + t], vp_r.at[4 + q], (s, c, q))

    def vec_core():
        vc[c] = grad_vec[...]
        vcore().start()

    def vec_plane():
        vcore().wait_recv()
        vs[s] = vc[0] + vc[1]
        for k in (1, 2, 3):
            vplane(k).start()

    def vec_z():
        for k in (1, 2, 3):
            vplane(k).wait_recv()
        vx[...] = (vs[0] + vs[1]) + (vs[2] + vs[3])
        vz[z] = vx[z]
        for t, q in enumerate(zz):
            vz_out(q, t).start()

    def vec_end():
        for t, q in enumerate(zz):
            vz_in(q, t).wait_recv()
        acc = vz[0]
        for j in range(1, W):
            acc = acc + vz[j]
        g_vec[...] = acc
        vcore().wait_send()
        for k in (1, 2, 3):
            vplane(k).wait_send()
        for t, q in enumerate(zz):
            vz_out(q, t).wait_send()

    kinds = (2, 1, 0, 0)

    def view(ref, a, cc, ss, half=None):
        return ref.at[(slice(None),) + place(kinds[a], cc, ss, half)]

    def within(a, half):
        n, m = ((group // S, width // 2), (group, ff // 8), (ff // W // 8, width))[kinds[a]]
        if kinds[a] == 0:
            return (slice(0, n), slice(0, 128) if half == 0 else slice(128, m))
        if kinds[a] == 1:
            return (slice(half * (n // 2), (half + 1) * (n // 2)), slice(0, m))
        return (slice(0, n), slice(half * (m // 2), (half + 1) * (m // 2)))

    def core_move(a):
        return remote(view(P[a], a, 1 - c, None), CR[a], core_s.at[a], core_r.at[a], sib)

    def add_into(a, cc, ss, half, more):
        at = place(kinds[a], cc, ss, half)
        for j in range(W):
            P[a][(j,) + at] = (P[a][(j,) + at].astype(f32) + more(j).astype(f32)).astype(bf16)

    def core_add(a):
        core_move(a).wait_recv()
        add_into(a, c, None, None, lambda j: CR[a][j])

    def x1(a, half, slot):
        to = (s1, s2)[half]
        at = ((s1, s3) if half == 0 else (s2, s3))[slot]
        k = half * 2 + slot
        return remote(view(P[a], a, c, at, half), X1[a].at[(slot, slice(None)) + within(a, half)], x1_s.at[a, k],
                      x1_r.at[a, k], (to, c, z))

    def x1_send(a):
        for slot in (1, 0):
            for half in range(2):
                x1(a, half, slot).start()

    def x1_far(a):
        for half in range(2):
            x1(a, half, 1).wait_recv()
            add_into(a, c, (s2, s1)[half], half, lambda j: X1[a][(1, j) + within(a, half)])
            x2(a, half).start()

    def x1_own(a):
        for half in range(2):
            x1(a, half, 0).wait_recv()
            add_into(a, c, s, half, lambda j: X1[a][(0, j) + within(a, half)])

    def x2(a, half):
        to = (s2, s1)[half]
        return remote(view(P[a], a, c, to, half), X2[a].at[(slice(None),) + within(a, half)], x2_s.at[a, half],
                      x2_r.at[a, half], (to, c, z))

    def x2_add(a):
        for half in range(2):
            x2(a, half).wait_recv()
            add_into(a, c, s, half, lambda j: X2[a][(j,) + within(a, half)])

    def own_piece(a, q):
        return P[a].at[q].at[place(kinds[a], c, s)]

    def za(a, q, t):
        return remote(own_piece(a, q), Z[a].at[z], za_s.at[a, t], za_r.at[a, z], (s, c, q))

    def za_in(a, q, t):
        return remote(own_piece(a, q), Z[a].at[q], za_s.at[a, t], za_r.at[a, q], (s, c, q))

    def z_send(a):
        for t, q in enumerate(zz):
            za(a, q, t).start()
        Z[a][z] = own_piece(a, z)[...]

    def all_g(a, ref):
        return ref if a == 3 else ref

    def z_add(a):
        for t, q in enumerate(zz):
            za_in(a, q, t).wait_recv()
        at = place(kinds[a], c, s)
        if a == 3:
            for j in range(W):
                G[a][(j,) + at] = Z[a][j]
        else:
            acc = Z[a][0].astype(f32)
            for j in range(1, W):
                acc = acc + Z[a][j].astype(f32)
            G[a][at] = acc.astype(bf16)

    def g_view(a, cc, ss, half=None):
        at = place(kinds[a], cc, ss, half)
        return G[a].at[((slice(None),) + at) if a == 3 else at]

    def ga(a, kind):
        if kind < 2:
            ref, to = g_view(a, c, s), (s1, s2)[kind]
        else:
            ref, to = g_view(a, c, (s1, s2)[kind - 2], kind - 2), (s2, s1)[kind - 2]
        return remote(ref, ref, ga_s.at[a, kind], ga_r.at[a, kind], (to, c, z))

    def ga_in(a, kind):
        ref = g_view(a, c, (s1, s2)[kind]) if kind < 2 else g_view(a, c, s3, kind - 2)
        return remote(ref, ref, ga_s.at[a, kind], ga_r.at[a, kind], (s1, c, z))

    def gc(a):
        ref = g_view(a, c, None)
        return remote(ref, ref, gc_s.at[a], gc_r.at[a], sib)

    def gc_in(a):
        ref = g_view(a, 1 - c, None)
        return remote(ref, ref, gc_s.at[a], gc_r.at[a], sib)

    def g_send(a):
        ga(a, 0).start()
        ga(a, 1).start()

    def g_forward(a):
        for kind in range(2):
            ga_in(a, kind).wait_recv()
            ga(a, 2 + kind).start()

    def g_core(a):
        for kind in range(2):
            ga_in(a, 2 + kind).wait_recv()
        gc(a).start()

    def drain(a):
        core_move(a).wait_send()
        for half in range(2):
            x1(a, half, 0).wait_send()
            x1(a, half, 1).wait_send()
            x2(a, half).wait_send()
        for t, q in enumerate(zz):
            za(a, q, t).wait_send()
        for kind in range(4):
            ga(a, kind).wait_send()
        gc(a).wait_send()

    def weight_grad(a):
        w_finish((2, 1, 0)[a])
        if a == 0:
            for k in range(W):
                full_d[k] = tn(active[k], grad_branch[...]).astype(bf16)
        elif a == 1:
            for k in range(W):
                made = tn(hidden_low[...], grad_inner[k]).astype(bf16)
                for j in range(W):
                    full_i[j, :, k * width : (k + 1) * width] = made[j * group : (j + 1) * group]
        else:
            made = tn(ctx[...], grad_attn[...]).astype(bf16)
            for j in range(W):
                full_o[j] = made[j * group : (j + 1) * group]
        core_move(a).start()

    stages.update(core_add=core_add, x1_send=x1_send, x1_far=x1_far, x1_own=x1_own, x2_add=x2_add, z_send=z_send,
                  z_add=z_add, g_send=g_send, g_forward=g_forward, g_core=g_core, weight_grad=weight_grad,
                  vec_core=lambda a: vec_core(), vec_plane=lambda a: vec_plane(), vec_z=lambda a: vec_z(),
                  vec_end=lambda a: vec_end())

    cuts = dims["cuts"]

    def vec_of(k):
        n = (b_o, gain_1, shift_1, b_d, gain_2, shift_2, b_i)[k].shape[0]
        return jnp.concatenate([vecs[j, :, cuts[k] : cuts[k] + n] for j in range(W)], axis=1)

    def norm(values, gain, shift):
        centred = values - jnp.mean(values, axis=-1, keepdims=True)
        inverse = lax.rsqrt(jnp.mean(centred * centred, axis=-1, keepdims=True) + norm_eps)
        normed = centred * inverse
        return normed * gain + shift, normed, inverse

    def norm_back(grad, normed, inverse, gain):
        scaled = grad * gain
        return inverse * (
            scaled
            - jnp.mean(scaled, axis=-1, keepdims=True)
            - normed * jnp.mean(scaled * normed, axis=-1, keepdims=True)
        )

    def put_vec(k, values):
        n = values.shape[1] // W
        for j in range(W):
            grad_vec[j, :, cuts[k] : cuts[k] + n] = values[:, j * n : (j + 1) * n]

    def total_of(values):
        return jnp.sum(values, axis=0, keepdims=True)

    gain_a, gain_b = vec_of(1), vec_of(4)
    w_ready(0)
    summed = tokens[...].astype(f32) + (nn(ctx[...], full_o[...].reshape(width, width)) + vec_of(0))
    hidden, normed_1, inverse_1 = norm(summed, gain_a, vec_of(2))
    hidden_low[...] = hidden.astype(bf16)
    run("seq_f0")
    w_ready(1)
    spans = [slice(k * width, (k + 1) * width) for k in range(W)]
    bias_in = vec_of(6)
    for k, span in enumerate(spans):
        inner = nn(hidden_low[...], full_i[:, :, span].reshape(width, width)) + bias_in[:, span]
        cdf = 0.5 * (1.0 + lax.erf(inner * (0.5**0.5)))
        active[k] = (inner * cdf).astype(bf16)
        slope[k] = (cdf + inner * (jnp.exp(-0.5 * inner * inner) * dims["density"])).astype(slope.dtype)
    run("seq_f1")
    w_ready(2)
    branch = vec_of(3)
    for k in range(W):
        branch = branch + nn(active[k], full_d[k])
    out, normed_2, inverse_2 = norm(hidden + branch, gain_b, vec_of(5))
    result[...] = out.astype(bf16)
    grad_out = cot[0].astype(f32)
    put_vec(4, total_of(grad_out * normed_2))
    put_vec(5, total_of(grad_out))
    grad_res = norm_back(grad_out, normed_2, inverse_2, gain_b)
    grad_branch[...] = grad_res.astype(bf16)
    put_vec(3, total_of(grad_branch[...].astype(f32)))
    for k in range(W):
        low = (nt(grad_branch[...], full_d[k]) * slope[k].astype(f32)).astype(bf16)
        grad_inner[k] = low
        grad_vec[k, :, cuts[6] : cuts[6] + width] = total_of(low.astype(f32))
    run("seq_f2")
    grad_hidden = grad_res
    for k, span in enumerate(spans):
        grad_hidden = grad_hidden + nt(grad_inner[k], full_i[:, :, span].reshape(width, width))
    put_vec(1, total_of(grad_hidden * normed_1))
    put_vec(2, total_of(grad_hidden))
    grad_first = norm_back(grad_hidden, normed_1, inverse_1, gain_a)
    res[...] = grad_first
    grad_attn[...] = grad_first.astype(bf16)
    put_vec(0, total_of(grad_attn[...].astype(f32)))
    grad_ctx = nt(grad_attn[...], full_o[...].reshape(width, width)).astype(bf16)
    for q in zz:
        cx(q).wait_send()
    d_send = ctx_send
    for j in range(W):
        d_send[j] = grad_ctx[:, j * group : (j + 1) * group]

    def da(q):
        return remote(d_send.at[q], d_recv.at[z], da_s.at[q], da_r.at[z], (s, c, q))

    def da_in(q):
        return remote(d_send.at[q], d_recv.at[q], da_s.at[q], da_r.at[q], (s, c, q))

    for q in zz:
        da(q).start()
    d_recv[z] = d_send[z]

    kt[...] = kx[...].astype(f32).T.astype(bf16)
    dk[...] = jnp.zeros_like(dk)
    dv[...] = jnp.zeros_like(dv)
    run("seq_b")

    def attend_back(step, carry):
        i = lax.div(step, heads)
        h = lax.rem(step, heads)
        b = lax.rem(z + i, W)

        @pl.when((h == 0) & (i > 0))
        def _():
            da_in(b).wait_recv()

        at = pl.ds(pl.multiple_of(b * rows, rows), rows)
        here = pl.ds(pl.multiple_of(h * head_dim, head_dim), head_dim)
        got = d_recv[b].astype(f32)
        got = jnp.concatenate([got, jnp.zeros((rows, LANES - group), f32)], axis=1)
        mask = (lane >= h * head_dim) & (lane < (h + 1) * head_dim)
        grad = jnp.where(mask, got, 0.0)
        delta = jnp.sum(grad.T[:group] * att_t[:, at], axis=0, keepdims=True)
        grad = grad.astype(bf16)
        query = qx[pl.ds(pl.multiple_of(h * block + b * rows, rows), rows), :]
        log_mass = lse[h, :, at]
        acc = None
        for n in range(n_chunks):
            span = slice(n * chunk, (n + 1) * chunk)
            weights = jnp.exp(nt(kx[span, :], query) - log_mass)
            grad_weights = nt(vv[span, :], grad)
            grad_scores = (weights * (grad_weights - delta)).astype(bf16)
            dv[span, :] += nn(weights.astype(bf16), grad)
            dk[span, :] += nn(grad_scores, query)
            add = nn(kt[here, span], grad_scores)
            acc = add if acc is None else acc + add
        dq_t[here, at] = acc * dims["scale"]

        for when, name, a in dims["moves_b"]:
            @pl.when(step == when)
            def _():
                stages[name](a)

        return carry

    lax.fori_loop(0, W * heads, attend_back, 0)

    def kv_move():
        return remote(kv_send, kv_recv, kb_s.at[0], kb_r.at[0], sib)

    other = pl.ds(pl.multiple_of((1 - c) * block, block), block)
    own = pl.ds(pl.multiple_of(c * block, block), block)
    kv_send[:block] = dk[other, :].astype(bf16)
    kv_send[block:] = dv[other, :].astype(bf16)
    kv_move().start()
    run("seq_k")
    pad = jnp.zeros((block, LANES - group), bf16)
    dqkv[:, :LANES] = jnp.concatenate([dq_t[...].T.astype(bf16), pad], axis=1)
    kv_move().wait_recv()
    keep = lane < group
    for m, ref in ((0, dk), (1, dv)):
        whole = ref[own, :] + kv_recv[m * block : (m + 1) * block].astype(f32)
        dqkv[:, (m + 1) * LANES : (m + 2) * LANES] = jnp.where(keep, whole, 0.0).astype(bf16)

    def rx_out(d, step, lane_):
        slot = jnp.where((lane_ == 1) & (d == z - 1 if step < 0 else d == z), W, d)
        return remote(px.at[d], rx.at[slot], rx_s.at[d], rx_r.at[slot], (s, c, z + step))

    def rx_in(slot):
        return remote(px.at[0], rx.at[slot], rx_s.at[0], rx_r.at[slot], (s, c, z))

    def make(d):
        at = pl.ds(pl.multiple_of(d * rows, rows), rows)
        return nt(dqkv[at, :], wcol[...])

    def line(k):
        far = W - 1 - k // 2
        right = jnp.where(z < W // 2, k % 2 == 0, k % 2 == 1)
        d = jnp.where(right, far, W - 1 - far)

        @pl.when(right & (d > z))
        def _():
            px[d] = make(d).astype(bf16)

            @pl.when(z > 0)
            def _():
                rx_in(d).wait_recv()
                px[d] = (px[d].astype(f32) + rx[d].astype(f32)).astype(bf16)

            rx_out(d, 1, 0).start()

        @pl.when(jnp.logical_not(right) & (d < z))
        def _():
            px[d] = make(d).astype(bf16)

            @pl.when(z < W - 1)
            def _():
                rx_in(d).wait_recv()
                px[d] = (px[d].astype(f32) + rx[d].astype(f32)).astype(bf16)

            rx_out(d, -1, 1).start()

    def grad_proj(part):
        made = None
        for j in range(W):
            add = tn(toks[j], dqkv[j * rows : (j + 1) * rows, :])
            made = add if made is None else made + add
        made = made.astype(bf16)
        for j in range(W):
            w_send[j] = made[j * group : (j + 1) * group]
        core_move(3).start()

    def bcore():
        return remote(bc.at[c], bc.at[c], bp_s.at[0], bp_r.at[0], sib)

    def bplane(k):
        return remote(bs.at[s], bs.at[s], bp_s.at[k], bp_r.at[k], (s ^ k, c, z))

    def b_core(part):
        sums = nn(jnp.ones((8, block), bf16), dqkv[...])[0:1]
        bc[c] = jnp.concatenate([sums[:, :LANES], sums[:, 2 * LANES :]], axis=1)
        bcore().start()

    def b_plane(part):
        bcore().wait_recv()
        bs[s] = bc[0] + bc[1]
        for k in (1, 2, 3):
            bplane(k).start()

    def own_rows(part):
        g_tok[...] = make(z) + res[...]

    stages.update(grad_proj=grad_proj, line=line, b_core=b_core, b_plane=b_plane, own_rows=own_rows)
    run("seq_l")

    @pl.when(z > 0)
    def _():
        rx_in(z).wait_recv()
        g_tok[...] += rx[z].astype(f32)

    @pl.when(z < W - 1)
    def _():
        rx_in(W).wait_recv()
        g_tok[...] += rx[W].astype(f32)

    run("seq_g")
    for k in (1, 2, 3):
        bplane(k).wait_recv()
    tot = (bs[0] + bs[1]) + (bs[2] + bs[3])
    g_b[...] = tot
    bcore().wait_send()
    for k in (1, 2, 3):
        bplane(k).wait_send()
    kv_move().wait_send()
    for q in zz:
        da(q).wait_send()
    for j in range(W):
        @pl.when(j > z)
        def _():
            rx_out(j, 1, 0).wait_send()

        @pl.when(j < z)
        def _():
            rx_out(j, -1, 1).wait_send()

    for a in range(4):
        gc_in(a).wait_recv()
        drain(a)


    @pl.when(z + 1 < W)
    def _():
        for j in range(W):
            @pl.when(j <= z)
            def _():
                tok_copy(j, 1, 0).wait_send()

    @pl.when(z > 0)
    def _():
        for j in range(W):
            @pl.when(j >= z)
            def _():
                tok_copy(j, -1, 1).wait_send()

    for q in zz:
        seg_out(q).wait_send()
        vec_out(q).wait_send()
        for k in range(4):
            wp(q, k).wait_send()


def layer_call(dims, *operands):
    S, W, heads = dims["S"], dims["W"], dims["heads"]
    tokens, w_i = operands[0], operands[-2]
    rows, width = tokens.shape
    group = width // W
    block = rows * W
    total = 2 * block
    ff = w_i.shape[1]
    f32, bf16 = jnp.float32, jnp.bfloat16
    vm = pl.BlockSpec(memory_space=pltpu.VMEM)
    hb = pl.BlockSpec(memory_space=pl.ANY)
    dma = pltpu.SemaphoreType.DMA
    shape = jax.ShapeDtypeStruct
    vmem = pltpu.VMEM
    n_vec = dims["n_vec"]
    halves = ((ff // W // 2, width), (group, ff // 2), (group, width // 2), (group, width // 2))
    pieces = ((ff // W // 8, width), (group, ff // 8), (group // S, width // 2), (group // S, width // 2))
    return pl.pallas_call(
        partial(layer_kernel, dims),
        name="layer",
        out_shape=(
            shape((rows, width), bf16),
            shape((rows, width), f32),
            shape((ff // W, width), bf16),
            shape((group, ff), bf16),
            shape((group, width), bf16),
            shape((W, group, 3 * LANES), bf16),
            shape((1, n_vec), f32),
            shape((1, 2 * LANES), f32),
        ),
        in_specs=[vm] * 15 + [hb] * 3,
        out_specs=tuple([vm] * 8),
        scratch_shapes=[
            vmem((W, rows, width), bf16),
            vmem((width, 3 * LANES), bf16),
            vmem((heads * block, LANES), bf16),
            vmem((total, LANES), bf16),
            vmem((total, LANES), bf16),
            vmem((group, block), f32),
            vmem((heads, 1, block), f32),
            vmem((rows, width), bf16),
            vmem((rows, width), f32),
            vmem((W, rows, width), bf16),
            vmem((rows, width), bf16),
            vmem((rows, width), bf16),
            vmem((W, rows, width), bf16),
            vmem((rows, width), bf16),
            vmem((W, 1, n_vec), f32),
            vmem((W, group, width), bf16),
            vmem((W, group, ff), bf16),
            vmem((W, ff // W, width), bf16),
            vmem((W, 1, n_vec), f32),
            vmem((W, rows, width), dims["slope"]),
            vmem((W, 1, rows), f32),
            vmem((W, group, 3 * LANES), bf16),
            vmem((LANES, total), bf16),
            vmem((total, rows), f32),
            vmem((total, rows), f32),
            vmem((W, rows, group), bf16),
            vmem((W, rows, group), bf16),
            vmem((W, rows, group), bf16),
            vmem((block, 3 * LANES), bf16),
            vmem((2 * block, LANES), bf16),
            vmem((W + 1, rows, width), bf16),
            *[vmem((W,) + h, bf16) for h in halves],
            *[vmem((2, W) + p, bf16) for p in pieces],
            *[vmem((W,) + p, bf16) for p in pieces],
            *[vmem((W,) + p, bf16) for p in pieces],
            vmem((W, 1, n_vec), f32),
            vmem((2, W, 1, n_vec), f32),
            vmem((S, W, 1, n_vec), f32),
            vmem((W, 1, n_vec), f32),
            vmem((2, 1, 2 * LANES), f32),
            vmem((S, 1, 2 * LANES), f32),
            dma((2, W)), dma((W,)), dma((2, W)), dma((2, W)), dma((W,)), dma((W,)),
            dma((W, 4)), dma((W, 4)), dma((2, W)), dma((2, W)), dma((W,)), dma((W,)),
            dma((3, W)), dma((3, W)), dma((3, W, 4)), dma((3, W, 4)), dma((3, W)), dma((3, W)),
            dma((3,)),
            dma((W,)), dma((W,)), dma((1,)), dma((1,)), dma((W,)), dma((W + 1,)),
            dma((4,)), dma((4,)), dma((4, 4)), dma((4, 4)), dma((4, 2)), dma((4, 2)),
            dma((4, W)), dma((4, W)), dma((4, 4)), dma((4, 4)), dma((4,)), dma((4,)),
            dma((4 + W,)), dma((4 + W,)), dma((4,)), dma((4,)),
        ],
        compiler_params=pltpu.CompilerParams(
            collective_id=1, has_side_effects=True, vmem_limit_bytes=VMEM_LIMIT
        ),
    )(*operands)


def finish_kernel(dims, result, g_tok, gd, gi, go, gq, vec, g_b,
                  o_res, o_tok, o_q, o_bq, o_k, o_v, o_bv, o_o, o_s0, o_s1, o_s2, o_i, o_s3, o_d, o_s4, o_s5, o_s6):
    f32 = jnp.float32
    W = dims["W"]
    group = o_q.shape[0]
    o_res[0] = result[...]
    o_tok[0] = g_tok[...].astype(jnp.bfloat16)
    o_d[...] = gd[...].astype(f32)
    o_i[...] = gi[...].astype(f32)
    o_o[...] = go[...].astype(f32)
    for j in range(W):
        for m, ref in enumerate((o_q, o_k, o_v)):
            ref[:, j * group : (j + 1) * group] = gq[j, :, m * LANES : m * LANES + group].astype(f32)
    o_bq[...] = g_b[0, :group]
    o_bv[...] = g_b[0, LANES : LANES + group]
    for ref, lo in zip((o_s0, o_s1, o_s2, o_s4, o_s5, o_s6, o_s3), dims["cuts"]):
        ref[...] = vec[0, lo : lo + ref.shape[0]]


def finish_call(dims, result, g_tok, gd, gi, go, gq, vec, g_b):
    f32, bf16 = jnp.float32, jnp.bfloat16
    W = dims["W"]
    rows, width = result.shape
    group = width // W
    ff = width * W
    vm = pl.BlockSpec(memory_space=pltpu.VMEM)
    shape = jax.ShapeDtypeStruct
    small, mat = shape((group,), f32), shape((group, width), f32)
    return pl.pallas_call(
        partial(finish_kernel, dims),
        name="finish",
        out_shape=(shape((1, rows, width), bf16), shape((1, rows, width), bf16), mat, small, mat, mat, small, mat,
                   small, small, small, shape((group, ff), f32), shape((ff // W,), f32), shape((ff // W, width), f32),
                   small, small, small),
        in_specs=[vm] * 8,
        out_specs=tuple([vm] * 17),
        compiler_params=pltpu.CompilerParams(vmem_limit_bytes=VMEM_LIMIT),
    )(result, g_tok, gd, gi, go, gq, vec, g_b)


def fast_device(dims, tokens, segment_ids, w_query, b_query, w_key, w_value, b_value, w_out, b_out, gain_attn,
                shift_attn, w_in, b_in, w_down, b_down, gain_ffn, shift_ffn, cotangent):
    made = layer_call(dims, tokens[0], segment_ids, w_query, w_key, w_value, b_query, b_value, b_out, gain_attn, shift_attn,
                      b_in, b_down, gain_ffn, shift_ffn, cotangent, w_out, w_in, w_down)
    return finish_call(dims, *made)


def plan(mesh):
    return dict(
        S=mesh.shape["seq"], W=mesh.shape["wsh"], heads=HEADS // mesh.shape["wsh"], scale=0.125, chunk=512,
        cuts=(0, 256, 512, 768, 1024, 1280, 1536), n_vec=2304, density=1.0 / math.sqrt(2.0 * math.pi), slope=jnp.bfloat16,
        first=[1, 0],
        seq_t=[("qkv_z", 0), ("qkv_plane", 0), ("forward", 1), ("qkv_core", 0), ("near", 0), ("near", 1), ("plane", 1),
               ("forward", 2), ("near", 2), ("plane", 0), ("cross", 1), ("start", 2), ("forward", 3), ("near", 3),
               ("cross", 0), ("core", 1)],
        moves_a=[(2, "core", 0), (5, "plane", 2), (10, "cross", 2)],
        seq_f0=[], seq_f1=[("core", 2)], seq_f2=[("weight_grad", 0)],
        seq_b=[("core_add", 0), ("x1_send", 0), ("weight_grad", 1), ("weight_grad", 2), ("vec_core", 0)],
        moves_b=[(2, "core_add", 1), (4, "x1_far", 0), (5, "x1_send", 1), (5, "vec_plane", 0), (7, "core_add", 2), (8, "x1_own", 0),
                 (8, "x1_send", 2), (10, "vec_z", 0)],
        seq_k=[("x2_add", 0), ("z_send", 0)],
        seq_l=[("line", 0), ("x1_far", 1), ("grad_proj", 0), ("b_core", 0), ("line", 1), ("core_add", 3), ("x1_send", 3), ("x1_own", 1),
               ("x1_far", 2), ("b_plane", 0), ("x1_own", 2), ("line", 2), ("z_add", 0), ("g_send", 0), ("x2_add", 1), ("z_send", 1),
               ("line", 3), ("x2_add", 2), ("z_send", 2), ("x1_far", 3), ("x1_own", 3), ("g_forward", 0), ("line", 4), ("line", 5),
               ("own_rows", 0), ("vec_end", 0), ("g_core", 0), ("x2_add", 3), ("z_send", 3), ("z_add", 2), ("g_send", 2),
               ("z_add", 1), ("g_send", 1), ("z_add", 3), ("g_send", 3), ("g_forward", 2), ("g_forward", 1), ("g_core", 2), ("g_forward", 3)],
        seq_g=[("g_core", 1), ("g_core", 3)],
    )


def solution(mesh):
    fast = mesh.shape["seq"] == 4 and mesh.shape["ctx"] == 2 and HEADS % mesh.shape["wsh"] == 0
    return jax.shard_map(
        partial(fast_device, plan(mesh)) if fast else per_device,
        mesh=mesh,
        in_specs=(
            P("seq", ("ctx", "wsh"), None),
            P("seq", ("ctx", "wsh")),
            P("wsh", None),
            P("wsh"),
            P("wsh", None),
            P("wsh", None),
            P("wsh"),
            P("wsh", None),
            P("wsh"),
            P("wsh"),
            P("wsh"),
            P("wsh", None),
            P("wsh"),
            P("wsh", None),
            P("wsh"),
            P("wsh"),
            P("wsh"),
            P("seq", ("ctx", "wsh"), None),
        ),
        out_specs=(
            P("seq", ("ctx", "wsh"), None),
            P("seq", ("ctx", "wsh"), None),
            P("wsh", None),
            P("wsh"),
            P("wsh", None),
            P("wsh", None),
            P("wsh"),
            P("wsh", None),
            P("wsh"),
            P("wsh"),
            P("wsh"),
            P("wsh", None),
            P("wsh"),
            P("wsh", None),
            P("wsh"),
            P("wsh"),
            P("wsh"),
        ),
        check_vma=False,
    )
```

```python
from functools import partial
import math

import jax
import jax.numpy as jnp
from jax import lax
from jax.experimental import pallas as pl
from jax.experimental.pallas import tpu as pltpu
from jax.sharding import PartitionSpec as P

HEADS = 12


norm_eps = 1e-12
masked_fill = -1e30


def matmul(left, right):
    return jnp.dot(left, right, preferred_element_type=jnp.float32)


def matmul_left_t(left, right):
    return lax.dot_general(
        left, right, (((0,), (0,)), ((), ())), preferred_element_type=jnp.float32
    )


def matmul_right_t(left, right):
    return lax.dot_general(
        left, right, (((1,), (1,)), ((), ())), preferred_element_type=jnp.float32
    )


def normalize(values, gain, shift):
    centre = jnp.mean(values, axis=-1, keepdims=True)
    centred = values - centre
    inverse = lax.rsqrt(jnp.mean(centred * centred, axis=-1, keepdims=True) + norm_eps)
    normed = centred * inverse
    return (normed * gain + shift, normed, inverse)


def normalize_back(grad_out, normed, inverse, gain):
    grad_gain = jnp.sum(grad_out * normed, axis=0)
    grad_shift = jnp.sum(grad_out, axis=0)
    scaled = grad_out * gain
    grad_in = inverse * (
        scaled
        - jnp.mean(scaled, axis=-1, keepdims=True)
        - normed * jnp.mean(scaled * normed, axis=-1, keepdims=True)
    )
    return (grad_in, grad_gain, grad_shift)


def block_scores(query_blk, key_blk, seg_query, seg_key, score_scale):
    scores = (
        jnp.einsum("qhd,khd->hqk", query_blk, key_blk, preferred_element_type=jnp.float32)
        * score_scale
    )
    same_doc = seg_query[:, None] == seg_key[None, :]
    return (jnp.where(same_doc[None], scores, masked_fill), same_doc)


def block_grads(
    query_blk, dctx_blk, lse_blk, delta_blk, seg_query, key_blk, value_blk, seg_key, score_scale
):
    scores, same_doc = block_scores(query_blk, key_blk, seg_query, seg_key, score_scale)
    weights = jnp.where(same_doc[None], jnp.exp(scores - lse_blk.T[:, :, None]), 0.0)
    grad_weights = jnp.einsum(
        "qhd,khd->hqk", dctx_blk, value_blk, preferred_element_type=jnp.float32
    )
    grad_scores = (weights * (grad_weights - delta_blk.T[:, :, None])).astype(jnp.bfloat16)
    grad_query = None
    grad_key = None
    grad_value = None
    grad_query = (
        jnp.einsum("hqk,khd->qhd", grad_scores, key_blk, preferred_element_type=jnp.float32)
        * score_scale
    )
    grad_key = (
        jnp.einsum("hqk,qhd->khd", grad_scores, query_blk, preferred_element_type=jnp.float32)
        * score_scale
    )
    grad_value = jnp.einsum(
        "hqk,qhd->khd", weights.astype(jnp.bfloat16), dctx_blk, preferred_element_type=jnp.float32
    )
    return (grad_query, grad_key, grad_value)


def per_device(
    tokens,
    segment_ids,
    w_query,
    b_query,
    w_key,
    w_value,
    b_value,
    w_out,
    b_out,
    gain_attn,
    shift_attn,
    w_in,
    b_in,
    w_down,
    b_down,
    gain_ffn,
    shift_ffn,
    cotangent,
):
    (
        full_query,
        bias_query,
        full_key,
        full_value,
        bias_value,
        full_out,
        bias_out,
        gain_one,
        shift_one,
        full_in,
        bias_in,
        full_down,
        bias_down,
        gain_two,
        shift_two,
    ) = (
        lax.all_gather(w_query, "wsh", axis=0, tiled=True),
        lax.all_gather(b_query, "wsh", axis=0, tiled=True),
        lax.all_gather(w_key, "wsh", axis=0, tiled=True),
        lax.all_gather(w_value, "wsh", axis=0, tiled=True),
        lax.all_gather(b_value, "wsh", axis=0, tiled=True),
        lax.all_gather(w_out, "wsh", axis=0, tiled=True),
        lax.all_gather(b_out, "wsh", axis=0, tiled=True),
        lax.all_gather(gain_attn, "wsh", axis=0, tiled=True),
        lax.all_gather(shift_attn, "wsh", axis=0, tiled=True),
        lax.all_gather(w_in, "wsh", axis=0, tiled=True),
        lax.all_gather(b_in, "wsh", axis=0, tiled=True),
        lax.all_gather(w_down, "wsh", axis=0, tiled=True),
        lax.all_gather(b_down, "wsh", axis=0, tiled=True),
        lax.all_gather(gain_ffn, "wsh", axis=0, tiled=True),
        lax.all_gather(shift_ffn, "wsh", axis=0, tiled=True),
    )
    inputs = tokens[0]
    rows = inputs.shape[0]
    width = inputs.shape[1]
    head_dim = width // HEADS
    score_scale = 1.0 / math.sqrt(head_dim)
    seg_float = segment_ids[0].astype(jnp.bfloat16)
    queries = (matmul(inputs, full_query) + bias_query.astype(jnp.float32)).astype(jnp.bfloat16)
    key_rows = matmul(inputs, full_key).astype(jnp.bfloat16)
    values = (matmul(inputs, full_value) + bias_value.astype(jnp.float32)).astype(jnp.bfloat16)
    keys_all, values_all, segs_all = (
        lax.all_gather(key_rows, ("ctx", "wsh"), axis=0, tiled=True),
        lax.all_gather(values, ("ctx", "wsh"), axis=0, tiled=True),
        lax.all_gather(seg_float, ("ctx", "wsh"), axis=0, tiled=True),
    )
    total = keys_all.shape[0]
    key_block = min(512, total)
    block_count = total // key_block
    key_blocks = keys_all.reshape(block_count, key_block, HEADS, head_dim)
    value_blocks = values_all.reshape(block_count, key_block, HEADS, head_dim)
    seg_blocks = segs_all.reshape(block_count, key_block)
    query_heads = queries.reshape(rows, HEADS, head_dim)

    def forward_block(carry, block):
        run_max, run_sum, accum = carry
        key_blk, value_blk, seg_blk = block
        scores, same_doc = block_scores(query_heads, key_blk, seg_float, seg_blk, score_scale)
        new_max = jnp.maximum(run_max, jnp.max(scores, axis=2))
        raised = jnp.where(same_doc[None], jnp.exp(scores - new_max[:, :, None]), 0.0)
        factor = jnp.exp(run_max - new_max)
        run_sum = run_sum * factor + jnp.sum(raised, axis=2)
        accum = accum * factor.T[:, :, None] + jnp.einsum(
            "hqk,khd->qhd",
            raised.astype(jnp.bfloat16),
            value_blk,
            preferred_element_type=jnp.float32,
        )
        return ((new_max, run_sum, accum), None)

    start_state = (
        jnp.full((HEADS, rows), masked_fill, jnp.float32),
        jnp.zeros((HEADS, rows), jnp.float32),
        jnp.zeros((rows, HEADS, head_dim), jnp.float32),
    )
    (run_max, run_sum, accum), unused = lax.scan(
        forward_block, start_state, (key_blocks, value_blocks, seg_blocks)
    )
    attended = accum / run_sum.T[:, :, None]
    lse_rows = (run_max + jnp.log(run_sum)).T
    context = attended.reshape(rows, width).astype(jnp.bfloat16)
    attn_out = matmul(context, full_out) + bias_out.astype(jnp.float32)
    gain_first = gain_one.astype(jnp.float32)
    gain_second = gain_two.astype(jnp.float32)
    hidden, normed_one, inverse_one = normalize(
        inputs.astype(jnp.float32) + attn_out, gain_first, shift_one.astype(jnp.float32)
    )
    hidden_low = hidden.astype(jnp.bfloat16)
    inner = matmul(hidden_low, full_in) + bias_in.astype(jnp.float32)
    active_float, gelu_pull = jax.vjp(partial(jax.nn.gelu, approximate=False), inner)
    active = active_float.astype(jnp.bfloat16)
    branch = matmul(active, full_down) + bias_down.astype(jnp.float32)
    result, normed_two, inverse_two = normalize(
        hidden + branch, gain_second, shift_two.astype(jnp.float32)
    )
    grad_out = cotangent[0].astype(jnp.float32)
    grad_res_two, grad_gain_two, grad_shift_two = normalize_back(
        grad_out, normed_two, inverse_two, gain_second
    )
    grad_branch = grad_res_two.astype(jnp.bfloat16)
    grad_bias_down = jnp.sum(grad_branch.astype(jnp.float32), axis=0)
    grad_full_down = matmul_left_t(active, grad_branch)
    grad_inner = gelu_pull(matmul_right_t(grad_branch, full_down))[0].astype(jnp.bfloat16)
    grad_bias_in = jnp.sum(grad_inner.astype(jnp.float32), axis=0)
    grad_full_in = matmul_left_t(hidden_low, grad_inner)
    grad_hidden = grad_res_two + matmul_right_t(grad_inner, full_in)
    grad_res_one, grad_gain_one, grad_shift_one = normalize_back(
        grad_hidden, normed_one, inverse_one, gain_first
    )
    grad_attn = grad_res_one.astype(jnp.bfloat16)
    grad_bias_out = jnp.sum(grad_attn.astype(jnp.float32), axis=0)
    grad_full_out = matmul_left_t(context, grad_attn)
    grad_context = matmul_right_t(grad_attn, full_out).astype(jnp.bfloat16)
    dctx_heads = grad_context.reshape(rows, HEADS, head_dim)
    delta_rows = jnp.sum(dctx_heads.astype(jnp.float32) * attended, axis=2)
    zero_heads = jnp.zeros((rows, HEADS, head_dim), jnp.float32)

    def back_block(grad_acc, block):
        key_blk, value_blk, seg_blk = block
        part_query, part_key, part_value = block_grads(
            query_heads,
            dctx_heads,
            lse_rows,
            delta_rows,
            seg_float,
            key_blk,
            value_blk,
            seg_blk,
            score_scale,
        )
        return (grad_acc + part_query, (part_key, part_value))

    grad_q, (key_parts, value_parts) = lax.scan(
        back_block, zero_heads, (key_blocks, value_blocks, seg_blocks)
    )
    grad_key_own, grad_value_own = (
        lax.psum_scatter(
            key_parts.reshape(total, width), ("ctx", "wsh"), scatter_dimension=0, tiled=True
        ),
        lax.psum_scatter(
            value_parts.reshape(total, width), ("ctx", "wsh"), scatter_dimension=0, tiled=True
        ),
    )
    grad_queries = grad_q.reshape(rows, width).astype(jnp.bfloat16)
    grad_keys = grad_key_own.astype(jnp.bfloat16)
    grad_values = grad_value_own.astype(jnp.bfloat16)
    grad_full_query = matmul_left_t(inputs, grad_queries)
    grad_bias_query = jnp.sum(grad_queries.astype(jnp.float32), axis=0)
    grad_full_key = matmul_left_t(inputs, grad_keys)
    grad_full_value = matmul_left_t(inputs, grad_values)
    grad_bias_value = jnp.sum(grad_values.astype(jnp.float32), axis=0)
    grad_input = (
        grad_res_one
        + matmul_right_t(grad_queries, full_query)
        + matmul_right_t(grad_keys, full_key)
        + matmul_right_t(grad_values, full_value)
    )
    (
        share_query,
        share_bias_query,
        share_key,
        share_value,
        share_bias_value,
        share_out,
        share_bias_out,
        share_gain_one,
        share_shift_one,
        share_in,
        share_bias_in,
        share_down,
        share_bias_down,
        share_gain_two,
        share_shift_two,
    ) = (
        lax.psum_scatter(
            grad_full_query.astype(jnp.bfloat16), "wsh", scatter_dimension=0, tiled=True
        ).astype(jnp.float32),
        lax.psum_scatter(
            grad_bias_query.astype(jnp.bfloat16), "wsh", scatter_dimension=0, tiled=True
        ).astype(jnp.float32),
        lax.psum_scatter(
            grad_full_key.astype(jnp.bfloat16), "wsh", scatter_dimension=0, tiled=True
        ).astype(jnp.float32),
        lax.psum_scatter(
            grad_full_value.astype(jnp.bfloat16), "wsh", scatter_dimension=0, tiled=True
        ).astype(jnp.float32),
        lax.psum_scatter(
            grad_bias_value.astype(jnp.bfloat16), "wsh", scatter_dimension=0, tiled=True
        ).astype(jnp.float32),
        lax.psum_scatter(
            grad_full_out.astype(jnp.bfloat16), "wsh", scatter_dimension=0, tiled=True
        ).astype(jnp.float32),
        lax.psum_scatter(
            grad_bias_out.astype(jnp.bfloat16), "wsh", scatter_dimension=0, tiled=True
        ).astype(jnp.float32),
        lax.psum_scatter(
            grad_gain_one.astype(jnp.bfloat16), "wsh", scatter_dimension=0, tiled=True
        ).astype(jnp.float32),
        lax.psum_scatter(
            grad_shift_one.astype(jnp.bfloat16), "wsh", scatter_dimension=0, tiled=True
        ).astype(jnp.float32),
        lax.psum_scatter(
            grad_full_in.astype(jnp.bfloat16), "wsh", scatter_dimension=0, tiled=True
        ).astype(jnp.float32),
        lax.psum_scatter(
            grad_bias_in.astype(jnp.bfloat16), "wsh", scatter_dimension=0, tiled=True
        ).astype(jnp.float32),
        lax.psum_scatter(
            grad_full_down.astype(jnp.bfloat16), "wsh", scatter_dimension=0, tiled=True
        ).astype(jnp.float32),
        lax.psum_scatter(
            grad_bias_down.astype(jnp.bfloat16), "wsh", scatter_dimension=0, tiled=True
        ).astype(jnp.float32),
        lax.psum_scatter(
            grad_gain_two.astype(jnp.bfloat16), "wsh", scatter_dimension=0, tiled=True
        ).astype(jnp.float32),
        lax.psum_scatter(
            grad_shift_two.astype(jnp.bfloat16), "wsh", scatter_dimension=0, tiled=True
        ).astype(jnp.float32),
    )
    summed = lax.psum(
        (
            share_query,
            share_bias_query,
            share_key,
            share_value,
            share_bias_value,
            share_out,
            share_bias_out,
            share_gain_one,
            share_shift_one,
            share_in,
            share_bias_in,
            share_down,
            share_bias_down,
            share_gain_two,
            share_shift_two,
        ),
        ("seq", "ctx"),
    )
    return (
        result.astype(jnp.bfloat16)[None],
        grad_input.astype(jnp.bfloat16)[None],
        summed[0],
        summed[1],
        summed[2],
        summed[3],
        summed[4],
        summed[5],
        summed[6],
        summed[7],
        summed[8],
        summed[9],
        summed[10],
        summed[11],
        summed[12],
        summed[13],
        summed[14],
    )


MESH_ID = pl.DeviceIdType.MESH
LANES = 256
IDS = 16
BIG = float(2.0**99)
VMEM_LIMIT = 62 * 2**20


def remote(src, dst, send, recv, where):
    return pltpu.make_async_remote_copy(
        src_ref=src, dst_ref=dst, send_sem=send, recv_sem=recv, device_id=where, device_id_type=MESH_ID
    )


def nt(left, right):
    return lax.dot_general(left, right, (((1,), (1,)), ((), ())), preferred_element_type=jnp.float32)


def tn(left, right):
    return lax.dot_general(left, right, (((0,), (0,)), ((), ())), preferred_element_type=jnp.float32)


def nn(left, right):
    return jnp.dot(left, right, preferred_element_type=jnp.float32)


def greet(peers):
    barrier = pltpu.get_barrier_semaphore()
    for peer in peers:
        pl.semaphore_signal(barrier, inc=1, device_id=peer, device_id_type=MESH_ID)
    pl.semaphore_wait(barrier, len(peers))


def layer_kernel(
    dims,
    tokens, seg, w_q, w_k, w_v, b_q, b_v, b_o, gain_1, shift_1, b_i, b_d, gain_2, shift_2, cot, w_o, w_i, w_d,
    result, g_tok, gd, gi, go, gq, g_vec, g_b,
    toks, wcol, qx, kx, vv, att_t, lse, ctx, res, active, grad_branch, hidden_low, grad_inner, grad_attn, grad_vec,
    full_o, full_i, full_d, vecs, slope, segs, w_send, vt, scores, dv, ctx_send, ctx_recv, d_recv, dqkv, kv_recv, rx,
    bufs, deltas, vx, vc, vs, vz, bc, bs,
    tok_s, tok_r, sv_s, sv_r, wz_s, wz_r, wp_s, wp_r, kv_s, kv_r, cx_s, cx_r,
    fz_s, fz_r, fx_s, fx_r, fc_s, fc_r, loc,
    da_s, da_r, kb_s, kb_r, rx_s, rx_r, core_s, core_r, x1_s, x1_r, x2_s, x2_r, za_s, za_r, ga_s, ga_r, gc_s, gc_r,
    vp_s, vp_r, bp_s, bp_r,
):
    S, W, heads = dims["S"], dims["W"], dims["heads"]
    rows, width = tokens.shape
    f32, bf16 = jnp.float32, jnp.bfloat16
    group = width // W
    head_dim = group // heads
    block = rows * W
    total = 2 * block
    ff = w_i.shape[1]
    P = (full_d, full_d, full_i, full_i, full_o, w_send)
    G = (gd, gd, gi, gi, go, gq)
    CR, X1, X2, Z = bufs[:6], bufs[6:12], bufs[12:18], bufs[18:24]
    last = 5
    kt, dk, kv_send, px, dq_t = vt, scores, kx, active, att_t

    def run(name):
        for stage, part in dims[name]:
            stages[stage](part)

    s, c, z = lax.axis_index("seq"), lax.axis_index("ctx"), lax.axis_index("wsh")
    sib = (s, 1 - c, z)
    s1, s2, s3 = s ^ 1, s ^ 2, s ^ 3
    shifts = list(range(1, W))
    zz = [lax.rem(z + t, W) for t in shifts]
    barrier = pltpu.get_barrier_semaphore()
    peers = [sib] + [(p, c, z) for p in (s1, s2, s3)] + [(s, c, q) for q in zz]
    for peer in peers:
        pl.semaphore_signal(barrier, inc=1, device_id=peer, device_id_type=MESH_ID)
    toks[z] = tokens[...]
    segs[z] = seg[...].astype(jnp.float32)
    for ref, lo in zip((b_o, gain_1, shift_1, b_d, gain_2, shift_2, b_i), dims["cuts"]):
        vecs[z, :, lo : lo + ref.shape[0]] = ref[...].astype(jnp.float32).reshape(1, -1)

    for j in range(W):
        for m, ref in enumerate((w_q, w_k, w_v)):
            part = ref[:, j * group : (j + 1) * group]
            part = jnp.concatenate([part, jnp.zeros((group, LANES - group), part.dtype)], axis=1)
            w_send[j, :, m * LANES : (m + 1) * LANES] = part

    pl.semaphore_wait(barrier, len(peers))

    slab, wide = group // S, 3 * LANES // 2

    def col_at(ref, base, cc, ss):
        rows_at = pl.ds(pl.multiple_of(base + (0 if ss is None else ss * slab), 16), group if ss is None else slab)
        return ref.at[rows_at, pl.ds(pl.multiple_of(cc * wide, 128), wide)]

    def wz(q):
        return remote(col_at(w_send.at[q], 0, c, s), col_at(wcol, z * group, c, s), wz_s.at[q], wz_r.at[z], (s, c, q))

    def wz_in(q):
        here = col_at(wcol, q * group, c, s)
        return remote(here, here, wz_s.at[q], wz_r.at[q], (s, c, q))

    def wp(q, k):
        ref = col_at(wcol, q * group, c, s if k else None)
        return remote(ref, ref, wp_s.at[q, k], wp_r.at[q, k], (s ^ k, c, z) if k else sib)

    def wp_in(q, k):
        ref = col_at(wcol, q * group, c, s ^ k) if k else col_at(wcol, q * group, 1 - c, None)
        return remote(ref, ref, wp_s.at[q, k], wp_r.at[q, k], sib)

    def seg_out(q):
        return remote(segs.at[z], segs.at[z], sv_s.at[0, q], sv_r.at[0, z], (s, c, q))

    def seg_in(q):
        return remote(segs.at[q], segs.at[q], sv_s.at[0, q], sv_r.at[0, q], (s, c, q))

    def vec_out(q):
        return remote(vecs.at[z], vecs.at[z], sv_s.at[1, q], sv_r.at[1, z], (s, c, q))

    def vec_in(q):
        return remote(vecs.at[q], vecs.at[q], sv_s.at[1, q], sv_r.at[1, q], (s, c, q))

    def tok_copy(slot, step, lane):
        return remote(toks.at[slot], toks.at[slot], tok_s.at[lane, slot], tok_r.at[slot], (s, c, z + step))

    def cut_of(how, row, n, m, shard, whole):
        return dict(how=how, row=row, n=n, m=m, shard=shard, whole=whole)

    down = ff // W // 2
    cuts_o = cut_of(0, 0, group, width, w_o, full_o)
    cuts_i = [cut_of(1, u * (group // 2), group // 2, ff, w_i, full_i) for u in range(2)]
    cuts_d = [cut_of(2, u * down, down, width, w_d, full_d) for u in range(2)]
    parts = (cuts_o, *cuts_i, *cuts_d)

    def place(cut, cc, ss, half=None):
        n, m = cut["n"], cut["m"]
        if cut["how"] == 0:
            row, size = (0, n) if ss is None else (ss * (n // S), n // S)
            col, wide = cc * (m // 2), m // 2
            if half is not None:
                col, wide = col + (0 if half == 0 else 128), (128 if half == 0 else m // 2 - 128)
        elif cut["how"] == 1:
            row, size = 0, n
            col, wide = cc * (m // 2) + (0 if ss is None else ss * (m // 8)), m // 2 if ss is None else m // 8
            if half is not None:
                row, size = half * (n // 2), n // 2
        else:
            row, size = cc * (n // 2) + (0 if ss is None else ss * (n // 8)), n // 2 if ss is None else n // 8
            col, wide = 0, m
            if half is not None:
                col, wide = half * (m // 2), m // 2
        row = cut["row"] + row
        if not isinstance(row, int):
            row = pl.multiple_of(row, 16)
        if not isinstance(col, int):
            col = pl.multiple_of(col, 128)
        return pl.ds(row, size), pl.ds(col, wide)

    def rows_of(part, q, cc, ss, half=None):
        return parts[part]["whole"].at[q].at[place(parts[part], cc, ss, half)]

    def own_copy(w):
        shard, whole = ((w_o, full_o), (w_i, full_i), (w_d, full_d))[w]
        return pltpu.make_async_copy(shard, whole.at[z], loc.at[w])

    def fz(part, q):
        src = parts[part]["shard"].at[place(parts[part], c, s)]
        return remote(src, rows_of(part, z, c, s), fz_s.at[part, q], fz_r.at[part, z], (s, c, q))

    def fz_in(part, q):
        here = rows_of(part, q, c, s)
        return remote(here, here, fz_s.at[part, q], fz_r.at[part, q], (s, c, q))

    def fx(part, q, kind):
        if kind < 2:
            ref, to = rows_of(part, q, c, s), (s1, s2)[kind]
        else:
            ref, to = rows_of(part, q, c, (s1, s2)[kind - 2], kind - 2), (s2, s1)[kind - 2]
        return remote(ref, ref, fx_s.at[part, q, kind], fx_r.at[part, q, kind], (to, c, z))

    def fx_in(part, q, kind):
        if kind < 2:
            ref = rows_of(part, q, c, (s1, s2)[kind])
        else:
            ref = rows_of(part, q, c, s3, kind - 2)
        return remote(ref, ref, fx_s.at[part, q, kind], fx_r.at[part, q, kind], (s1, c, z))

    def fc(part, q):
        ref = rows_of(part, q, c, None)
        return remote(ref, ref, fc_s.at[part, q], fc_r.at[part, q], sib)

    def fc_in(part, q):
        ref = rows_of(part, q, 1 - c, None)
        return remote(ref, ref, fc_s.at[part, q], fc_r.at[part, q], sib)

    def w_start(part):
        for q in zz:
            fz(part, q).start()

    def w_plane(part):
        for q in zz:
            fz_in(part, q).wait_recv()
            fx(part, q, 0).start()
            fx(part, q, 1).start()

    def w_cross(part):
        for q in zz:
            fx_in(part, q, 0).wait_recv()
            fx(part, q, 2).start()
            fx_in(part, q, 1).wait_recv()
            fx(part, q, 3).start()

    def w_core(part):
        for q in zz:
            fx_in(part, q, 2).wait_recv()
            fx_in(part, q, 3).wait_recv()
            fc(part, q).start()

    def w_ready(w):
        own_copy(w).wait()
        for part in ((0,), (1, 2), (3, 4))[w]:
            for q in zz:
                fc_in(part, q).wait_recv()

    stages = dict(plane=w_plane, cross=w_cross, core=w_core, start=w_start)

    def w_finish(part):
        for q in zz:
            fz(part, q).wait_send()
            for kind in range(4):
                fx(part, q, kind).wait_send()
            fc(part, q).wait_send()


    for q in zz:
        wz(q).start()
        seg_out(q).start()
    for w in range(3):
        own_copy(w).start()
    for part in dims["first"]:
        w_start(part)
    @pl.when(z + 1 < W)
    def _():
        tok_copy(z, 1, 0).start()

    @pl.when(z > 0)
    def _():
        tok_copy(z, -1, 1).start()

    for q in zz:
        vec_out(q).start()

    lane = lax.broadcasted_iota(jnp.int32, (1, LANES), 1)
    spot = lax.broadcasted_iota(jnp.int32, (IDS, LANES), 1) - lax.broadcasted_iota(jnp.int32, (IDS, LANES), 0)
    lanes_in = lax.broadcasted_iota(jnp.int32, (IDS, LANES), 1)
    in_ext = (lanes_in >= group) & (lanes_in < group + IDS)
    put_q = jnp.where(spot == group, 1.0, 0.0).astype(jnp.bfloat16)
    put_k = jnp.where(in_ext & (spot != group), -BIG, 0.0).astype(jnp.bfloat16)
    pad = jnp.zeros((1, LANES - group), jnp.float32)
    bias_q = jnp.concatenate([b_q[...].astype(jnp.float32).reshape(1, -1), pad], axis=1)
    bias_v = jnp.concatenate([b_v[...].astype(jnp.float32).reshape(1, -1), pad], axis=1)
    ids = lax.broadcasted_iota(jnp.int32, (IDS, rows), 0).astype(jnp.float32)

    def k_rows(owner, slot):
        return pl.ds(pl.multiple_of(owner * block + slot * rows, rows), rows)

    def kv(slot, which):
        ref = (kx, vv)[which].at[k_rows(c, slot), :]
        return remote(ref, ref, kv_s.at[which, slot], kv_r.at[which, slot], sib)

    def kv_in(slot, which):
        ref = (kx, vv)[which].at[k_rows(1 - c, slot), :]
        return remote(ref, ref, kv_s.at[which, slot], kv_r.at[which, slot], sib)

    def project(slot):
        made = nn(toks[slot], wcol[...])
        hot = jnp.where(jnp.broadcast_to(segs[slot], (IDS, rows)) == ids, 1.0, 0.0).astype(jnp.bfloat16)
        q_low = (made[:, :LANES] + bias_q).astype(jnp.bfloat16).astype(jnp.float32) * dims["scale"]
        ext_q = tn(hot, put_q)
        for h in range(heads):
            mine = (lane >= h * head_dim) & (lane < (h + 1) * head_dim)
            qx[pl.ds(pl.multiple_of(h * block + slot * rows, rows), rows), :] = (
                jnp.where(mine, q_low, 0.0) + ext_q
            ).astype(jnp.bfloat16)
        kx[k_rows(c, slot), :] = (made[:, LANES : 2 * LANES] + tn(hot, put_k)).astype(jnp.bfloat16)
        vv[k_rows(c, slot), :] = (made[:, 2 * LANES :] + bias_v).astype(jnp.bfloat16)
        kv(slot, 0).start()
        kv(slot, 1).start()

    def qkv_z(part):
        for q in zz:
            wz_in(q).wait_recv()
            for k in (1, 2, 3):
                wp(q, k).start()

    def qkv_plane(part):
        for q in zz:
            for k in (1, 2, 3):
                wp_in(q, k).wait_recv()
            wp(q, 0).start()
        wcol[pl.ds(pl.multiple_of(z * group, 16), group), :] = w_send[z]

    def qkv_core(part):
        for q in zz:
            wp_in(q, 0).wait_recv()
            seg_in(q).wait_recv()

    def forward(far):
        @pl.when(z >= far)
        def _():
            tok_copy(z - far, 1, 0).wait_recv()

            @pl.when(z + 1 < W)
            def _():
                tok_copy(z - far, 1, 0).start()

        @pl.when(z + far < W)
        def _():
            tok_copy(z + far, 1, 0).wait_recv()

            @pl.when(z > 0)
            def _():
                tok_copy(z + far, -1, 1).start()

    def near(far):
        def side(k, carry):
            slot = jnp.where(k == 0, z - far, z + far)

            @pl.when((slot >= 0) & (slot < W))
            def _():
                project(slot)

            return carry

        if far == 0:
            project(z)
        else:
            lax.fori_loop(0, 2, side, 0)

    stages.update(qkv_z=qkv_z, qkv_plane=qkv_plane, qkv_core=qkv_core, forward=forward, near=near)
    for name, part in dims["seq_t"]:
        stages[name](part)
    for j in range(W):
        kv_in(j, 0).wait_recv()
        kv_in(j, 1).wait_recv()
    vt[...] = vv[...].astype(jnp.float32).T.astype(jnp.bfloat16)

    chunk = dims["chunk"]
    n_chunks = total // chunk

    def cx(b):
        return remote(ctx_send.at[b], ctx_recv.at[z], cx_s.at[b], cx_r.at[z], (s, c, b))

    def cx_in(b):
        return remote(ctx_send.at[b], ctx_recv.at[b], cx_s.at[b], cx_r.at[b], (s, c, b))

    def attend(step, carry):
        i = lax.div(step, heads)
        h = lax.rem(step, heads)
        b = lax.rem(z + 1 + i, W)
        query = qx[pl.ds(pl.multiple_of(h * block + b * rows, rows), rows), :]
        top = None
        for n in range(n_chunks):
            got = nt(kx[n * chunk : (n + 1) * chunk, :], query)
            scores[n * chunk : (n + 1) * chunk, :] = got
            high = jnp.max(got, axis=0, keepdims=True)
            top = high if top is None else jnp.maximum(top, high)
        mass = None
        out = None
        here = pl.ds(pl.multiple_of(h * head_dim, head_dim), head_dim)
        for n in range(n_chunks):
            raised = jnp.exp(scores[n * chunk : (n + 1) * chunk, :] - top)
            add = jnp.sum(raised, axis=0, keepdims=True)
            mass = add if mass is None else mass + add
            piece_out = nn(vt[here, n * chunk : (n + 1) * chunk], raised.astype(jnp.bfloat16))
            out = piece_out if out is None else out + piece_out
        att_t[here, pl.ds(pl.multiple_of(b * rows, rows), rows)] = out / mass
        lse[h, :, pl.ds(pl.multiple_of(b * rows, rows), rows)] = top + jnp.log(mass)

        @pl.when(h == heads - 1)
        def _():
            done = att_t[:, pl.ds(pl.multiple_of(b * rows, rows), rows)]
            ctx_send[b] = done.T.astype(jnp.bfloat16)

            @pl.when(i < W - 1)
            def _():
                cx(b).start()

            @pl.when(i == W - 1)
            def _():
                ctx_recv[b] = ctx_send[b]

        for when, name, part in dims["moves_a"]:
            @pl.when(step == when)
            def _():
                stages[name](part)

        return carry

    lax.fori_loop(0, W * heads, attend, 0)
    for q in zz:
        wz(q).wait_send()
    for j in range(W):
        kv(j, 0).wait_send()
        kv(j, 1).wait_send()
    for q in zz:
        cx_in(q).wait_recv()
    for j in range(W):
        ctx[:, j * group : (j + 1) * group] = ctx_recv[j]
    for q in zz:
        vec_in(q).wait_recv()

    def vcore():
        return remote(vc.at[c], vc.at[c], vp_s.at[0], vp_r.at[0], sib)

    def vplane(k):
        return remote(vs.at[s], vs.at[s], vp_s.at[k], vp_r.at[k], (s ^ k, c, z))

    def vz_out(q, t):
        return remote(vx.at[q], vz.at[z], vp_s.at[4 + t], vp_r.at[4 + z], (s, c, q))

    def vz_in(q, t):
        return remote(vx.at[q], vz.at[q], vp_s.at[4 + t], vp_r.at[4 + q], (s, c, q))

    def vec_core():
        vc[c] = grad_vec[...]
        vcore().start()

    def vec_plane():
        vcore().wait_recv()
        vs[s] = vc[0] + vc[1]
        for k in (1, 2, 3):
            vplane(k).start()

    def vec_z():
        for k in (1, 2, 3):
            vplane(k).wait_recv()
        vx[...] = (vs[0] + vs[1]) + (vs[2] + vs[3])
        vz[z] = vx[z]
        for t, q in enumerate(zz):
            vz_out(q, t).start()

    def vec_end():
        for t, q in enumerate(zz):
            vz_in(q, t).wait_recv()
        acc = vz[0]
        for j in range(1, W):
            acc = acc + vz[j]
        g_vec[...] = acc
        vcore().wait_send()
        for k in (1, 2, 3):
            vplane(k).wait_send()
        for t, q in enumerate(zz):
            vz_out(q, t).wait_send()

    kinds = (*cuts_d, *cuts_i, cuts_o, cuts_o)

    def view(ref, a, cc, ss, half=None):
        return ref.at[(slice(None),) + place(kinds[a], cc, ss, half)]

    def within(a, half):
        n, m = kinds[a]["n"], kinds[a]["m"]
        if kinds[a]["how"] == 0:
            return (slice(0, n // S), slice(0, 128) if half == 0 else slice(128, m // 2))
        if kinds[a]["how"] == 1:
            return (slice(half * (n // 2), (half + 1) * (n // 2)), slice(0, m // 8))
        return (slice(0, n // 8), slice(half * (m // 2), (half + 1) * (m // 2)))

    def core_move(a):
        return remote(view(P[a], a, 1 - c, None), CR[a], core_s.at[a], core_r.at[a], sib)

    def add_into(a, cc, ss, half, more):
        at = place(kinds[a], cc, ss, half)
        for j in range(W):
            P[a][(j,) + at] = (P[a][(j,) + at].astype(f32) + more(j).astype(f32)).astype(bf16)

    def core_add(a):
        core_move(a).wait_recv()
        add_into(a, c, None, None, lambda j: CR[a][j])

    def x1(a, half, slot):
        to = (s1, s2)[half]
        at = ((s1, s3) if half == 0 else (s2, s3))[slot]
        k = half * 2 + slot
        return remote(view(P[a], a, c, at, half), X1[a].at[(slot, slice(None)) + within(a, half)], x1_s.at[a, k],
                      x1_r.at[a, k], (to, c, z))

    def x1_send(a):
        for slot in (1, 0):
            for half in range(2):
                x1(a, half, slot).start()

    def x1_far(a):
        for half in range(2):
            x1(a, half, 1).wait_recv()
            add_into(a, c, (s2, s1)[half], half, lambda j: X1[a][(1, j) + within(a, half)])
            x2(a, half).start()

    def x1_own(a):
        for half in range(2):
            x1(a, half, 0).wait_recv()
            add_into(a, c, s, half, lambda j: X1[a][(0, j) + within(a, half)])

    def x2(a, half):
        to = (s2, s1)[half]
        return remote(view(P[a], a, c, to, half), X2[a].at[(slice(None),) + within(a, half)], x2_s.at[a, half],
                      x2_r.at[a, half], (to, c, z))

    def x2_add(a):
        for half in range(2):
            x2(a, half).wait_recv()
            add_into(a, c, s, half, lambda j: X2[a][(j,) + within(a, half)])

    def own_piece(a, q):
        return P[a].at[q].at[place(kinds[a], c, s)]

    def za(a, q, t):
        return remote(own_piece(a, q), Z[a].at[z], za_s.at[a, t], za_r.at[a, z], (s, c, q))

    def za_in(a, q, t):
        return remote(own_piece(a, q), Z[a].at[q], za_s.at[a, t], za_r.at[a, q], (s, c, q))

    def z_send(a):
        for t, q in enumerate(zz):
            za(a, q, t).start()
        Z[a][z] = own_piece(a, z)[...]

    def z_add(a):
        for t, q in enumerate(zz):
            za_in(a, q, t).wait_recv()
        at = place(kinds[a], c, s)
        if a == last:
            for j in range(W):
                G[a][(j,) + at] = Z[a][j]
        else:
            acc = Z[a][0].astype(f32)
            for j in range(1, W):
                acc = acc + Z[a][j].astype(f32)
            G[a][at] = acc.astype(bf16)

    def g_view(a, cc, ss, half=None):
        at = place(kinds[a], cc, ss, half)
        return G[a].at[((slice(None),) + at) if a == last else at]

    def ga(a, kind):
        if kind < 2:
            ref, to = g_view(a, c, s), (s1, s2)[kind]
        else:
            ref, to = g_view(a, c, (s1, s2)[kind - 2], kind - 2), (s2, s1)[kind - 2]
        return remote(ref, ref, ga_s.at[a, kind], ga_r.at[a, kind], (to, c, z))

    def ga_in(a, kind):
        ref = g_view(a, c, (s1, s2)[kind]) if kind < 2 else g_view(a, c, s3, kind - 2)
        return remote(ref, ref, ga_s.at[a, kind], ga_r.at[a, kind], (s1, c, z))

    def gc(a):
        ref = g_view(a, c, None)
        return remote(ref, ref, gc_s.at[a], gc_r.at[a], sib)

    def gc_in(a):
        ref = g_view(a, 1 - c, None)
        return remote(ref, ref, gc_s.at[a], gc_r.at[a], sib)

    def g_send(a):
        ga(a, 0).start()
        ga(a, 1).start()

    def g_forward(a):
        for kind in range(2):
            ga_in(a, kind).wait_recv()
            ga(a, 2 + kind).start()

    def g_core(a):
        for kind in range(2):
            ga_in(a, 2 + kind).wait_recv()
        gc(a).start()

    def drain(a):
        core_move(a).wait_send()
        for half in range(2):
            x1(a, half, 0).wait_send()
            x1(a, half, 1).wait_send()
            x2(a, half).wait_send()
        for t, q in enumerate(zz):
            za(a, q, t).wait_send()
        for kind in range(4):
            ga(a, kind).wait_send()
        gc(a).wait_send()

    def weight_grad(a):
        if a < 2:
            w_finish(3 + a)
            lanes = slice(a * down, (a + 1) * down)
            for k in range(W):
                full_d[k, lanes, :] = tn(active[k, :, lanes], grad_branch[...]).astype(bf16)
            core_move(a).start()
        elif a == 2:
            w_finish(1)
            w_finish(2)
            for k in range(W):
                made = tn(hidden_low[...], grad_inner[k]).astype(bf16)
                for j in range(W):
                    full_i[j, :, k * width : (k + 1) * width] = made[j * group : (j + 1) * group]
            core_move(2).start()
            core_move(3).start()
        else:
            w_finish(0)
            made = tn(ctx[...], grad_attn[...]).astype(bf16)
            for j in range(W):
                full_o[j] = made[j * group : (j + 1) * group]
            core_move(4).start()

    stages.update(core_add=core_add, x1_send=x1_send, x1_far=x1_far, x1_own=x1_own, x2_add=x2_add, z_send=z_send,
                  z_add=z_add, g_send=g_send, g_forward=g_forward, g_core=g_core, weight_grad=weight_grad,
                  vec_core=lambda a: vec_core(), vec_plane=lambda a: vec_plane(), vec_z=lambda a: vec_z(),
                  vec_end=lambda a: vec_end())

    cuts = dims["cuts"]

    def vec_of(k):
        n = (b_o, gain_1, shift_1, b_d, gain_2, shift_2, b_i)[k].shape[0]
        return jnp.concatenate([vecs[j, :, cuts[k] : cuts[k] + n] for j in range(W)], axis=1)

    def norm(values, gain, shift):
        centred = values - jnp.mean(values, axis=-1, keepdims=True)
        inverse = lax.rsqrt(jnp.mean(centred * centred, axis=-1, keepdims=True) + norm_eps)
        normed = centred * inverse
        return normed * gain + shift, normed, inverse

    def norm_back(grad, normed, inverse, gain):
        scaled = grad * gain
        return inverse * (
            scaled
            - jnp.mean(scaled, axis=-1, keepdims=True)
            - normed * jnp.mean(scaled * normed, axis=-1, keepdims=True)
        )

    def put_vec(k, values):
        n = values.shape[1] // W
        for j in range(W):
            grad_vec[j, :, cuts[k] : cuts[k] + n] = values[:, j * n : (j + 1) * n]

    def total_of(values):
        return jnp.sum(values, axis=0, keepdims=True)

    gain_a, gain_b = vec_of(1), vec_of(4)
    w_ready(0)
    summed = tokens[...].astype(f32) + (nn(ctx[...], full_o[...].reshape(width, width)) + vec_of(0))
    hidden, normed_1, inverse_1 = norm(summed, gain_a, vec_of(2))
    hidden_low[...] = hidden.astype(bf16)
    run("seq_f0")
    w_ready(1)
    spans = [slice(k * width, (k + 1) * width) for k in range(W)]
    bias_in = vec_of(6)
    for k, span in enumerate(spans):
        inner = nn(hidden_low[...], full_i[:, :, span].reshape(width, width)) + bias_in[:, span]
        cdf = 0.5 * (1.0 + lax.erf(inner * (0.5**0.5)))
        active[k] = (inner * cdf).astype(bf16)
        slope[k] = (cdf + inner * (jnp.exp(-0.5 * inner * inner) * dims["density"])).astype(slope.dtype)
    run("seq_f1")
    w_ready(2)
    branch = vec_of(3)
    for k in range(W):
        branch = branch + nn(active[k], full_d[k])
    out, normed_2, inverse_2 = norm(hidden + branch, gain_b, vec_of(5))
    result[...] = out.astype(bf16)
    grad_out = cot[0].astype(f32)
    put_vec(4, total_of(grad_out * normed_2))
    put_vec(5, total_of(grad_out))
    grad_res = norm_back(grad_out, normed_2, inverse_2, gain_b)
    grad_branch[...] = grad_res.astype(bf16)
    put_vec(3, total_of(grad_branch[...].astype(f32)))
    for k in range(W):
        low = (nt(grad_branch[...], full_d[k]) * slope[k].astype(f32)).astype(bf16)
        grad_inner[k] = low
        grad_vec[k, :, cuts[6] : cuts[6] + width] = total_of(low.astype(f32))
    run("seq_f2")
    grad_hidden = grad_res
    for k, span in enumerate(spans):
        grad_hidden = grad_hidden + nt(grad_inner[k], full_i[:, :, span].reshape(width, width))
    put_vec(1, total_of(grad_hidden * normed_1))
    put_vec(2, total_of(grad_hidden))
    grad_first = norm_back(grad_hidden, normed_1, inverse_1, gain_a)
    res[...] = grad_first
    grad_attn[...] = grad_first.astype(bf16)
    put_vec(0, total_of(grad_attn[...].astype(f32)))
    grad_ctx = nt(grad_attn[...], full_o[...].reshape(width, width)).astype(bf16)
    for q in zz:
        cx(q).wait_send()
    d_send = ctx_send
    for j in range(W):
        d_send[j] = grad_ctx[:, j * group : (j + 1) * group]

    def da(q):
        return remote(d_send.at[q], d_recv.at[z], da_s.at[q], da_r.at[z], (s, c, q))

    def da_in(q):
        return remote(d_send.at[q], d_recv.at[q], da_s.at[q], da_r.at[q], (s, c, q))

    for q in zz:
        da(q).start()
    d_recv[z] = d_send[z]

    kt[...] = kx[...].astype(f32).T.astype(bf16)
    dk[...] = jnp.zeros_like(dk)
    dv[...] = jnp.zeros_like(dv)
    run("seq_b")

    def attend_back(step, carry):
        i = lax.div(step, heads)
        h = lax.rem(step, heads)
        b = lax.rem(z + i, W)

        @pl.when((h == 0) & (i > 0))
        def _():
            da_in(b).wait_recv()

        at = pl.ds(pl.multiple_of(b * rows, rows), rows)
        here = pl.ds(pl.multiple_of(h * head_dim, head_dim), head_dim)
        got = d_recv[b].astype(f32)
        got = jnp.concatenate([got, jnp.zeros((rows, LANES - group), f32)], axis=1)
        mask = (lane >= h * head_dim) & (lane < (h + 1) * head_dim)
        grad = jnp.where(mask, got, 0.0).astype(bf16)

        @pl.when(h == 0)
        def _():
            both = got.T[:group] * att_t[:, at]
            for k in range(heads):
                deltas[k] = jnp.sum(both[k * head_dim : (k + 1) * head_dim], axis=0, keepdims=True)

        delta = deltas[h]
        query = qx[pl.ds(pl.multiple_of(h * block + b * rows, rows), rows), :]
        log_mass = lse[h, :, at]
        acc = None
        for n in range(n_chunks):
            span = slice(n * chunk, (n + 1) * chunk)
            weights = jnp.exp(nt(kx[span, :], query) - log_mass)
            grad_weights = nt(vv[span, :], grad)
            grad_scores = (weights * (grad_weights - delta)).astype(bf16)
            dv[span, :] += nn(weights.astype(bf16), grad)
            dk[span, :] += nn(grad_scores, query)
            add = nn(kt[here, span], grad_scores)
            acc = add if acc is None else acc + add
        dq_t[here, at] = acc * dims["scale"]

        for when, name, a in dims["moves_b"]:
            @pl.when(step == when)
            def _():
                stages[name](a)

        return carry

    lax.fori_loop(0, W * heads, attend_back, 0)

    def kv_move():
        return remote(kv_send, kv_recv, kb_s.at[0], kb_r.at[0], sib)

    other = pl.ds(pl.multiple_of((1 - c) * block, block), block)
    own = pl.ds(pl.multiple_of(c * block, block), block)
    kv_send[:block] = dk[other, :].astype(bf16)
    kv_send[block:] = dv[other, :].astype(bf16)
    kv_move().start()
    run("seq_k")
    pad = jnp.zeros((block, LANES - group), bf16)
    dqkv[:, :LANES] = jnp.concatenate([dq_t[...].T.astype(bf16), pad], axis=1)
    kv_move().wait_recv()
    keep = lane < group
    for m, ref in ((0, dk), (1, dv)):
        whole = ref[own, :] + kv_recv[m * block : (m + 1) * block].astype(f32)
        dqkv[:, (m + 1) * LANES : (m + 2) * LANES] = jnp.where(keep, whole, 0.0).astype(bf16)

    def rx_out(d, step, lane_):
        slot = jnp.where((lane_ == 1) & (d == z - 1 if step < 0 else d == z), W, d)
        return remote(px.at[d], rx.at[slot], rx_s.at[d], rx_r.at[slot], (s, c, z + step))

    def rx_in(slot):
        return remote(px.at[0], rx.at[slot], rx_s.at[0], rx_r.at[slot], (s, c, z))

    def make(d):
        at = pl.ds(pl.multiple_of(d * rows, rows), rows)
        return nt(dqkv[at, :], wcol[...])

    def line(k):
        far = W - 1 - k // 2
        right = jnp.where(z < W // 2, k % 2 == 0, k % 2 == 1)
        d = jnp.where(right, far, W - 1 - far)

        @pl.when(right & (d > z))
        def _():
            px[d] = make(d).astype(bf16)

            @pl.when(z > 0)
            def _():
                rx_in(d).wait_recv()
                px[d] = (px[d].astype(f32) + rx[d].astype(f32)).astype(bf16)

            rx_out(d, 1, 0).start()

        @pl.when(jnp.logical_not(right) & (d < z))
        def _():
            px[d] = make(d).astype(bf16)

            @pl.when(z < W - 1)
            def _():
                rx_in(d).wait_recv()
                px[d] = (px[d].astype(f32) + rx[d].astype(f32)).astype(bf16)

            rx_out(d, -1, 1).start()

    def grad_proj(part):
        made = None
        for j in range(W):
            add = tn(toks[j], dqkv[j * rows : (j + 1) * rows, :])
            made = add if made is None else made + add
        made = made.astype(bf16)
        for j in range(W):
            w_send[j] = made[j * group : (j + 1) * group]
        core_move(last).start()

    def bcore():
        return remote(bc.at[c], bc.at[c], bp_s.at[0], bp_r.at[0], sib)

    def bplane(k):
        return remote(bs.at[s], bs.at[s], bp_s.at[k], bp_r.at[k], (s ^ k, c, z))

    def b_core(part):
        sums = nn(jnp.ones((8, block), bf16), dqkv[...])[0:1]
        bc[c] = jnp.concatenate([sums[:, :LANES], sums[:, 2 * LANES :]], axis=1)
        bcore().start()

    def b_plane(part):
        bcore().wait_recv()
        bs[s] = bc[0] + bc[1]
        for k in (1, 2, 3):
            bplane(k).start()

    def own_rows(part):
        res[...] += make(z)

    stages.update(grad_proj=grad_proj, line=line, b_core=b_core, b_plane=b_plane, own_rows=own_rows)
    run("seq_l")

    @pl.when(z > 0)
    def _():
        rx_in(z).wait_recv()
        res[...] += rx[z].astype(f32)

    @pl.when(z < W - 1)
    def _():
        rx_in(W).wait_recv()
        res[...] += rx[W].astype(f32)

    g_tok[...] = res[...].astype(bf16)
    run("seq_g")
    for k in (1, 2, 3):
        bplane(k).wait_recv()
    tot = (bs[0] + bs[1]) + (bs[2] + bs[3])
    g_b[...] = tot
    bcore().wait_send()
    for k in (1, 2, 3):
        bplane(k).wait_send()
    kv_move().wait_send()
    for q in zz:
        da(q).wait_send()
    for j in range(W):
        @pl.when(j > z)
        def _():
            rx_out(j, 1, 0).wait_send()

        @pl.when(j < z)
        def _():
            rx_out(j, -1, 1).wait_send()

    for a in range(6):
        gc_in(a).wait_recv()
        drain(a)


    @pl.when(z + 1 < W)
    def _():
        for j in range(W):
            @pl.when(j <= z)
            def _():
                tok_copy(j, 1, 0).wait_send()

    @pl.when(z > 0)
    def _():
        for j in range(W):
            @pl.when(j >= z)
            def _():
                tok_copy(j, -1, 1).wait_send()

    for q in zz:
        seg_out(q).wait_send()
        vec_out(q).wait_send()
        for k in range(4):
            wp(q, k).wait_send()


def layer_call(dims, *operands):
    S, W, heads = dims["S"], dims["W"], dims["heads"]
    tokens, w_i = operands[0], operands[-2]
    rows, width = tokens.shape
    group = width // W
    block = rows * W
    total = 2 * block
    ff = w_i.shape[1]
    f32, bf16 = jnp.float32, jnp.bfloat16
    vm = pl.BlockSpec(memory_space=pltpu.VMEM)
    hb = pl.BlockSpec(memory_space=pl.ANY)
    dma = pltpu.SemaphoreType.DMA
    shape = jax.ShapeDtypeStruct
    vmem = pltpu.VMEM
    n_vec = dims["n_vec"]
    n_d, n_i = ff // W // 2, group // 2
    halves = ((n_d // 2, width),) * 2 + ((n_i, ff // 2),) * 2 + ((group, width // 2),) * 2
    pieces = ((n_d // 8, width),) * 2 + ((n_i, ff // 8),) * 2 + ((group // S, width // 2),) * 2
    return pl.pallas_call(
        partial(layer_kernel, dims),
        name="layer",
        out_shape=(
            shape((rows, width), bf16),
            shape((rows, width), bf16),
            shape((ff // W, width), bf16),
            shape((group, ff), bf16),
            shape((group, width), bf16),
            shape((W, group, 3 * LANES), bf16),
            shape((1, n_vec), f32),
            shape((1, 2 * LANES), f32),
        ),
        in_specs=[vm] * 15 + [hb] * 3,
        out_specs=tuple([vm] * 8),
        scratch_shapes=[
            vmem((W, rows, width), bf16),
            vmem((width, 3 * LANES), bf16),
            vmem((heads * block, LANES), bf16),
            vmem((total, LANES), bf16),
            vmem((total, LANES), bf16),
            vmem((group, block), f32),
            vmem((heads, 1, block), f32),
            vmem((rows, width), bf16),
            vmem((rows, width), f32),
            vmem((W, rows, width), bf16),
            vmem((rows, width), bf16),
            vmem((rows, width), bf16),
            vmem((W, rows, width), bf16),
            vmem((rows, width), bf16),
            vmem((W, 1, n_vec), f32),
            vmem((W, group, width), bf16),
            vmem((W, group, ff), bf16),
            vmem((W, ff // W, width), bf16),
            vmem((W, 1, n_vec), f32),
            vmem((W, rows, width), dims["slope"]),
            vmem((W, 1, rows), f32),
            vmem((W, group, 3 * LANES), bf16),
            vmem((LANES, total), bf16),
            vmem((total, rows), f32),
            vmem((total, rows), f32),
            vmem((W, rows, group), bf16),
            vmem((W, rows, group), bf16),
            vmem((W, rows, group), bf16),
            vmem((block, 3 * LANES), bf16),
            vmem((2 * block, LANES), bf16),
            vmem((W + 1, rows, width), bf16),
            [vmem((W,) + h, bf16) for h in halves]
            + [vmem((2, W) + p, bf16) for p in pieces]
            + [vmem((W,) + p, bf16) for p in pieces] * 2,
            vmem((heads, 1, rows), f32),
            vmem((W, 1, n_vec), f32),
            vmem((2, W, 1, n_vec), f32),
            vmem((S, W, 1, n_vec), f32),
            vmem((W, 1, n_vec), f32),
            vmem((2, 1, 2 * LANES), f32),
            vmem((S, 1, 2 * LANES), f32),
            dma((2, W)), dma((W,)), dma((2, W)), dma((2, W)), dma((W,)), dma((W,)),
            dma((W, 4)), dma((W, 4)), dma((2, W)), dma((2, W)), dma((W,)), dma((W,)),
            dma((5, W)), dma((5, W)), dma((5, W, 4)), dma((5, W, 4)), dma((5, W)), dma((5, W)),
            dma((3,)),
            dma((W,)), dma((W,)), dma((1,)), dma((1,)), dma((W,)), dma((W + 1,)),
            dma((6,)), dma((6,)), dma((6, 4)), dma((6, 4)), dma((6, 2)), dma((6, 2)),
            dma((6, W)), dma((6, W)), dma((6, 4)), dma((6, 4)), dma((6,)), dma((6,)),
            dma((4 + W,)), dma((4 + W,)), dma((4,)), dma((4,)),
        ],
        compiler_params=pltpu.CompilerParams(
            collective_id=1, has_side_effects=True, vmem_limit_bytes=VMEM_LIMIT
        ),
    )(*operands)


def finish_kernel(dims, result, g_tok, gd, gi, go, gq, vec, g_b,
                  o_res, o_tok, o_q, o_bq, o_k, o_v, o_bv, o_o, o_s0, o_s1, o_s2, o_i, o_s3, o_d, o_s4, o_s5, o_s6):
    f32 = jnp.float32
    W = dims["W"]
    group = o_bq.shape[0]
    o_res[0] = result[...]
    o_tok[0] = g_tok[...]
    o_d[...] = gd[...].astype(f32)
    o_i[...] = gi[...].astype(f32)
    o_o[...] = go[...].astype(f32)
    for j in range(W):
        for m, ref in enumerate((o_q, o_k, o_v)):
            ref[:, j * group : (j + 1) * group] = gq[j, :, m * LANES : m * LANES + group].astype(f32)
    o_bq[...] = g_b[0, :group]
    o_bv[...] = g_b[0, LANES : LANES + group]
    for ref, lo in zip((o_s0, o_s1, o_s2, o_s4, o_s5, o_s6, o_s3), dims["cuts"]):
        ref[...] = vec[0, lo : lo + ref.shape[0]]


def finish_call(dims, result, g_tok, gd, gi, go, gq, vec, g_b):
    f32, bf16 = jnp.float32, jnp.bfloat16
    W, steps = dims["W"], 4
    rows, width = result.shape
    group = width // W
    ff = gi.shape[1]
    down = gd.shape[0]
    shape = jax.ShapeDtypeStruct
    small, mat = shape((group,), f32), shape((group, width), f32)

    def cut(n, m):
        return pl.BlockSpec((n // steps, m), lambda k: (k, 0))

    def deep(d, n, m):
        return pl.BlockSpec((d, n // steps, m), lambda k: (0, k, 0))

    def flat(n):
        return pl.BlockSpec((n,), lambda k: (0,))

    def whole(a):
        return pl.BlockSpec(a.shape, lambda k: (0, 0))

    one, sheet = flat(group), cut(group, width)
    return pl.pallas_call(
        partial(finish_kernel, dims),
        name="finish",
        grid=(steps,),
        out_shape=(shape((1, rows, width), bf16), shape((1, rows, width), bf16), mat, small, mat, mat, small, mat,
                   small, small, small, shape((group, ff), f32), shape((ff // W,), f32), shape((down, width), f32),
                   small, small, small),
        in_specs=[cut(rows, width), cut(rows, width), cut(down, width), cut(group, ff), sheet,
                  deep(W, group, gq.shape[2]), whole(vec), whole(g_b)],
        out_specs=(deep(1, rows, width), deep(1, rows, width), sheet, one, sheet, sheet, one, sheet, one, one, one,
                   cut(group, ff), flat(ff // W), cut(down, width), one, one, one),
        compiler_params=pltpu.CompilerParams(vmem_limit_bytes=VMEM_LIMIT),
    )(result, g_tok, gd, gi, go, gq, vec, g_b)


def fast_device(dims, tokens, segment_ids, w_query, b_query, w_key, w_value, b_value, w_out, b_out, gain_attn,
                shift_attn, w_in, b_in, w_down, b_down, gain_ffn, shift_ffn, cotangent):
    made = layer_call(dims, tokens[0], segment_ids, w_query, w_key, w_value, b_query, b_value, b_out, gain_attn, shift_attn,
                      b_in, b_down, gain_ffn, shift_ffn, cotangent, w_out, w_in, w_down)
    return finish_call(dims, *made)


def plan(mesh):
    return dict(
        S=mesh.shape["seq"], W=mesh.shape["wsh"], heads=HEADS // mesh.shape["wsh"], scale=0.125, chunk=512,
        cuts=(0, 256, 512, 768, 1024, 1280, 1536), n_vec=2304, density=1.0 / math.sqrt(2.0 * math.pi), slope=jnp.bfloat16,
        first=[],
        seq_t=[
            ("start", 0), ("forward", 1), ("qkv_z", 0), ("qkv_plane", 0), ("qkv_core", 0), ("plane", 0),
            ("start", 1), ("start", 2), ("forward", 2), ("near", 1), ("plane", 1), ("near", 0), ("plane", 2),
            ("forward", 3), ("start", 3), ("near", 2), ("cross", 1), ("near", 3),
        ],
        moves_a=[
            (0, "cross", 0), (1, "start", 4), (1, "plane", 3), (3, "cross", 2), (6, "cross", 3), (8, "plane", 4),
            (8, "core", 2), (8, "core", 1), (10, "core", 0), (11, "cross", 4), (11, "core", 3),
        ],
        seq_f0=[
            ("core", 4),
        ],
        seq_f1=[],
        seq_f2=[
            ("weight_grad", 1), ("weight_grad", 0),
        ],
        seq_b=[
            ("core_add", 1), ("x1_send", 1), ("core_add", 0), ("vec_core", 0),
        ],
        moves_b=[
            (0, "x1_send", 0), (1, "weight_grad", 3), (1, "weight_grad", 2), (1, "core_add", 4),
            (3, "x1_far", 0), (3, "x1_far", 1), (4, "x1_send", 4), (5, "vec_plane", 0), (5, "x1_own", 0),
            (5, "x2_add", 0), (6, "z_send", 0), (6, "core_add", 3), (7, "x1_send", 3), (7, "x1_own", 1),
            (7, "x2_add", 1), (8, "x1_far", 4), (8, "core_add", 2), (8, "x1_send", 2), (8, "z_send", 1),
            (9, "x1_far", 3), (10, "vec_z", 0), (10, "z_add", 0), (10, "x1_own", 4), (11, "x1_own", 3),
        ],
        seq_k=[
            ("x2_add", 4), ("z_send", 4), ("z_add", 1), ("x1_far", 2),
        ],
        seq_l=[
            ("line", 0), ("grad_proj", 0), ("x1_own", 2), ("b_core", 0), ("x2_add", 2), ("z_send", 2),
            ("core_add", 5), ("x1_send", 5), ("b_plane", 0), ("line", 1), ("g_send", 0), ("x1_far", 5),
            ("line", 2), ("x1_own", 5), ("x2_add", 5), ("z_send", 5), ("g_forward", 0), ("g_send", 1),
            ("z_add", 2), ("own_rows", 0), ("z_add", 4), ("line", 3), ("line", 4), ("g_send", 4), ("x2_add", 3),
            ("vec_end", 0), ("z_send", 3), ("g_send", 2), ("line", 5), ("z_add", 5), ("g_send", 5),
        ],
        seq_g=[
            ("g_forward", 1), ("g_forward", 4), ("g_forward", 5), ("z_add", 3), ("g_send", 3), ("g_core", 0),
            ("g_core", 1), ("g_core", 5), ("g_forward", 2), ("g_forward", 3), ("g_core", 4), ("g_core", 2),
            ("g_core", 3),
        ],
    )


def solution(mesh):
    fast = mesh.shape["seq"] == 4 and mesh.shape["ctx"] == 2 and HEADS % mesh.shape["wsh"] == 0
    return jax.shard_map(
        partial(fast_device, plan(mesh)) if fast else per_device,
        mesh=mesh,
        in_specs=(
            P("seq", ("ctx", "wsh"), None),
            P("seq", ("ctx", "wsh")),
            P("wsh", None),
            P("wsh"),
            P("wsh", None),
            P("wsh", None),
            P("wsh"),
            P("wsh", None),
            P("wsh"),
            P("wsh"),
            P("wsh"),
            P("wsh", None),
            P("wsh"),
            P("wsh", None),
            P("wsh"),
            P("wsh"),
            P("wsh"),
            P("seq", ("ctx", "wsh"), None),
        ),
        out_specs=(
            P("seq", ("ctx", "wsh"), None),
            P("seq", ("ctx", "wsh"), None),
            P("wsh", None),
            P("wsh"),
            P("wsh", None),
            P("wsh", None),
            P("wsh"),
            P("wsh", None),
            P("wsh"),
            P("wsh"),
            P("wsh"),
            P("wsh", None),
            P("wsh"),
            P("wsh", None),
            P("wsh"),
            P("wsh"),
            P("wsh"),
        ),
        check_vma=False,
    )
```

```python
from functools import partial
import math

import jax
import jax.numpy as jnp
from jax import lax
from jax.experimental import pallas as pl
from jax.experimental.pallas import tpu as pltpu
from jax.sharding import PartitionSpec as P

HEADS = 12


norm_eps = 1e-12
masked_fill = -1e30


def matmul(left, right):
    return jnp.dot(left, right, preferred_element_type=jnp.float32)


def matmul_left_t(left, right):
    return lax.dot_general(
        left, right, (((0,), (0,)), ((), ())), preferred_element_type=jnp.float32
    )


def matmul_right_t(left, right):
    return lax.dot_general(
        left, right, (((1,), (1,)), ((), ())), preferred_element_type=jnp.float32
    )


def normalize(values, gain, shift):
    centre = jnp.mean(values, axis=-1, keepdims=True)
    centred = values - centre
    inverse = lax.rsqrt(jnp.mean(centred * centred, axis=-1, keepdims=True) + norm_eps)
    normed = centred * inverse
    return (normed * gain + shift, normed, inverse)


def normalize_back(grad_out, normed, inverse, gain):
    grad_gain = jnp.sum(grad_out * normed, axis=0)
    grad_shift = jnp.sum(grad_out, axis=0)
    scaled = grad_out * gain
    grad_in = inverse * (
        scaled
        - jnp.mean(scaled, axis=-1, keepdims=True)
        - normed * jnp.mean(scaled * normed, axis=-1, keepdims=True)
    )
    return (grad_in, grad_gain, grad_shift)


def block_scores(query_blk, key_blk, seg_query, seg_key, score_scale):
    scores = (
        jnp.einsum("qhd,khd->hqk", query_blk, key_blk, preferred_element_type=jnp.float32)
        * score_scale
    )
    same_doc = seg_query[:, None] == seg_key[None, :]
    return (jnp.where(same_doc[None], scores, masked_fill), same_doc)


def block_grads(
    query_blk, dctx_blk, lse_blk, delta_blk, seg_query, key_blk, value_blk, seg_key, score_scale
):
    scores, same_doc = block_scores(query_blk, key_blk, seg_query, seg_key, score_scale)
    weights = jnp.where(same_doc[None], jnp.exp(scores - lse_blk.T[:, :, None]), 0.0)
    grad_weights = jnp.einsum(
        "qhd,khd->hqk", dctx_blk, value_blk, preferred_element_type=jnp.float32
    )
    grad_scores = (weights * (grad_weights - delta_blk.T[:, :, None])).astype(jnp.bfloat16)
    grad_query = None
    grad_key = None
    grad_value = None
    grad_query = (
        jnp.einsum("hqk,khd->qhd", grad_scores, key_blk, preferred_element_type=jnp.float32)
        * score_scale
    )
    grad_key = (
        jnp.einsum("hqk,qhd->khd", grad_scores, query_blk, preferred_element_type=jnp.float32)
        * score_scale
    )
    grad_value = jnp.einsum(
        "hqk,qhd->khd", weights.astype(jnp.bfloat16), dctx_blk, preferred_element_type=jnp.float32
    )
    return (grad_query, grad_key, grad_value)


def per_device(
    tokens,
    segment_ids,
    w_query,
    b_query,
    w_key,
    w_value,
    b_value,
    w_out,
    b_out,
    gain_attn,
    shift_attn,
    w_in,
    b_in,
    w_down,
    b_down,
    gain_ffn,
    shift_ffn,
    cotangent,
):
    (
        full_query,
        bias_query,
        full_key,
        full_value,
        bias_value,
        full_out,
        bias_out,
        gain_one,
        shift_one,
        full_in,
        bias_in,
        full_down,
        bias_down,
        gain_two,
        shift_two,
    ) = (
        lax.all_gather(w_query, "wsh", axis=0, tiled=True),
        lax.all_gather(b_query, "wsh", axis=0, tiled=True),
        lax.all_gather(w_key, "wsh", axis=0, tiled=True),
        lax.all_gather(w_value, "wsh", axis=0, tiled=True),
        lax.all_gather(b_value, "wsh", axis=0, tiled=True),
        lax.all_gather(w_out, "wsh", axis=0, tiled=True),
        lax.all_gather(b_out, "wsh", axis=0, tiled=True),
        lax.all_gather(gain_attn, "wsh", axis=0, tiled=True),
        lax.all_gather(shift_attn, "wsh", axis=0, tiled=True),
        lax.all_gather(w_in, "wsh", axis=0, tiled=True),
        lax.all_gather(b_in, "wsh", axis=0, tiled=True),
        lax.all_gather(w_down, "wsh", axis=0, tiled=True),
        lax.all_gather(b_down, "wsh", axis=0, tiled=True),
        lax.all_gather(gain_ffn, "wsh", axis=0, tiled=True),
        lax.all_gather(shift_ffn, "wsh", axis=0, tiled=True),
    )
    inputs = tokens[0]
    rows = inputs.shape[0]
    width = inputs.shape[1]
    head_dim = width // HEADS
    score_scale = 1.0 / math.sqrt(head_dim)
    seg_float = segment_ids[0].astype(jnp.bfloat16)
    queries = (matmul(inputs, full_query) + bias_query.astype(jnp.float32)).astype(jnp.bfloat16)
    key_rows = matmul(inputs, full_key).astype(jnp.bfloat16)
    values = (matmul(inputs, full_value) + bias_value.astype(jnp.float32)).astype(jnp.bfloat16)
    keys_all, values_all, segs_all = (
        lax.all_gather(key_rows, ("ctx", "wsh"), axis=0, tiled=True),
        lax.all_gather(values, ("ctx", "wsh"), axis=0, tiled=True),
        lax.all_gather(seg_float, ("ctx", "wsh"), axis=0, tiled=True),
    )
    total = keys_all.shape[0]
    key_block = min(512, total)
    block_count = total // key_block
    key_blocks = keys_all.reshape(block_count, key_block, HEADS, head_dim)
    value_blocks = values_all.reshape(block_count, key_block, HEADS, head_dim)
    seg_blocks = segs_all.reshape(block_count, key_block)
    query_heads = queries.reshape(rows, HEADS, head_dim)

    def forward_block(carry, block):
        run_max, run_sum, accum = carry
        key_blk, value_blk, seg_blk = block
        scores, same_doc = block_scores(query_heads, key_blk, seg_float, seg_blk, score_scale)
        new_max = jnp.maximum(run_max, jnp.max(scores, axis=2))
        raised = jnp.where(same_doc[None], jnp.exp(scores - new_max[:, :, None]), 0.0)
        factor = jnp.exp(run_max - new_max)
        run_sum = run_sum * factor + jnp.sum(raised, axis=2)
        accum = accum * factor.T[:, :, None] + jnp.einsum(
            "hqk,khd->qhd",
            raised.astype(jnp.bfloat16),
            value_blk,
            preferred_element_type=jnp.float32,
        )
        return ((new_max, run_sum, accum), None)

    start_state = (
        jnp.full((HEADS, rows), masked_fill, jnp.float32),
        jnp.zeros((HEADS, rows), jnp.float32),
        jnp.zeros((rows, HEADS, head_dim), jnp.float32),
    )
    (run_max, run_sum, accum), unused = lax.scan(
        forward_block, start_state, (key_blocks, value_blocks, seg_blocks)
    )
    attended = accum / run_sum.T[:, :, None]
    lse_rows = (run_max + jnp.log(run_sum)).T
    context = attended.reshape(rows, width).astype(jnp.bfloat16)
    attn_out = matmul(context, full_out) + bias_out.astype(jnp.float32)
    gain_first = gain_one.astype(jnp.float32)
    gain_second = gain_two.astype(jnp.float32)
    hidden, normed_one, inverse_one = normalize(
        inputs.astype(jnp.float32) + attn_out, gain_first, shift_one.astype(jnp.float32)
    )
    hidden_low = hidden.astype(jnp.bfloat16)
    inner = matmul(hidden_low, full_in) + bias_in.astype(jnp.float32)
    active_float, gelu_pull = jax.vjp(partial(jax.nn.gelu, approximate=False), inner)
    active = active_float.astype(jnp.bfloat16)
    branch = matmul(active, full_down) + bias_down.astype(jnp.float32)
    result, normed_two, inverse_two = normalize(
        hidden + branch, gain_second, shift_two.astype(jnp.float32)
    )
    grad_out = cotangent[0].astype(jnp.float32)
    grad_res_two, grad_gain_two, grad_shift_two = normalize_back(
        grad_out, normed_two, inverse_two, gain_second
    )
    grad_branch = grad_res_two.astype(jnp.bfloat16)
    grad_bias_down = jnp.sum(grad_branch.astype(jnp.float32), axis=0)
    grad_full_down = matmul_left_t(active, grad_branch)
    grad_inner = gelu_pull(matmul_right_t(grad_branch, full_down))[0].astype(jnp.bfloat16)
    grad_bias_in = jnp.sum(grad_inner.astype(jnp.float32), axis=0)
    grad_full_in = matmul_left_t(hidden_low, grad_inner)
    grad_hidden = grad_res_two + matmul_right_t(grad_inner, full_in)
    grad_res_one, grad_gain_one, grad_shift_one = normalize_back(
        grad_hidden, normed_one, inverse_one, gain_first
    )
    grad_attn = grad_res_one.astype(jnp.bfloat16)
    grad_bias_out = jnp.sum(grad_attn.astype(jnp.float32), axis=0)
    grad_full_out = matmul_left_t(context, grad_attn)
    grad_context = matmul_right_t(grad_attn, full_out).astype(jnp.bfloat16)
    dctx_heads = grad_context.reshape(rows, HEADS, head_dim)
    delta_rows = jnp.sum(dctx_heads.astype(jnp.float32) * attended, axis=2)
    zero_heads = jnp.zeros((rows, HEADS, head_dim), jnp.float32)

    def back_block(grad_acc, block):
        key_blk, value_blk, seg_blk = block
        part_query, part_key, part_value = block_grads(
            query_heads,
            dctx_heads,
            lse_rows,
            delta_rows,
            seg_float,
            key_blk,
            value_blk,
            seg_blk,
            score_scale,
        )
        return (grad_acc + part_query, (part_key, part_value))

    grad_q, (key_parts, value_parts) = lax.scan(
        back_block, zero_heads, (key_blocks, value_blocks, seg_blocks)
    )
    grad_key_own, grad_value_own = (
        lax.psum_scatter(
            key_parts.reshape(total, width), ("ctx", "wsh"), scatter_dimension=0, tiled=True
        ),
        lax.psum_scatter(
            value_parts.reshape(total, width), ("ctx", "wsh"), scatter_dimension=0, tiled=True
        ),
    )
    grad_queries = grad_q.reshape(rows, width).astype(jnp.bfloat16)
    grad_keys = grad_key_own.astype(jnp.bfloat16)
    grad_values = grad_value_own.astype(jnp.bfloat16)
    grad_full_query = matmul_left_t(inputs, grad_queries)
    grad_bias_query = jnp.sum(grad_queries.astype(jnp.float32), axis=0)
    grad_full_key = matmul_left_t(inputs, grad_keys)
    grad_full_value = matmul_left_t(inputs, grad_values)
    grad_bias_value = jnp.sum(grad_values.astype(jnp.float32), axis=0)
    grad_input = (
        grad_res_one
        + matmul_right_t(grad_queries, full_query)
        + matmul_right_t(grad_keys, full_key)
        + matmul_right_t(grad_values, full_value)
    )
    (
        share_query,
        share_bias_query,
        share_key,
        share_value,
        share_bias_value,
        share_out,
        share_bias_out,
        share_gain_one,
        share_shift_one,
        share_in,
        share_bias_in,
        share_down,
        share_bias_down,
        share_gain_two,
        share_shift_two,
    ) = (
        lax.psum_scatter(
            grad_full_query.astype(jnp.bfloat16), "wsh", scatter_dimension=0, tiled=True
        ).astype(jnp.float32),
        lax.psum_scatter(
            grad_bias_query.astype(jnp.bfloat16), "wsh", scatter_dimension=0, tiled=True
        ).astype(jnp.float32),
        lax.psum_scatter(
            grad_full_key.astype(jnp.bfloat16), "wsh", scatter_dimension=0, tiled=True
        ).astype(jnp.float32),
        lax.psum_scatter(
            grad_full_value.astype(jnp.bfloat16), "wsh", scatter_dimension=0, tiled=True
        ).astype(jnp.float32),
        lax.psum_scatter(
            grad_bias_value.astype(jnp.bfloat16), "wsh", scatter_dimension=0, tiled=True
        ).astype(jnp.float32),
        lax.psum_scatter(
            grad_full_out.astype(jnp.bfloat16), "wsh", scatter_dimension=0, tiled=True
        ).astype(jnp.float32),
        lax.psum_scatter(
            grad_bias_out.astype(jnp.bfloat16), "wsh", scatter_dimension=0, tiled=True
        ).astype(jnp.float32),
        lax.psum_scatter(
            grad_gain_one.astype(jnp.bfloat16), "wsh", scatter_dimension=0, tiled=True
        ).astype(jnp.float32),
        lax.psum_scatter(
            grad_shift_one.astype(jnp.bfloat16), "wsh", scatter_dimension=0, tiled=True
        ).astype(jnp.float32),
        lax.psum_scatter(
            grad_full_in.astype(jnp.bfloat16), "wsh", scatter_dimension=0, tiled=True
        ).astype(jnp.float32),
        lax.psum_scatter(
            grad_bias_in.astype(jnp.bfloat16), "wsh", scatter_dimension=0, tiled=True
        ).astype(jnp.float32),
        lax.psum_scatter(
            grad_full_down.astype(jnp.bfloat16), "wsh", scatter_dimension=0, tiled=True
        ).astype(jnp.float32),
        lax.psum_scatter(
            grad_bias_down.astype(jnp.bfloat16), "wsh", scatter_dimension=0, tiled=True
        ).astype(jnp.float32),
        lax.psum_scatter(
            grad_gain_two.astype(jnp.bfloat16), "wsh", scatter_dimension=0, tiled=True
        ).astype(jnp.float32),
        lax.psum_scatter(
            grad_shift_two.astype(jnp.bfloat16), "wsh", scatter_dimension=0, tiled=True
        ).astype(jnp.float32),
    )
    summed = lax.psum(
        (
            share_query,
            share_bias_query,
            share_key,
            share_value,
            share_bias_value,
            share_out,
            share_bias_out,
            share_gain_one,
            share_shift_one,
            share_in,
            share_bias_in,
            share_down,
            share_bias_down,
            share_gain_two,
            share_shift_two,
        ),
        ("seq", "ctx"),
    )
    return (
        result.astype(jnp.bfloat16)[None],
        grad_input.astype(jnp.bfloat16)[None],
        summed[0],
        summed[1],
        summed[2],
        summed[3],
        summed[4],
        summed[5],
        summed[6],
        summed[7],
        summed[8],
        summed[9],
        summed[10],
        summed[11],
        summed[12],
        summed[13],
        summed[14],
    )


(DO_START, DO_PLANE, DO_CROSS, DO_CORE, DO_QKV_Z, DO_QKV_PLANE,
 DO_QKV_CORE, DO_FORWARD, DO_NEAR, DO_WEIGHT_GRAD, DO_CORE_ADD, DO_X1_SEND,
 DO_X1_FAR, DO_X1_OWN, DO_X2_ADD, DO_Z_SEND, DO_Z_ADD, DO_G_SEND,
 DO_G_FORWARD, DO_G_CORE, DO_VEC_CORE, DO_VEC_PLANE, DO_VEC_Z, DO_VEC_END,
 DO_LINE, DO_GRAD_PROJ, DO_B_CORE, DO_B_PLANE, DO_OWN_ROWS) = range(29)


MESH_ID = pl.DeviceIdType.MESH
LANES = 256
IDS = 16
BIG = float(2.0**99)
VMEM_LIMIT = 62 * 2**20


def remote(src, dst, send, recv, where):
    return pltpu.make_async_remote_copy(
        src_ref=src, dst_ref=dst, send_sem=send, recv_sem=recv, device_id=where, device_id_type=MESH_ID
    )


def nt(left, right):
    return lax.dot_general(left, right, (((1,), (1,)), ((), ())), preferred_element_type=jnp.float32)


def tn(left, right):
    return lax.dot_general(left, right, (((0,), (0,)), ((), ())), preferred_element_type=jnp.float32)


def nn(left, right):
    return jnp.dot(left, right, preferred_element_type=jnp.float32)


def greet(peers):
    barrier = pltpu.get_barrier_semaphore()
    for peer in peers:
        pl.semaphore_signal(barrier, inc=1, device_id=peer, device_id_type=MESH_ID)
    pl.semaphore_wait(barrier, len(peers))


def layer_kernel(
    dims,
    tokens, seg, w_q, w_k, w_v, b_q, b_v, b_o, gain_1, shift_1, b_i, b_d, gain_2, shift_2, cot, w_o, w_i, w_d,
    result, g_tok, gd, gi, go, gq, g_vec, g_b,
    toks, wcol, qx, kx, vv, att_t, lse, ctx, res, active, grad_branch, hidden_low, grad_inner, grad_attn, grad_vec,
    full_o, full_i, full_d, vecs, slope, segs, w_send, vt, scores, dv, ctx_send, ctx_recv, d_recv, dqkv, kv_recv, rx,
    bufs, deltas, vx, vc, vs, vz, bc, bs,
    tok_s, tok_r, sv_s, sv_r, wz_s, wz_r, wp_s, wp_r, kv_s, kv_r, cx_s, cx_r,
    fz_s, fz_r, fx_s, fx_r, fc_s, fc_r, loc,
    da_s, da_r, kb_s, kb_r, rx_s, rx_r, core_s, core_r, x1_s, x1_r, x2_s, x2_r, za_s, za_r, ga_s, ga_r, gc_s, gc_r,
    vp_s, vp_r, bp_s, bp_r,
):
    S, W, heads = dims["S"], dims["W"], dims["heads"]
    rows, width = tokens.shape
    f32, bf16 = jnp.float32, jnp.bfloat16
    group = width // W
    head_dim = group // heads
    block = rows * W
    total = 2 * block
    ff = w_i.shape[1]
    P = (full_d, full_d, full_i, full_i, full_o, w_send)
    G = (gd, gd, gi, gi, go, gq)
    CR, X1, X2, Z = bufs[:6], bufs[6:12], bufs[12:18], bufs[18:24]
    last = 5
    kt, dk, kv_send, px, dq_t = vt, scores, kx, active, att_t

    def run(name):
        for stage, part in dims[name]:
            stages[stage](part)

    s, c, z = lax.axis_index("seq"), lax.axis_index("ctx"), lax.axis_index("wsh")
    sib = (s, 1 - c, z)
    s1, s2, s3 = s ^ 1, s ^ 2, s ^ 3
    shifts = list(range(1, W))
    zz = [lax.rem(z + t, W) for t in shifts]
    barrier = pltpu.get_barrier_semaphore()
    peers = [sib] + [(p, c, z) for p in (s1, s2, s3)] + [(s, c, q) for q in zz]
    for peer in peers:
        pl.semaphore_signal(barrier, inc=1, device_id=peer, device_id_type=MESH_ID)
    toks[z] = tokens[...]
    segs[z] = seg[...].astype(jnp.float32)
    for ref, lo in zip((b_o, gain_1, shift_1, b_d, gain_2, shift_2, b_i), dims["cuts"]):
        vecs[z, :, lo : lo + ref.shape[0]] = ref[...].astype(jnp.float32).reshape(1, -1)

    for j in range(W):
        for m, ref in enumerate((w_q, w_k, w_v)):
            part = ref[:, j * group : (j + 1) * group]
            part = jnp.concatenate([part, jnp.zeros((group, LANES - group), part.dtype)], axis=1)
            w_send[j, :, m * LANES : (m + 1) * LANES] = part

    pl.semaphore_wait(barrier, len(peers))

    slab, wide = group // S, 3 * LANES // 2

    def col_at(ref, base, cc, ss):
        rows_at = pl.ds(pl.multiple_of(base + (0 if ss is None else ss * slab), 16), group if ss is None else slab)
        return ref.at[rows_at, pl.ds(pl.multiple_of(cc * wide, 128), wide)]

    def wz(q):
        return remote(col_at(w_send.at[q], 0, c, s), col_at(wcol, z * group, c, s), wz_s.at[q], wz_r.at[z], (s, c, q))

    def wz_in(q):
        here = col_at(wcol, q * group, c, s)
        return remote(here, here, wz_s.at[q], wz_r.at[q], (s, c, q))

    def wp(q, k):
        ref = col_at(wcol, q * group, c, s if k else None)
        return remote(ref, ref, wp_s.at[q, k], wp_r.at[q, k], (s ^ k, c, z) if k else sib)

    def wp_in(q, k):
        ref = col_at(wcol, q * group, c, s ^ k) if k else col_at(wcol, q * group, 1 - c, None)
        return remote(ref, ref, wp_s.at[q, k], wp_r.at[q, k], sib)

    def seg_out(q):
        return remote(segs.at[z], segs.at[z], sv_s.at[0, q], sv_r.at[0, z], (s, c, q))

    def seg_in(q):
        return remote(segs.at[q], segs.at[q], sv_s.at[0, q], sv_r.at[0, q], (s, c, q))

    def vec_out(q):
        return remote(vecs.at[z], vecs.at[z], sv_s.at[1, q], sv_r.at[1, z], (s, c, q))

    def vec_in(q):
        return remote(vecs.at[q], vecs.at[q], sv_s.at[1, q], sv_r.at[1, q], (s, c, q))

    def tok_copy(slot, step, lane):
        return remote(toks.at[slot], toks.at[slot], tok_s.at[lane, slot], tok_r.at[slot], (s, c, z + step))

    def cut_of(how, row, n, m, shard, whole):
        return dict(how=how, row=row, n=n, m=m, shard=shard, whole=whole)

    down = ff // W // 2
    cuts_o = cut_of(0, 0, group, width, w_o, full_o)
    cuts_i = [cut_of(1, u * (group // 2), group // 2, ff, w_i, full_i) for u in range(2)]
    cuts_d = [cut_of(2, u * down, down, width, w_d, full_d) for u in range(2)]
    parts = (cuts_o, *cuts_i, *cuts_d)

    def place(cut, cc, ss, half=None):
        n, m = cut["n"], cut["m"]
        if cut["how"] == 0:
            row, size = (0, n) if ss is None else (ss * (n // S), n // S)
            col, wide = cc * (m // 2), m // 2
            if half is not None:
                col, wide = col + (0 if half == 0 else 128), (128 if half == 0 else m // 2 - 128)
        elif cut["how"] == 1:
            row, size = 0, n
            col, wide = cc * (m // 2) + (0 if ss is None else ss * (m // 8)), m // 2 if ss is None else m // 8
            if half is not None:
                row, size = half * (n // 2), n // 2
        else:
            row, size = cc * (n // 2) + (0 if ss is None else ss * (n // 8)), n // 2 if ss is None else n // 8
            col, wide = 0, m
            if half is not None:
                col, wide = half * (m // 2), m // 2
        row = cut["row"] + row
        if not isinstance(row, int):
            row = pl.multiple_of(row, 16)
        if not isinstance(col, int):
            col = pl.multiple_of(col, 128)
        return pl.ds(row, size), pl.ds(col, wide)

    def rows_of(part, q, cc, ss, half=None):
        return parts[part]["whole"].at[q].at[place(parts[part], cc, ss, half)]

    def own_copy(w):
        shard, whole = ((w_o, full_o), (w_i, full_i), (w_d, full_d))[w]
        return pltpu.make_async_copy(shard, whole.at[z], loc.at[w])

    def fz(part, q):
        src = parts[part]["shard"].at[place(parts[part], c, s)]
        return remote(src, rows_of(part, z, c, s), fz_s.at[part, q], fz_r.at[part, z], (s, c, q))

    def fz_in(part, q):
        here = rows_of(part, q, c, s)
        return remote(here, here, fz_s.at[part, q], fz_r.at[part, q], (s, c, q))

    def fx(part, q, kind):
        if kind < 2:
            ref, to = rows_of(part, q, c, s), (s1, s2)[kind]
        else:
            ref, to = rows_of(part, q, c, (s1, s2)[kind - 2], kind - 2), (s2, s1)[kind - 2]
        return remote(ref, ref, fx_s.at[part, q, kind], fx_r.at[part, q, kind], (to, c, z))

    def fx_in(part, q, kind):
        if kind < 2:
            ref = rows_of(part, q, c, (s1, s2)[kind])
        else:
            ref = rows_of(part, q, c, s3, kind - 2)
        return remote(ref, ref, fx_s.at[part, q, kind], fx_r.at[part, q, kind], (s1, c, z))

    def fc(part, q):
        ref = rows_of(part, q, c, None)
        return remote(ref, ref, fc_s.at[part, q], fc_r.at[part, q], sib)

    def fc_in(part, q):
        ref = rows_of(part, q, 1 - c, None)
        return remote(ref, ref, fc_s.at[part, q], fc_r.at[part, q], sib)

    def w_start(part):
        for q in zz:
            fz(part, q).start()

    def w_plane(part):
        for q in zz:
            fz_in(part, q).wait_recv()
            fx(part, q, 0).start()
            fx(part, q, 1).start()

    def w_cross(part):
        for q in zz:
            fx_in(part, q, 0).wait_recv()
            fx(part, q, 2).start()
            fx_in(part, q, 1).wait_recv()
            fx(part, q, 3).start()

    def w_core(part):
        for q in zz:
            fx_in(part, q, 2).wait_recv()
            fx_in(part, q, 3).wait_recv()
            fc(part, q).start()

    def w_ready(w):
        own_copy(w).wait()
        for part in ((0,), (1, 2), (3, 4))[w]:
            for q in zz:
                fc_in(part, q).wait_recv()

    stages = {DO_PLANE: w_plane, DO_CROSS: w_cross, DO_CORE: w_core, DO_START: w_start}

    def w_finish(part):
        for q in zz:
            fz(part, q).wait_send()
            for kind in range(4):
                fx(part, q, kind).wait_send()
            fc(part, q).wait_send()


    for q in zz:
        wz(q).start()
        seg_out(q).start()
    for w in range(3):
        own_copy(w).start()
    for part in dims["first"]:
        w_start(part)
    @pl.when(z + 1 < W)
    def _():
        tok_copy(z, 1, 0).start()

    @pl.when(z > 0)
    def _():
        tok_copy(z, -1, 1).start()

    for q in zz:
        vec_out(q).start()

    lane = lax.broadcasted_iota(jnp.int32, (1, LANES), 1)
    spot = lax.broadcasted_iota(jnp.int32, (IDS, LANES), 1) - lax.broadcasted_iota(jnp.int32, (IDS, LANES), 0)
    lanes_in = lax.broadcasted_iota(jnp.int32, (IDS, LANES), 1)
    in_ext = (lanes_in >= group) & (lanes_in < group + IDS)
    put_q = jnp.where(spot == group, 1.0, 0.0).astype(jnp.bfloat16)
    put_k = jnp.where(in_ext & (spot != group), -BIG, 0.0).astype(jnp.bfloat16)
    pad = jnp.zeros((1, LANES - group), jnp.float32)
    bias_q = jnp.concatenate([b_q[...].astype(jnp.float32).reshape(1, -1), pad], axis=1)
    bias_v = jnp.concatenate([b_v[...].astype(jnp.float32).reshape(1, -1), pad], axis=1)
    ids = lax.broadcasted_iota(jnp.int32, (IDS, rows), 0).astype(jnp.float32)

    def k_rows(owner, slot):
        return pl.ds(pl.multiple_of(owner * block + slot * rows, rows), rows)

    def kv(slot, which):
        ref = (kx, vv)[which].at[k_rows(c, slot), :]
        return remote(ref, ref, kv_s.at[which, slot], kv_r.at[which, slot], sib)

    def kv_in(slot, which):
        ref = (kx, vv)[which].at[k_rows(1 - c, slot), :]
        return remote(ref, ref, kv_s.at[which, slot], kv_r.at[which, slot], sib)

    def project(slot):
        made = nn(toks[slot], wcol[...])
        hot = jnp.where(jnp.broadcast_to(segs[slot], (IDS, rows)) == ids, 1.0, 0.0).astype(jnp.bfloat16)
        q_low = (made[:, :LANES] + bias_q).astype(jnp.bfloat16).astype(jnp.float32) * dims["scale"]
        ext_q = tn(hot, put_q)
        for h in range(heads):
            mine = (lane >= h * head_dim) & (lane < (h + 1) * head_dim)
            qx[pl.ds(pl.multiple_of(h * block + slot * rows, rows), rows), :] = (
                jnp.where(mine, q_low, 0.0) + ext_q
            ).astype(jnp.bfloat16)
        kx[k_rows(c, slot), :] = (made[:, LANES : 2 * LANES] + tn(hot, put_k)).astype(jnp.bfloat16)
        vv[k_rows(c, slot), :] = (made[:, 2 * LANES :] + bias_v).astype(jnp.bfloat16)
        kv(slot, 0).start()
        kv(slot, 1).start()

    def qkv_z(part):
        for q in zz:
            wz_in(q).wait_recv()
            for k in (1, 2, 3):
                wp(q, k).start()

    def qkv_plane(part):
        for q in zz:
            for k in (1, 2, 3):
                wp_in(q, k).wait_recv()
            wp(q, 0).start()
        wcol[pl.ds(pl.multiple_of(z * group, 16), group), :] = w_send[z]

    def qkv_core(part):
        for q in zz:
            wp_in(q, 0).wait_recv()
            seg_in(q).wait_recv()

    def forward(far):
        @pl.when(z >= far)
        def _():
            tok_copy(z - far, 1, 0).wait_recv()

            @pl.when(z + 1 < W)
            def _():
                tok_copy(z - far, 1, 0).start()

        @pl.when(z + far < W)
        def _():
            tok_copy(z + far, 1, 0).wait_recv()

            @pl.when(z > 0)
            def _():
                tok_copy(z + far, -1, 1).start()

    def near(far):
        def side(k, carry):
            slot = jnp.where(k == 0, z - far, z + far)

            @pl.when((slot >= 0) & (slot < W))
            def _():
                project(slot)

            return carry

        if far == 0:
            project(z)
        else:
            lax.fori_loop(0, 2, side, 0)

    stages.update({
        DO_QKV_Z: qkv_z, DO_QKV_PLANE: qkv_plane, DO_QKV_CORE: qkv_core, DO_FORWARD: forward, DO_NEAR: near,
    })
    for name, part in dims["seq_t"]:
        stages[name](part)
    for j in range(W):
        kv_in(j, 0).wait_recv()
        kv_in(j, 1).wait_recv()
    vt[...] = vv[...].astype(jnp.float32).T.astype(jnp.bfloat16)

    chunk = dims["chunk"]
    n_chunks = total // chunk

    def cx(b):
        return remote(ctx_send.at[b], ctx_recv.at[z], cx_s.at[b], cx_r.at[z], (s, c, b))

    def cx_in(b):
        return remote(ctx_send.at[b], ctx_recv.at[b], cx_s.at[b], cx_r.at[b], (s, c, b))

    def attend(step, carry):
        i = lax.div(step, heads)
        h = lax.rem(step, heads)
        b = lax.rem(z + 1 + i, W)
        query = qx[pl.ds(pl.multiple_of(h * block + b * rows, rows), rows), :]
        top = None
        for n in range(n_chunks):
            got = nt(kx[n * chunk : (n + 1) * chunk, :], query)
            scores[n * chunk : (n + 1) * chunk, :] = got
            high = jnp.max(got, axis=0, keepdims=True)
            top = high if top is None else jnp.maximum(top, high)
        mass = None
        out = None
        here = pl.ds(pl.multiple_of(h * head_dim, head_dim), head_dim)
        for n in range(n_chunks):
            raised = jnp.exp(scores[n * chunk : (n + 1) * chunk, :] - top)
            add = jnp.sum(raised, axis=0, keepdims=True)
            mass = add if mass is None else mass + add
            piece_out = nn(vt[here, n * chunk : (n + 1) * chunk], raised.astype(jnp.bfloat16))
            out = piece_out if out is None else out + piece_out
        att_t[here, pl.ds(pl.multiple_of(b * rows, rows), rows)] = out / mass
        lse[h, :, pl.ds(pl.multiple_of(b * rows, rows), rows)] = top + jnp.log(mass)

        @pl.when(h == heads - 1)
        def _():
            done = att_t[:, pl.ds(pl.multiple_of(b * rows, rows), rows)]
            ctx_send[b] = done.T.astype(jnp.bfloat16)

            @pl.when(i < W - 1)
            def _():
                cx(b).start()

            @pl.when(i == W - 1)
            def _():
                ctx_recv[b] = ctx_send[b]

        for when, name, part in dims["moves_a"]:
            @pl.when(step == when)
            def _():
                stages[name](part)

        return carry

    lax.fori_loop(0, W * heads, attend, 0)
    for q in zz:
        wz(q).wait_send()
    for j in range(W):
        kv(j, 0).wait_send()
        kv(j, 1).wait_send()
    for q in zz:
        cx_in(q).wait_recv()
    for j in range(W):
        ctx[:, j * group : (j + 1) * group] = ctx_recv[j]
    for q in zz:
        vec_in(q).wait_recv()

    def vcore():
        return remote(vc.at[c], vc.at[c], vp_s.at[0], vp_r.at[0], sib)

    def vplane(k):
        return remote(vs.at[s], vs.at[s], vp_s.at[k], vp_r.at[k], (s ^ k, c, z))

    def vz_out(q, t):
        return remote(vx.at[q], vz.at[z], vp_s.at[4 + t], vp_r.at[4 + z], (s, c, q))

    def vz_in(q, t):
        return remote(vx.at[q], vz.at[q], vp_s.at[4 + t], vp_r.at[4 + q], (s, c, q))

    def vec_core():
        vc[c] = grad_vec[...]
        vcore().start()

    def vec_plane():
        vcore().wait_recv()
        vs[s] = vc[0] + vc[1]
        for k in (1, 2, 3):
            vplane(k).start()

    def vec_z():
        for k in (1, 2, 3):
            vplane(k).wait_recv()
        vx[...] = (vs[0] + vs[1]) + (vs[2] + vs[3])
        vz[z] = vx[z]
        for t, q in enumerate(zz):
            vz_out(q, t).start()

    def vec_end():
        for t, q in enumerate(zz):
            vz_in(q, t).wait_recv()
        acc = vz[0]
        for j in range(1, W):
            acc = acc + vz[j]
        g_vec[...] = acc
        vcore().wait_send()
        for k in (1, 2, 3):
            vplane(k).wait_send()
        for t, q in enumerate(zz):
            vz_out(q, t).wait_send()

    kinds = (*cuts_d, *cuts_i, cuts_o, cuts_o)

    def view(ref, a, cc, ss, half=None):
        return ref.at[(slice(None),) + place(kinds[a], cc, ss, half)]

    def within(a, half):
        n, m = kinds[a]["n"], kinds[a]["m"]
        if kinds[a]["how"] == 0:
            return (slice(0, n // S), slice(0, 128) if half == 0 else slice(128, m // 2))
        if kinds[a]["how"] == 1:
            return (slice(half * (n // 2), (half + 1) * (n // 2)), slice(0, m // 8))
        return (slice(0, n // 8), slice(half * (m // 2), (half + 1) * (m // 2)))

    def core_move(a):
        return remote(view(P[a], a, 1 - c, None), CR[a], core_s.at[a], core_r.at[a], sib)

    def add_into(a, cc, ss, half, more):
        at = place(kinds[a], cc, ss, half)
        for j in range(W):
            P[a][(j,) + at] = (P[a][(j,) + at].astype(f32) + more(j).astype(f32)).astype(bf16)

    def core_add(a):
        core_move(a).wait_recv()
        add_into(a, c, None, None, lambda j: CR[a][j])

    def x1(a, half, slot):
        to = (s1, s2)[half]
        at = ((s1, s3) if half == 0 else (s2, s3))[slot]
        k = half * 2 + slot
        return remote(view(P[a], a, c, at, half), X1[a].at[(slot, slice(None)) + within(a, half)], x1_s.at[a, k],
                      x1_r.at[a, k], (to, c, z))

    def x1_send(a):
        for slot in (1, 0):
            for half in range(2):
                x1(a, half, slot).start()

    def x1_far(a):
        for half in range(2):
            x1(a, half, 1).wait_recv()
            add_into(a, c, (s2, s1)[half], half, lambda j: X1[a][(1, j) + within(a, half)])
            x2(a, half).start()

    def x1_own(a):
        for half in range(2):
            x1(a, half, 0).wait_recv()
            add_into(a, c, s, half, lambda j: X1[a][(0, j) + within(a, half)])

    def x2(a, half):
        to = (s2, s1)[half]
        return remote(view(P[a], a, c, to, half), X2[a].at[(slice(None),) + within(a, half)], x2_s.at[a, half],
                      x2_r.at[a, half], (to, c, z))

    def x2_add(a):
        for half in range(2):
            x2(a, half).wait_recv()
            add_into(a, c, s, half, lambda j: X2[a][(j,) + within(a, half)])

    def own_piece(a, q):
        return P[a].at[q].at[place(kinds[a], c, s)]

    def za(a, q, t):
        return remote(own_piece(a, q), Z[a].at[z], za_s.at[a, t], za_r.at[a, z], (s, c, q))

    def za_in(a, q, t):
        return remote(own_piece(a, q), Z[a].at[q], za_s.at[a, t], za_r.at[a, q], (s, c, q))

    def z_send(a):
        for t, q in enumerate(zz):
            za(a, q, t).start()
        Z[a][z] = own_piece(a, z)[...]

    def z_add(a):
        for t, q in enumerate(zz):
            za_in(a, q, t).wait_recv()
        at = place(kinds[a], c, s)
        if a == last:
            for j in range(W):
                G[a][(j,) + at] = Z[a][j]
        else:
            acc = Z[a][0].astype(f32)
            for j in range(1, W):
                acc = acc + Z[a][j].astype(f32)
            G[a][at] = acc.astype(bf16)

    def g_view(a, cc, ss, half=None):
        at = place(kinds[a], cc, ss, half)
        return G[a].at[((slice(None),) + at) if a == last else at]

    def ga(a, kind):
        if kind < 2:
            ref, to = g_view(a, c, s), (s1, s2)[kind]
        else:
            ref, to = g_view(a, c, (s1, s2)[kind - 2], kind - 2), (s2, s1)[kind - 2]
        return remote(ref, ref, ga_s.at[a, kind], ga_r.at[a, kind], (to, c, z))

    def ga_in(a, kind):
        ref = g_view(a, c, (s1, s2)[kind]) if kind < 2 else g_view(a, c, s3, kind - 2)
        return remote(ref, ref, ga_s.at[a, kind], ga_r.at[a, kind], (s1, c, z))

    def gc(a):
        ref = g_view(a, c, None)
        return remote(ref, ref, gc_s.at[a], gc_r.at[a], sib)

    def gc_in(a):
        ref = g_view(a, 1 - c, None)
        return remote(ref, ref, gc_s.at[a], gc_r.at[a], sib)

    def g_send(a):
        ga(a, 0).start()
        ga(a, 1).start()

    def g_forward(a):
        for kind in range(2):
            ga_in(a, kind).wait_recv()
            ga(a, 2 + kind).start()

    def g_core(a):
        for kind in range(2):
            ga_in(a, 2 + kind).wait_recv()
        gc(a).start()

    def drain(a):
        core_move(a).wait_send()
        for half in range(2):
            x1(a, half, 0).wait_send()
            x1(a, half, 1).wait_send()
            x2(a, half).wait_send()
        for t, q in enumerate(zz):
            za(a, q, t).wait_send()
        for kind in range(4):
            ga(a, kind).wait_send()
        gc(a).wait_send()

    def weight_grad(a):
        if a < 2:
            w_finish(3 + a)
            lanes = slice(a * down, (a + 1) * down)
            for k in range(W):
                full_d[k, lanes, :] = tn(active[k, :, lanes], grad_branch[...]).astype(bf16)
            core_move(a).start()
        elif a == 2:
            w_finish(1)
            w_finish(2)
            for k in range(W):
                made = tn(hidden_low[...], grad_inner[k]).astype(bf16)
                for j in range(W):
                    full_i[j, :, k * width : (k + 1) * width] = made[j * group : (j + 1) * group]
            core_move(2).start()
            core_move(3).start()
        else:
            w_finish(0)
            made = tn(ctx[...], grad_attn[...]).astype(bf16)
            for j in range(W):
                full_o[j] = made[j * group : (j + 1) * group]
            core_move(4).start()

    stages.update({
        DO_CORE_ADD: core_add, DO_X1_SEND: x1_send, DO_X1_FAR: x1_far, DO_X1_OWN: x1_own, DO_X2_ADD: x2_add,
        DO_Z_SEND: z_send, DO_Z_ADD: z_add, DO_G_SEND: g_send, DO_G_FORWARD: g_forward, DO_G_CORE: g_core,
        DO_WEIGHT_GRAD: weight_grad, DO_VEC_CORE: lambda a: vec_core(), DO_VEC_PLANE: lambda a: vec_plane(),
        DO_VEC_Z: lambda a: vec_z(), DO_VEC_END: lambda a: vec_end(),
    })

    cuts = dims["cuts"]

    def vec_of(k):
        n = (b_o, gain_1, shift_1, b_d, gain_2, shift_2, b_i)[k].shape[0]
        return jnp.concatenate([vecs[j, :, cuts[k] : cuts[k] + n] for j in range(W)], axis=1)

    def norm(values, gain, shift):
        centred = values - jnp.mean(values, axis=-1, keepdims=True)
        inverse = lax.rsqrt(jnp.mean(centred * centred, axis=-1, keepdims=True) + norm_eps)
        normed = centred * inverse
        return normed * gain + shift, normed, inverse

    def norm_back(grad, normed, inverse, gain):
        scaled = grad * gain
        return inverse * (
            scaled
            - jnp.mean(scaled, axis=-1, keepdims=True)
            - normed * jnp.mean(scaled * normed, axis=-1, keepdims=True)
        )

    def put_vec(k, values):
        n = values.shape[1] // W
        for j in range(W):
            grad_vec[j, :, cuts[k] : cuts[k] + n] = values[:, j * n : (j + 1) * n]

    def total_of(values):
        return jnp.sum(values, axis=0, keepdims=True)

    gain_a, gain_b = vec_of(1), vec_of(4)
    w_ready(0)
    summed = tokens[...].astype(f32) + (nn(ctx[...], full_o[...].reshape(width, width)) + vec_of(0))
    hidden, normed_1, inverse_1 = norm(summed, gain_a, vec_of(2))
    hidden_low[...] = hidden.astype(bf16)
    run("seq_f0")
    w_ready(1)
    spans = [slice(k * width, (k + 1) * width) for k in range(W)]
    bias_in = vec_of(6)
    for k, span in enumerate(spans):
        inner = nn(hidden_low[...], full_i[:, :, span].reshape(width, width)) + bias_in[:, span]
        cdf = 0.5 * (1.0 + lax.erf(inner * (0.5**0.5)))
        active[k] = (inner * cdf).astype(bf16)
        slope[k] = (cdf + inner * (jnp.exp(-0.5 * inner * inner) * dims["density"])).astype(slope.dtype)
    run("seq_f1")
    w_ready(2)
    branch = vec_of(3)
    for k in range(W):
        branch = branch + nn(active[k], full_d[k])
    out, normed_2, inverse_2 = norm(hidden + branch, gain_b, vec_of(5))
    result[...] = out.astype(bf16)
    grad_out = cot[0].astype(f32)
    put_vec(4, total_of(grad_out * normed_2))
    put_vec(5, total_of(grad_out))
    grad_res = norm_back(grad_out, normed_2, inverse_2, gain_b)
    grad_branch[...] = grad_res.astype(bf16)
    put_vec(3, total_of(grad_branch[...].astype(f32)))
    for k in range(W):
        low = (nt(grad_branch[...], full_d[k]) * slope[k].astype(f32)).astype(bf16)
        grad_inner[k] = low
        grad_vec[k, :, cuts[6] : cuts[6] + width] = total_of(low.astype(f32))
    run("seq_f2")
    grad_hidden = grad_res
    for k, span in enumerate(spans):
        grad_hidden = grad_hidden + nt(grad_inner[k], full_i[:, :, span].reshape(width, width))
    put_vec(1, total_of(grad_hidden * normed_1))
    put_vec(2, total_of(grad_hidden))
    grad_first = norm_back(grad_hidden, normed_1, inverse_1, gain_a)
    res[...] = grad_first
    grad_attn[...] = grad_first.astype(bf16)
    put_vec(0, total_of(grad_attn[...].astype(f32)))
    grad_ctx = nt(grad_attn[...], full_o[...].reshape(width, width)).astype(bf16)
    for q in zz:
        cx(q).wait_send()
    d_send = ctx_send
    for j in range(W):
        d_send[j] = grad_ctx[:, j * group : (j + 1) * group]

    def da(q):
        return remote(d_send.at[q], d_recv.at[z], da_s.at[q], da_r.at[z], (s, c, q))

    def da_in(q):
        return remote(d_send.at[q], d_recv.at[q], da_s.at[q], da_r.at[q], (s, c, q))

    for q in zz:
        da(q).start()
    d_recv[z] = d_send[z]

    kt[...] = kx[...].astype(f32).T.astype(bf16)
    dk[...] = jnp.zeros_like(dk)
    dv[...] = jnp.zeros_like(dv)
    run("seq_b")

    def attend_back(step, carry):
        i = lax.div(step, heads)
        h = lax.rem(step, heads)
        b = lax.rem(z + i, W)

        @pl.when((h == 0) & (i > 0))
        def _():
            da_in(b).wait_recv()

        at = pl.ds(pl.multiple_of(b * rows, rows), rows)
        here = pl.ds(pl.multiple_of(h * head_dim, head_dim), head_dim)
        got = d_recv[b].astype(f32)
        got = jnp.concatenate([got, jnp.zeros((rows, LANES - group), f32)], axis=1)
        mask = (lane >= h * head_dim) & (lane < (h + 1) * head_dim)
        grad = jnp.where(mask, got, 0.0).astype(bf16)

        @pl.when(h == 0)
        def _():
            both = got.T[:group] * att_t[:, at]
            for k in range(heads):
                deltas[k] = jnp.sum(both[k * head_dim : (k + 1) * head_dim], axis=0, keepdims=True)

        delta = deltas[h]
        query = qx[pl.ds(pl.multiple_of(h * block + b * rows, rows), rows), :]
        log_mass = lse[h, :, at]
        acc = None
        for n in range(n_chunks):
            span = slice(n * chunk, (n + 1) * chunk)
            weights = jnp.exp(nt(kx[span, :], query) - log_mass)
            grad_weights = nt(vv[span, :], grad)
            grad_scores = (weights * (grad_weights - delta)).astype(bf16)
            dv[span, :] += nn(weights.astype(bf16), grad)
            dk[span, :] += nn(grad_scores, query)
            add = nn(kt[here, span], grad_scores)
            acc = add if acc is None else acc + add
        dq_t[here, at] = acc * dims["scale"]

        for when, name, a in dims["moves_b"]:
            @pl.when(step == when)
            def _():
                stages[name](a)

        return carry

    lax.fori_loop(0, W * heads, attend_back, 0)

    def kv_move():
        return remote(kv_send, kv_recv, kb_s.at[0], kb_r.at[0], sib)

    other = pl.ds(pl.multiple_of((1 - c) * block, block), block)
    own = pl.ds(pl.multiple_of(c * block, block), block)
    kv_send[:block] = dk[other, :].astype(bf16)
    kv_send[block:] = dv[other, :].astype(bf16)
    kv_move().start()
    run("seq_k")
    pad = jnp.zeros((block, LANES - group), bf16)
    dqkv[:, :LANES] = jnp.concatenate([dq_t[...].T.astype(bf16), pad], axis=1)
    kv_move().wait_recv()
    keep = lane < group
    for m, ref in ((0, dk), (1, dv)):
        whole = ref[own, :] + kv_recv[m * block : (m + 1) * block].astype(f32)
        dqkv[:, (m + 1) * LANES : (m + 2) * LANES] = jnp.where(keep, whole, 0.0).astype(bf16)

    def rx_out(d, step, lane_):
        slot = jnp.where((lane_ == 1) & (d == z - 1 if step < 0 else d == z), W, d)
        return remote(px.at[d], rx.at[slot], rx_s.at[d], rx_r.at[slot], (s, c, z + step))

    def rx_in(slot):
        return remote(px.at[0], rx.at[slot], rx_s.at[0], rx_r.at[slot], (s, c, z))

    def make(d):
        at = pl.ds(pl.multiple_of(d * rows, rows), rows)
        return nt(dqkv[at, :], wcol[...])

    def line(k):
        far = W - 1 - k // 2
        right = jnp.where(z < W // 2, k % 2 == 0, k % 2 == 1)
        d = jnp.where(right, far, W - 1 - far)

        @pl.when(right & (d > z))
        def _():
            px[d] = make(d).astype(bf16)

            @pl.when(z > 0)
            def _():
                rx_in(d).wait_recv()
                px[d] = (px[d].astype(f32) + rx[d].astype(f32)).astype(bf16)

            rx_out(d, 1, 0).start()

        @pl.when(jnp.logical_not(right) & (d < z))
        def _():
            px[d] = make(d).astype(bf16)

            @pl.when(z < W - 1)
            def _():
                rx_in(d).wait_recv()
                px[d] = (px[d].astype(f32) + rx[d].astype(f32)).astype(bf16)

            rx_out(d, -1, 1).start()

    def grad_proj(part):
        made = None
        for j in range(W):
            add = tn(toks[j], dqkv[j * rows : (j + 1) * rows, :])
            made = add if made is None else made + add
        made = made.astype(bf16)
        for j in range(W):
            w_send[j] = made[j * group : (j + 1) * group]
        core_move(last).start()

    def bcore():
        return remote(bc.at[c], bc.at[c], bp_s.at[0], bp_r.at[0], sib)

    def bplane(k):
        return remote(bs.at[s], bs.at[s], bp_s.at[k], bp_r.at[k], (s ^ k, c, z))

    def b_core(part):
        sums = nn(jnp.ones((8, block), bf16), dqkv[...])[0:1]
        bc[c] = jnp.concatenate([sums[:, :LANES], sums[:, 2 * LANES :]], axis=1)
        bcore().start()

    def b_plane(part):
        bcore().wait_recv()
        bs[s] = bc[0] + bc[1]
        for k in (1, 2, 3):
            bplane(k).start()

    def own_rows(part):
        res[...] += make(z)

    stages.update({
        DO_GRAD_PROJ: grad_proj, DO_LINE: line, DO_B_CORE: b_core, DO_B_PLANE: b_plane, DO_OWN_ROWS: own_rows,
    })
    run("seq_l")

    @pl.when(z > 0)
    def _():
        rx_in(z).wait_recv()
        res[...] += rx[z].astype(f32)

    @pl.when(z < W - 1)
    def _():
        rx_in(W).wait_recv()
        res[...] += rx[W].astype(f32)

    g_tok[...] = res[...].astype(bf16)
    run("seq_g")
    for k in (1, 2, 3):
        bplane(k).wait_recv()
    tot = (bs[0] + bs[1]) + (bs[2] + bs[3])
    g_b[...] = tot
    bcore().wait_send()
    for k in (1, 2, 3):
        bplane(k).wait_send()
    kv_move().wait_send()
    for q in zz:
        da(q).wait_send()
    for j in range(W):
        @pl.when(j > z)
        def _():
            rx_out(j, 1, 0).wait_send()

        @pl.when(j < z)
        def _():
            rx_out(j, -1, 1).wait_send()

    for a in range(6):
        gc_in(a).wait_recv()
        drain(a)


    @pl.when(z + 1 < W)
    def _():
        for j in range(W):
            @pl.when(j <= z)
            def _():
                tok_copy(j, 1, 0).wait_send()

    @pl.when(z > 0)
    def _():
        for j in range(W):
            @pl.when(j >= z)
            def _():
                tok_copy(j, -1, 1).wait_send()

    for q in zz:
        seg_out(q).wait_send()
        vec_out(q).wait_send()
        for k in range(4):
            wp(q, k).wait_send()


def layer_call(dims, *operands):
    S, W, heads = dims["S"], dims["W"], dims["heads"]
    tokens, w_i = operands[0], operands[-2]
    rows, width = tokens.shape
    group = width // W
    block = rows * W
    total = 2 * block
    ff = w_i.shape[1]
    f32, bf16 = jnp.float32, jnp.bfloat16
    vm = pl.BlockSpec(memory_space=pltpu.VMEM)
    hb = pl.BlockSpec(memory_space=pl.ANY)
    dma = pltpu.SemaphoreType.DMA
    shape = jax.ShapeDtypeStruct
    vmem = pltpu.VMEM
    n_vec = dims["n_vec"]
    n_d, n_i = ff // W // 2, group // 2
    halves = ((n_d // 2, width),) * 2 + ((n_i, ff // 2),) * 2 + ((group, width // 2),) * 2
    pieces = ((n_d // 8, width),) * 2 + ((n_i, ff // 8),) * 2 + ((group // S, width // 2),) * 2
    return pl.pallas_call(
        partial(layer_kernel, dims),
        name="layer",
        out_shape=(
            shape((rows, width), bf16),
            shape((rows, width), bf16),
            shape((ff // W, width), bf16),
            shape((group, ff), bf16),
            shape((group, width), bf16),
            shape((W, group, 3 * LANES), bf16),
            shape((1, n_vec), f32),
            shape((1, 2 * LANES), f32),
        ),
        in_specs=[vm] * 15 + [hb] * 3,
        out_specs=tuple([vm] * 8),
        scratch_shapes=[
            vmem((W, rows, width), bf16),
            vmem((width, 3 * LANES), bf16),
            vmem((heads * block, LANES), bf16),
            vmem((total, LANES), bf16),
            vmem((total, LANES), bf16),
            vmem((group, block), f32),
            vmem((heads, 1, block), f32),
            vmem((rows, width), bf16),
            vmem((rows, width), f32),
            vmem((W, rows, width), bf16),
            vmem((rows, width), bf16),
            vmem((rows, width), bf16),
            vmem((W, rows, width), bf16),
            vmem((rows, width), bf16),
            vmem((W, 1, n_vec), f32),
            vmem((W, group, width), bf16),
            vmem((W, group, ff), bf16),
            vmem((W, ff // W, width), bf16),
            vmem((W, 1, n_vec), f32),
            vmem((W, rows, width), dims["slope"]),
            vmem((W, 1, rows), f32),
            vmem((W, group, 3 * LANES), bf16),
            vmem((LANES, total), bf16),
            vmem((total, rows), f32),
            vmem((total, rows), f32),
            vmem((W, rows, group), bf16),
            vmem((W, rows, group), bf16),
            vmem((W, rows, group), bf16),
            vmem((block, 3 * LANES), bf16),
            vmem((2 * block, LANES), bf16),
            vmem((W + 1, rows, width), bf16),
            [vmem((W,) + h, bf16) for h in halves]
            + [vmem((2, W) + p, bf16) for p in pieces]
            + [vmem((W,) + p, bf16) for p in pieces] * 2,
            vmem((heads, 1, rows), f32),
            vmem((W, 1, n_vec), f32),
            vmem((2, W, 1, n_vec), f32),
            vmem((S, W, 1, n_vec), f32),
            vmem((W, 1, n_vec), f32),
            vmem((2, 1, 2 * LANES), f32),
            vmem((S, 1, 2 * LANES), f32),
            dma((2, W)), dma((W,)), dma((2, W)), dma((2, W)), dma((W,)), dma((W,)),
            dma((W, 4)), dma((W, 4)), dma((2, W)), dma((2, W)), dma((W,)), dma((W,)),
            dma((5, W)), dma((5, W)), dma((5, W, 4)), dma((5, W, 4)), dma((5, W)), dma((5, W)),
            dma((3,)),
            dma((W,)), dma((W,)), dma((1,)), dma((1,)), dma((W,)), dma((W + 1,)),
            dma((6,)), dma((6,)), dma((6, 4)), dma((6, 4)), dma((6, 2)), dma((6, 2)),
            dma((6, W)), dma((6, W)), dma((6, 4)), dma((6, 4)), dma((6,)), dma((6,)),
            dma((4 + W,)), dma((4 + W,)), dma((4,)), dma((4,)),
        ],
        compiler_params=pltpu.CompilerParams(
            collective_id=1, has_side_effects=True, vmem_limit_bytes=VMEM_LIMIT
        ),
    )(*operands)


def finish_kernel(dims, result, g_tok, gd, gi, go, gq, vec, g_b,
                  o_res, o_tok, o_q, o_bq, o_k, o_v, o_bv, o_o, o_s0, o_s1, o_s2, o_i, o_s3, o_d, o_s4, o_s5, o_s6):
    f32 = jnp.float32
    W = dims["W"]
    group = o_bq.shape[0]
    o_res[0] = result[...]
    o_tok[0] = g_tok[...]
    o_d[...] = gd[...].astype(f32)
    o_i[...] = gi[...].astype(f32)
    o_o[...] = go[...].astype(f32)
    for j in range(W):
        for m, ref in enumerate((o_q, o_k, o_v)):
            ref[:, j * group : (j + 1) * group] = gq[j, :, m * LANES : m * LANES + group].astype(f32)
    o_bq[...] = g_b[0, :group]
    o_bv[...] = g_b[0, LANES : LANES + group]
    for ref, lo in zip((o_s0, o_s1, o_s2, o_s4, o_s5, o_s6, o_s3), dims["cuts"]):
        ref[...] = vec[0, lo : lo + ref.shape[0]]


def finish_call(dims, result, g_tok, gd, gi, go, gq, vec, g_b):
    f32, bf16 = jnp.float32, jnp.bfloat16
    W, steps = dims["W"], 4
    rows, width = result.shape
    group = width // W
    ff = gi.shape[1]
    down = gd.shape[0]
    shape = jax.ShapeDtypeStruct
    small, mat = shape((group,), f32), shape((group, width), f32)

    def cut(n, m):
        return pl.BlockSpec((n // steps, m), lambda k: (k, 0))

    def deep(d, n, m):
        return pl.BlockSpec((d, n // steps, m), lambda k: (0, k, 0))

    def flat(n):
        return pl.BlockSpec((n,), lambda k: (0,))

    def whole(a):
        return pl.BlockSpec(a.shape, lambda k: (0, 0))

    one, sheet = flat(group), cut(group, width)
    return pl.pallas_call(
        partial(finish_kernel, dims),
        name="finish",
        grid=(steps,),
        out_shape=(shape((1, rows, width), bf16), shape((1, rows, width), bf16), mat, small, mat, mat, small, mat,
                   small, small, small, shape((group, ff), f32), shape((ff // W,), f32), shape((down, width), f32),
                   small, small, small),
        in_specs=[cut(rows, width), cut(rows, width), cut(down, width), cut(group, ff), sheet,
                  deep(W, group, gq.shape[2]), whole(vec), whole(g_b)],
        out_specs=(deep(1, rows, width), deep(1, rows, width), sheet, one, sheet, sheet, one, sheet, one, one, one,
                   cut(group, ff), flat(ff // W), cut(down, width), one, one, one),
        compiler_params=pltpu.CompilerParams(vmem_limit_bytes=VMEM_LIMIT),
    )(result, g_tok, gd, gi, go, gq, vec, g_b)


def fast_device(dims, tokens, segment_ids, w_query, b_query, w_key, w_value, b_value, w_out, b_out, gain_attn,
                shift_attn, w_in, b_in, w_down, b_down, gain_ffn, shift_ffn, cotangent):
    made = layer_call(dims, tokens[0], segment_ids, w_query, w_key, w_value, b_query, b_value, b_out, gain_attn, shift_attn,
                      b_in, b_down, gain_ffn, shift_ffn, cotangent, w_out, w_in, w_down)
    return finish_call(dims, *made)


def plan(mesh):
    return dict(
        S=mesh.shape["seq"], W=mesh.shape["wsh"], heads=HEADS // mesh.shape["wsh"], scale=0.125, chunk=512,
        cuts=(0, 256, 512, 768, 1024, 1280, 1536), n_vec=2304, density=1.0 / math.sqrt(2.0 * math.pi), slope=jnp.bfloat16,
        first=[],
        seq_t=[
            (DO_START, 0), (DO_FORWARD, 1), (DO_QKV_Z, 0), (DO_QKV_PLANE, 0), (DO_QKV_CORE, 0), (DO_PLANE, 0),
            (DO_START, 1), (DO_START, 2), (DO_FORWARD, 2), (DO_NEAR, 1), (DO_PLANE, 1), (DO_NEAR, 0),
            (DO_PLANE, 2), (DO_FORWARD, 3), (DO_START, 3), (DO_NEAR, 2), (DO_CROSS, 1), (DO_NEAR, 3),
        ],
        moves_a=[
            (0, DO_CROSS, 0), (1, DO_START, 4), (1, DO_PLANE, 3), (3, DO_CROSS, 2), (6, DO_CROSS, 3),
            (8, DO_PLANE, 4), (8, DO_CORE, 2), (8, DO_CORE, 1), (10, DO_CORE, 0), (11, DO_CROSS, 4),
            (11, DO_CORE, 3),
        ],
        seq_f0=[
            (DO_CORE, 4),
        ],
        seq_f1=[],
        seq_f2=[
            (DO_WEIGHT_GRAD, 1), (DO_WEIGHT_GRAD, 0),
        ],
        seq_b=[
            (DO_CORE_ADD, 1), (DO_X1_SEND, 1), (DO_CORE_ADD, 0), (DO_VEC_CORE, 0),
        ],
        moves_b=[
            (0, DO_X1_SEND, 0), (1, DO_WEIGHT_GRAD, 3), (1, DO_WEIGHT_GRAD, 2), (1, DO_CORE_ADD, 4),
            (3, DO_X1_FAR, 0), (3, DO_X1_FAR, 1), (4, DO_X1_SEND, 4), (5, DO_VEC_PLANE, 0), (5, DO_X1_OWN, 0),
            (5, DO_X2_ADD, 0), (6, DO_Z_SEND, 0), (6, DO_CORE_ADD, 3), (7, DO_X1_SEND, 3), (7, DO_X1_OWN, 1),
            (7, DO_X2_ADD, 1), (8, DO_X1_FAR, 4), (8, DO_CORE_ADD, 2), (8, DO_X1_SEND, 2), (8, DO_Z_SEND, 1),
            (9, DO_X1_FAR, 3), (10, DO_VEC_Z, 0), (10, DO_Z_ADD, 0), (10, DO_X1_OWN, 4), (11, DO_X1_OWN, 3),
        ],
        seq_k=[
            (DO_X2_ADD, 4), (DO_Z_SEND, 4), (DO_Z_ADD, 1), (DO_X1_FAR, 2),
        ],
        seq_l=[
            (DO_LINE, 0), (DO_GRAD_PROJ, 0), (DO_X1_OWN, 2), (DO_B_CORE, 0), (DO_X2_ADD, 2), (DO_Z_SEND, 2),
            (DO_CORE_ADD, 5), (DO_X1_SEND, 5), (DO_B_PLANE, 0), (DO_LINE, 1), (DO_G_SEND, 0), (DO_X1_FAR, 5),
            (DO_LINE, 2), (DO_X1_OWN, 5), (DO_X2_ADD, 5), (DO_Z_SEND, 5), (DO_G_FORWARD, 0), (DO_G_SEND, 1),
            (DO_Z_ADD, 2), (DO_OWN_ROWS, 0), (DO_Z_ADD, 4), (DO_LINE, 3), (DO_LINE, 4), (DO_G_SEND, 4),
            (DO_X2_ADD, 3), (DO_VEC_END, 0), (DO_Z_SEND, 3), (DO_G_SEND, 2), (DO_LINE, 5), (DO_Z_ADD, 5),
            (DO_G_SEND, 5),
        ],
        seq_g=[
            (DO_G_FORWARD, 1), (DO_G_FORWARD, 4), (DO_G_FORWARD, 5), (DO_Z_ADD, 3), (DO_G_SEND, 3),
            (DO_G_CORE, 0), (DO_G_CORE, 1), (DO_G_CORE, 5), (DO_G_FORWARD, 2), (DO_G_FORWARD, 3), (DO_G_CORE, 4),
            (DO_G_CORE, 2), (DO_G_CORE, 3),
        ],
    )


def solution(mesh):
    fast = mesh.shape["seq"] == 4 and mesh.shape["ctx"] == 2 and HEADS % mesh.shape["wsh"] == 0
    return jax.shard_map(
        partial(fast_device, plan(mesh)) if fast else per_device,
        mesh=mesh,
        in_specs=(
            P("seq", ("ctx", "wsh"), None),
            P("seq", ("ctx", "wsh")),
            P("wsh", None),
            P("wsh"),
            P("wsh", None),
            P("wsh", None),
            P("wsh"),
            P("wsh", None),
            P("wsh"),
            P("wsh"),
            P("wsh"),
            P("wsh", None),
            P("wsh"),
            P("wsh", None),
            P("wsh"),
            P("wsh"),
            P("wsh"),
            P("seq", ("ctx", "wsh"), None),
        ),
        out_specs=(
            P("seq", ("ctx", "wsh"), None),
            P("seq", ("ctx", "wsh"), None),
            P("wsh", None),
            P("wsh"),
            P("wsh", None),
            P("wsh", None),
            P("wsh"),
            P("wsh", None),
            P("wsh"),
            P("wsh"),
            P("wsh"),
            P("wsh", None),
            P("wsh"),
            P("wsh", None),
            P("wsh"),
            P("wsh"),
            P("wsh"),
        ),
        check_vma=False,
    )
```

```python
from functools import partial
import math

import jax
import jax.numpy as jnp
from jax import lax
from jax.experimental import pallas as pl
from jax.experimental.pallas import tpu as pltpu
from jax.sharding import PartitionSpec as P

HEADS = 12


norm_eps = 1e-12
masked_fill = -1e30


def matmul(left, right):
    return jnp.dot(left, right, preferred_element_type=jnp.float32)


def matmul_left_t(left, right):
    return lax.dot_general(
        left, right, (((0,), (0,)), ((), ())), preferred_element_type=jnp.float32
    )


def matmul_right_t(left, right):
    return lax.dot_general(
        left, right, (((1,), (1,)), ((), ())), preferred_element_type=jnp.float32
    )


def normalize(values, gain, shift):
    centre = jnp.mean(values, axis=-1, keepdims=True)
    centred = values - centre
    inverse = lax.rsqrt(jnp.mean(centred * centred, axis=-1, keepdims=True) + norm_eps)
    normed = centred * inverse
    return (normed * gain + shift, normed, inverse)


def normalize_back(grad_out, normed, inverse, gain):
    grad_gain = jnp.sum(grad_out * normed, axis=0)
    grad_shift = jnp.sum(grad_out, axis=0)
    scaled = grad_out * gain
    grad_in = inverse * (
        scaled
        - jnp.mean(scaled, axis=-1, keepdims=True)
        - normed * jnp.mean(scaled * normed, axis=-1, keepdims=True)
    )
    return (grad_in, grad_gain, grad_shift)


def block_scores(query_blk, key_blk, seg_query, seg_key, score_scale):
    scores = (
        jnp.einsum("qhd,khd->hqk", query_blk, key_blk, preferred_element_type=jnp.float32)
        * score_scale
    )
    same_doc = seg_query[:, None] == seg_key[None, :]
    return (jnp.where(same_doc[None], scores, masked_fill), same_doc)


def block_grads(
    query_blk, dctx_blk, lse_blk, delta_blk, seg_query, key_blk, value_blk, seg_key, score_scale
):
    scores, same_doc = block_scores(query_blk, key_blk, seg_query, seg_key, score_scale)
    weights = jnp.where(same_doc[None], jnp.exp(scores - lse_blk.T[:, :, None]), 0.0)
    grad_weights = jnp.einsum(
        "qhd,khd->hqk", dctx_blk, value_blk, preferred_element_type=jnp.float32
    )
    grad_scores = (weights * (grad_weights - delta_blk.T[:, :, None])).astype(jnp.bfloat16)
    grad_query = None
    grad_key = None
    grad_value = None
    grad_query = (
        jnp.einsum("hqk,khd->qhd", grad_scores, key_blk, preferred_element_type=jnp.float32)
        * score_scale
    )
    grad_key = (
        jnp.einsum("hqk,qhd->khd", grad_scores, query_blk, preferred_element_type=jnp.float32)
        * score_scale
    )
    grad_value = jnp.einsum(
        "hqk,qhd->khd", weights.astype(jnp.bfloat16), dctx_blk, preferred_element_type=jnp.float32
    )
    return (grad_query, grad_key, grad_value)


def per_device(
    tokens,
    segment_ids,
    w_query,
    b_query,
    w_key,
    w_value,
    b_value,
    w_out,
    b_out,
    gain_attn,
    shift_attn,
    w_in,
    b_in,
    w_down,
    b_down,
    gain_ffn,
    shift_ffn,
    cotangent,
):
    (
        full_query,
        bias_query,
        full_key,
        full_value,
        bias_value,
        full_out,
        bias_out,
        gain_one,
        shift_one,
        full_in,
        bias_in,
        full_down,
        bias_down,
        gain_two,
        shift_two,
    ) = (
        lax.all_gather(w_query, "wsh", axis=0, tiled=True),
        lax.all_gather(b_query, "wsh", axis=0, tiled=True),
        lax.all_gather(w_key, "wsh", axis=0, tiled=True),
        lax.all_gather(w_value, "wsh", axis=0, tiled=True),
        lax.all_gather(b_value, "wsh", axis=0, tiled=True),
        lax.all_gather(w_out, "wsh", axis=0, tiled=True),
        lax.all_gather(b_out, "wsh", axis=0, tiled=True),
        lax.all_gather(gain_attn, "wsh", axis=0, tiled=True),
        lax.all_gather(shift_attn, "wsh", axis=0, tiled=True),
        lax.all_gather(w_in, "wsh", axis=0, tiled=True),
        lax.all_gather(b_in, "wsh", axis=0, tiled=True),
        lax.all_gather(w_down, "wsh", axis=0, tiled=True),
        lax.all_gather(b_down, "wsh", axis=0, tiled=True),
        lax.all_gather(gain_ffn, "wsh", axis=0, tiled=True),
        lax.all_gather(shift_ffn, "wsh", axis=0, tiled=True),
    )
    inputs = tokens[0]
    rows = inputs.shape[0]
    width = inputs.shape[1]
    head_dim = width // HEADS
    score_scale = 1.0 / math.sqrt(head_dim)
    seg_float = segment_ids[0].astype(jnp.bfloat16)
    queries = (matmul(inputs, full_query) + bias_query.astype(jnp.float32)).astype(jnp.bfloat16)
    key_rows = matmul(inputs, full_key).astype(jnp.bfloat16)
    values = (matmul(inputs, full_value) + bias_value.astype(jnp.float32)).astype(jnp.bfloat16)
    keys_all, values_all, segs_all = (
        lax.all_gather(key_rows, ("ctx", "wsh"), axis=0, tiled=True),
        lax.all_gather(values, ("ctx", "wsh"), axis=0, tiled=True),
        lax.all_gather(seg_float, ("ctx", "wsh"), axis=0, tiled=True),
    )
    total = keys_all.shape[0]
    key_block = min(512, total)
    block_count = total // key_block
    key_blocks = keys_all.reshape(block_count, key_block, HEADS, head_dim)
    value_blocks = values_all.reshape(block_count, key_block, HEADS, head_dim)
    seg_blocks = segs_all.reshape(block_count, key_block)
    query_heads = queries.reshape(rows, HEADS, head_dim)

    def forward_block(carry, block):
        run_max, run_sum, accum = carry
        key_blk, value_blk, seg_blk = block
        scores, same_doc = block_scores(query_heads, key_blk, seg_float, seg_blk, score_scale)
        new_max = jnp.maximum(run_max, jnp.max(scores, axis=2))
        raised = jnp.where(same_doc[None], jnp.exp(scores - new_max[:, :, None]), 0.0)
        factor = jnp.exp(run_max - new_max)
        run_sum = run_sum * factor + jnp.sum(raised, axis=2)
        accum = accum * factor.T[:, :, None] + jnp.einsum(
            "hqk,khd->qhd",
            raised.astype(jnp.bfloat16),
            value_blk,
            preferred_element_type=jnp.float32,
        )
        return ((new_max, run_sum, accum), None)

    start_state = (
        jnp.full((HEADS, rows), masked_fill, jnp.float32),
        jnp.zeros((HEADS, rows), jnp.float32),
        jnp.zeros((rows, HEADS, head_dim), jnp.float32),
    )
    (run_max, run_sum, accum), unused = lax.scan(
        forward_block, start_state, (key_blocks, value_blocks, seg_blocks)
    )
    attended = accum / run_sum.T[:, :, None]
    lse_rows = (run_max + jnp.log(run_sum)).T
    context = attended.reshape(rows, width).astype(jnp.bfloat16)
    attn_out = matmul(context, full_out) + bias_out.astype(jnp.float32)
    gain_first = gain_one.astype(jnp.float32)
    gain_second = gain_two.astype(jnp.float32)
    hidden, normed_one, inverse_one = normalize(
        inputs.astype(jnp.float32) + attn_out, gain_first, shift_one.astype(jnp.float32)
    )
    hidden_low = hidden.astype(jnp.bfloat16)
    inner = matmul(hidden_low, full_in) + bias_in.astype(jnp.float32)
    active_float, gelu_pull = jax.vjp(partial(jax.nn.gelu, approximate=False), inner)
    active = active_float.astype(jnp.bfloat16)
    branch = matmul(active, full_down) + bias_down.astype(jnp.float32)
    result, normed_two, inverse_two = normalize(
        hidden + branch, gain_second, shift_two.astype(jnp.float32)
    )
    grad_out = cotangent[0].astype(jnp.float32)
    grad_res_two, grad_gain_two, grad_shift_two = normalize_back(
        grad_out, normed_two, inverse_two, gain_second
    )
    grad_branch = grad_res_two.astype(jnp.bfloat16)
    grad_bias_down = jnp.sum(grad_branch.astype(jnp.float32), axis=0)
    grad_full_down = matmul_left_t(active, grad_branch)
    grad_inner = gelu_pull(matmul_right_t(grad_branch, full_down))[0].astype(jnp.bfloat16)
    grad_bias_in = jnp.sum(grad_inner.astype(jnp.float32), axis=0)
    grad_full_in = matmul_left_t(hidden_low, grad_inner)
    grad_hidden = grad_res_two + matmul_right_t(grad_inner, full_in)
    grad_res_one, grad_gain_one, grad_shift_one = normalize_back(
        grad_hidden, normed_one, inverse_one, gain_first
    )
    grad_attn = grad_res_one.astype(jnp.bfloat16)
    grad_bias_out = jnp.sum(grad_attn.astype(jnp.float32), axis=0)
    grad_full_out = matmul_left_t(context, grad_attn)
    grad_context = matmul_right_t(grad_attn, full_out).astype(jnp.bfloat16)
    dctx_heads = grad_context.reshape(rows, HEADS, head_dim)
    delta_rows = jnp.sum(dctx_heads.astype(jnp.float32) * attended, axis=2)
    zero_heads = jnp.zeros((rows, HEADS, head_dim), jnp.float32)

    def back_block(grad_acc, block):
        key_blk, value_blk, seg_blk = block
        part_query, part_key, part_value = block_grads(
            query_heads,
            dctx_heads,
            lse_rows,
            delta_rows,
            seg_float,
            key_blk,
            value_blk,
            seg_blk,
            score_scale,
        )
        return (grad_acc + part_query, (part_key, part_value))

    grad_q, (key_parts, value_parts) = lax.scan(
        back_block, zero_heads, (key_blocks, value_blocks, seg_blocks)
    )
    grad_key_own, grad_value_own = (
        lax.psum_scatter(
            key_parts.reshape(total, width), ("ctx", "wsh"), scatter_dimension=0, tiled=True
        ),
        lax.psum_scatter(
            value_parts.reshape(total, width), ("ctx", "wsh"), scatter_dimension=0, tiled=True
        ),
    )
    grad_queries = grad_q.reshape(rows, width).astype(jnp.bfloat16)
    grad_keys = grad_key_own.astype(jnp.bfloat16)
    grad_values = grad_value_own.astype(jnp.bfloat16)
    grad_full_query = matmul_left_t(inputs, grad_queries)
    grad_bias_query = jnp.sum(grad_queries.astype(jnp.float32), axis=0)
    grad_full_key = matmul_left_t(inputs, grad_keys)
    grad_full_value = matmul_left_t(inputs, grad_values)
    grad_bias_value = jnp.sum(grad_values.astype(jnp.float32), axis=0)
    grad_input = (
        grad_res_one
        + matmul_right_t(grad_queries, full_query)
        + matmul_right_t(grad_keys, full_key)
        + matmul_right_t(grad_values, full_value)
    )
    (
        share_query,
        share_bias_query,
        share_key,
        share_value,
        share_bias_value,
        share_out,
        share_bias_out,
        share_gain_one,
        share_shift_one,
        share_in,
        share_bias_in,
        share_down,
        share_bias_down,
        share_gain_two,
        share_shift_two,
    ) = (
        lax.psum_scatter(
            grad_full_query.astype(jnp.bfloat16), "wsh", scatter_dimension=0, tiled=True
        ).astype(jnp.float32),
        lax.psum_scatter(
            grad_bias_query.astype(jnp.bfloat16), "wsh", scatter_dimension=0, tiled=True
        ).astype(jnp.float32),
        lax.psum_scatter(
            grad_full_key.astype(jnp.bfloat16), "wsh", scatter_dimension=0, tiled=True
        ).astype(jnp.float32),
        lax.psum_scatter(
            grad_full_value.astype(jnp.bfloat16), "wsh", scatter_dimension=0, tiled=True
        ).astype(jnp.float32),
        lax.psum_scatter(
            grad_bias_value.astype(jnp.bfloat16), "wsh", scatter_dimension=0, tiled=True
        ).astype(jnp.float32),
        lax.psum_scatter(
            grad_full_out.astype(jnp.bfloat16), "wsh", scatter_dimension=0, tiled=True
        ).astype(jnp.float32),
        lax.psum_scatter(
            grad_bias_out.astype(jnp.bfloat16), "wsh", scatter_dimension=0, tiled=True
        ).astype(jnp.float32),
        lax.psum_scatter(
            grad_gain_one.astype(jnp.bfloat16), "wsh", scatter_dimension=0, tiled=True
        ).astype(jnp.float32),
        lax.psum_scatter(
            grad_shift_one.astype(jnp.bfloat16), "wsh", scatter_dimension=0, tiled=True
        ).astype(jnp.float32),
        lax.psum_scatter(
            grad_full_in.astype(jnp.bfloat16), "wsh", scatter_dimension=0, tiled=True
        ).astype(jnp.float32),
        lax.psum_scatter(
            grad_bias_in.astype(jnp.bfloat16), "wsh", scatter_dimension=0, tiled=True
        ).astype(jnp.float32),
        lax.psum_scatter(
            grad_full_down.astype(jnp.bfloat16), "wsh", scatter_dimension=0, tiled=True
        ).astype(jnp.float32),
        lax.psum_scatter(
            grad_bias_down.astype(jnp.bfloat16), "wsh", scatter_dimension=0, tiled=True
        ).astype(jnp.float32),
        lax.psum_scatter(
            grad_gain_two.astype(jnp.bfloat16), "wsh", scatter_dimension=0, tiled=True
        ).astype(jnp.float32),
        lax.psum_scatter(
            grad_shift_two.astype(jnp.bfloat16), "wsh", scatter_dimension=0, tiled=True
        ).astype(jnp.float32),
    )
    summed = lax.psum(
        (
            share_query,
            share_bias_query,
            share_key,
            share_value,
            share_bias_value,
            share_out,
            share_bias_out,
            share_gain_one,
            share_shift_one,
            share_in,
            share_bias_in,
            share_down,
            share_bias_down,
            share_gain_two,
            share_shift_two,
        ),
        ("seq", "ctx"),
    )
    return (
        result.astype(jnp.bfloat16)[None],
        grad_input.astype(jnp.bfloat16)[None],
        summed[0],
        summed[1],
        summed[2],
        summed[3],
        summed[4],
        summed[5],
        summed[6],
        summed[7],
        summed[8],
        summed[9],
        summed[10],
        summed[11],
        summed[12],
        summed[13],
        summed[14],
    )


(DO_START, DO_PLANE, DO_CROSS, DO_CORE, DO_QKV_Z, DO_QKV_PLANE,
 DO_QKV_CORE, DO_FORWARD, DO_NEAR, DO_WEIGHT_GRAD, DO_CORE_ADD, DO_X1_SEND,
 DO_X1_FAR, DO_X1_OWN, DO_X2_ADD, DO_Z_SEND, DO_Z_ADD, DO_G_SEND,
 DO_G_FORWARD, DO_G_CORE, DO_VEC_CORE, DO_VEC_PLANE, DO_VEC_Z, DO_VEC_END,
 DO_LINE, DO_GRAD_PROJ, DO_B_CORE, DO_B_PLANE, DO_OWN_ROWS) = range(29)


MESH_ID = pl.DeviceIdType.MESH
LANES = 256
IDS = 16
BIG = float(2.0**99)
VMEM_LIMIT = 62 * 2**20


def remote(src, dst, send, recv, where):
    return pltpu.make_async_remote_copy(
        src_ref=src, dst_ref=dst, send_sem=send, recv_sem=recv, device_id=where, device_id_type=MESH_ID
    )


def nt(left, right):
    return lax.dot_general(left, right, (((1,), (1,)), ((), ())), preferred_element_type=jnp.float32)


def tn(left, right):
    return lax.dot_general(left, right, (((0,), (0,)), ((), ())), preferred_element_type=jnp.float32)


def nn(left, right):
    return jnp.dot(left, right, preferred_element_type=jnp.float32)


def greet(peers):
    barrier = pltpu.get_barrier_semaphore()
    for peer in peers:
        pl.semaphore_signal(barrier, inc=1, device_id=peer, device_id_type=MESH_ID)
    pl.semaphore_wait(barrier, len(peers))


def layer_kernel(
    dims,
    tokens, seg, w_q, w_k, w_v, b_q, b_v, b_o, gain_1, shift_1, b_i, b_d, gain_2, shift_2, cot, w_o, w_i, w_d,
    result, g_tok, gd, gi, go, gq, g_vec, g_b,
    toks, wcol, qx, kx, vv, att_t, lse, ctx, res, active, grad_branch, hidden_low, grad_inner, grad_attn, grad_vec,
    full_o, full_i, full_d, vecs, slope, segs, w_send, vt, scores, dv, ctx_send, ctx_recv, d_recv, dqkv, kv_recv, rx,
    bufs, deltas, vx, vc, vs, vz, bc, bs,
    tok_s, tok_r, sv_s, sv_r, wz_s, wz_r, wp_s, wp_r, kv_s, kv_r, cx_s, cx_r,
    fz_s, fz_r, fx_s, fx_r, fc_s, fc_r, loc,
    da_s, da_r, kb_s, kb_r, rx_s, rx_r, core_s, core_r, x1_s, x1_r, x2_s, x2_r, za_s, za_r, ga_s, ga_r, gc_s, gc_r,
    vp_s, vp_r, bp_s, bp_r,
):
    S, W, heads = dims["S"], dims["W"], dims["heads"]
    rows, width = tokens.shape
    f32, bf16 = jnp.float32, jnp.bfloat16
    group = width // W
    head_dim = group // heads
    block = rows * W
    total = 2 * block
    ff = w_i.shape[1]
    P = (full_d, full_d, full_i, full_i, full_o, w_send)
    G = (gd, gd, gi, gi, go, gq)
    CR, X1, X2, Z = bufs[:6], bufs[6:12], bufs[12:18], bufs[18:24]
    last = 5
    kt, dk, kv_send, px, dq_t = vt, scores, kx, active, att_t

    def run(name):
        for stage, part in dims[name]:
            stages[stage](part)

    s, c, z = lax.axis_index("seq"), lax.axis_index("ctx"), lax.axis_index("wsh")
    sib = (s, 1 - c, z)
    s1, s2, s3 = s ^ 1, s ^ 2, s ^ 3
    shifts = list(range(1, W))
    zz = [lax.rem(z + t, W) for t in shifts]
    barrier = pltpu.get_barrier_semaphore()
    peers = [sib] + [(p, c, z) for p in (s1, s2, s3)] + [(s, c, q) for q in zz]
    for peer in peers:
        pl.semaphore_signal(barrier, inc=1, device_id=peer, device_id_type=MESH_ID)
    toks[z] = tokens[...]
    segs[z] = seg[...].astype(jnp.float32)
    for ref, lo in zip((b_o, gain_1, shift_1, b_d, gain_2, shift_2, b_i), dims["cuts"]):
        vecs[z, :, lo : lo + ref.shape[0]] = ref[...].astype(jnp.float32).reshape(1, -1)

    for j in range(W):
        for m, ref in enumerate((w_q, w_k, w_v)):
            part = ref[:, j * group : (j + 1) * group]
            part = jnp.concatenate([part, jnp.zeros((group, LANES - group), part.dtype)], axis=1)
            w_send[j, :, m * LANES : (m + 1) * LANES] = part

    pl.semaphore_wait(barrier, len(peers))

    slab, wide = group // S, 3 * LANES // 2

    def col_at(ref, base, cc, ss):
        rows_at = pl.ds(pl.multiple_of(base + (0 if ss is None else ss * slab), 16), group if ss is None else slab)
        return ref.at[rows_at, pl.ds(pl.multiple_of(cc * wide, 128), wide)]

    def wz(q):
        return remote(col_at(w_send.at[q], 0, c, s), col_at(wcol, z * group, c, s), wz_s.at[q], wz_r.at[z], (s, c, q))

    def wz_in(q):
        here = col_at(wcol, q * group, c, s)
        return remote(here, here, wz_s.at[q], wz_r.at[q], (s, c, q))

    def wp(q, k):
        ref = col_at(wcol, q * group, c, s if k else None)
        return remote(ref, ref, wp_s.at[q, k], wp_r.at[q, k], (s ^ k, c, z) if k else sib)

    def wp_in(q, k):
        ref = col_at(wcol, q * group, c, s ^ k) if k else col_at(wcol, q * group, 1 - c, None)
        return remote(ref, ref, wp_s.at[q, k], wp_r.at[q, k], sib)

    def seg_out(q):
        return remote(segs.at[z], segs.at[z], sv_s.at[0, q], sv_r.at[0, z], (s, c, q))

    def seg_in(q):
        return remote(segs.at[q], segs.at[q], sv_s.at[0, q], sv_r.at[0, q], (s, c, q))

    def vec_out(q):
        return remote(vecs.at[z], vecs.at[z], sv_s.at[1, q], sv_r.at[1, z], (s, c, q))

    def vec_in(q):
        return remote(vecs.at[q], vecs.at[q], sv_s.at[1, q], sv_r.at[1, q], (s, c, q))

    def tok_copy(slot, step, lane):
        return remote(toks.at[slot], toks.at[slot], tok_s.at[lane, slot], tok_r.at[slot], (s, c, z + step))

    def cut_of(how, row, n, m, shard, whole):
        return dict(how=how, row=row, n=n, m=m, shard=shard, whole=whole)

    down = ff // W // 2
    cuts_o = cut_of(0, 0, group, width, w_o, full_o)
    cuts_i = [cut_of(1, u * (group // 2), group // 2, ff, w_i, full_i) for u in range(2)]
    cuts_d = [cut_of(2, u * down, down, width, w_d, full_d) for u in range(2)]
    parts = (cuts_o, *cuts_i, *cuts_d)

    def place(cut, cc, ss, half=None):
        n, m = cut["n"], cut["m"]
        if cut["how"] == 0:
            row, size = (0, n) if ss is None else (ss * (n // S), n // S)
            col, wide = cc * (m // 2), m // 2
            if half is not None:
                col, wide = col + (0 if half == 0 else 128), (128 if half == 0 else m // 2 - 128)
        elif cut["how"] == 1:
            row, size = 0, n
            col, wide = cc * (m // 2) + (0 if ss is None else ss * (m // 8)), m // 2 if ss is None else m // 8
            if half is not None:
                row, size = half * (n // 2), n // 2
        else:
            row, size = cc * (n // 2) + (0 if ss is None else ss * (n // 8)), n // 2 if ss is None else n // 8
            col, wide = 0, m
            if half is not None:
                col, wide = half * (m // 2), m // 2
        row = cut["row"] + row
        if not isinstance(row, int):
            row = pl.multiple_of(row, 16)
        if not isinstance(col, int):
            col = pl.multiple_of(col, 128)
        return pl.ds(row, size), pl.ds(col, wide)

    def rows_of(part, q, cc, ss, half=None):
        return parts[part]["whole"].at[q].at[place(parts[part], cc, ss, half)]

    def own_copy(w):
        shard, whole = ((w_o, full_o), (w_i, full_i), (w_d, full_d))[w]
        return pltpu.make_async_copy(shard, whole.at[z], loc.at[w])

    def fz(part, q):
        src = parts[part]["shard"].at[place(parts[part], c, s)]
        return remote(src, rows_of(part, z, c, s), fz_s.at[part, q], fz_r.at[part, z], (s, c, q))

    def fz_in(part, q):
        here = rows_of(part, q, c, s)
        return remote(here, here, fz_s.at[part, q], fz_r.at[part, q], (s, c, q))

    def fx(part, q, kind):
        if kind < 2:
            ref, to = rows_of(part, q, c, s), (s1, s2)[kind]
        else:
            ref, to = rows_of(part, q, c, (s1, s2)[kind - 2], kind - 2), (s2, s1)[kind - 2]
        return remote(ref, ref, fx_s.at[part, q, kind], fx_r.at[part, q, kind], (to, c, z))

    def fx_in(part, q, kind):
        if kind < 2:
            ref = rows_of(part, q, c, (s1, s2)[kind])
        else:
            ref = rows_of(part, q, c, s3, kind - 2)
        return remote(ref, ref, fx_s.at[part, q, kind], fx_r.at[part, q, kind], (s1, c, z))

    def fc(part, q):
        ref = rows_of(part, q, c, None)
        return remote(ref, ref, fc_s.at[part, q], fc_r.at[part, q], sib)

    def fc_in(part, q):
        ref = rows_of(part, q, 1 - c, None)
        return remote(ref, ref, fc_s.at[part, q], fc_r.at[part, q], sib)

    def w_start(part):
        for q in zz:
            fz(part, q).start()

    def w_plane(part):
        for q in zz:
            fz_in(part, q).wait_recv()
            fx(part, q, 0).start()
            fx(part, q, 1).start()

    def w_cross(part):
        for q in zz:
            fx_in(part, q, 0).wait_recv()
            fx(part, q, 2).start()
            fx_in(part, q, 1).wait_recv()
            fx(part, q, 3).start()

    def w_core(part):
        for q in zz:
            fx_in(part, q, 2).wait_recv()
            fx_in(part, q, 3).wait_recv()
            fc(part, q).start()

    def w_ready(w):
        own_copy(w).wait()
        for part in ((0,), (1, 2), (3, 4))[w]:
            for q in zz:
                fc_in(part, q).wait_recv()

    stages = {DO_PLANE: w_plane, DO_CROSS: w_cross, DO_CORE: w_core, DO_START: w_start}

    def w_finish(part):
        for q in zz:
            fz(part, q).wait_send()
            for kind in range(4):
                fx(part, q, kind).wait_send()
            fc(part, q).wait_send()


    for q in zz:
        wz(q).start()
        seg_out(q).start()
    for w in range(3):
        own_copy(w).start()
    for part in dims["first"]:
        w_start(part)
    @pl.when(z + 1 < W)
    def _():
        tok_copy(z, 1, 0).start()

    @pl.when(z > 0)
    def _():
        tok_copy(z, -1, 1).start()

    for q in zz:
        vec_out(q).start()

    lane = lax.broadcasted_iota(jnp.int32, (1, LANES), 1)
    spot = lax.broadcasted_iota(jnp.int32, (IDS, LANES), 1) - lax.broadcasted_iota(jnp.int32, (IDS, LANES), 0)
    lanes_in = lax.broadcasted_iota(jnp.int32, (IDS, LANES), 1)
    in_ext = (lanes_in >= group) & (lanes_in < group + IDS)
    put_q = jnp.where(spot == group, 1.0, 0.0).astype(jnp.bfloat16)
    put_k = jnp.where(in_ext & (spot != group), -BIG, 0.0).astype(jnp.bfloat16)
    pad = jnp.zeros((1, LANES - group), jnp.float32)
    bias_q = jnp.concatenate([b_q[...].astype(jnp.float32).reshape(1, -1), pad], axis=1)
    bias_v = jnp.concatenate([b_v[...].astype(jnp.float32).reshape(1, -1), pad], axis=1)
    ids = lax.broadcasted_iota(jnp.int32, (IDS, rows), 0).astype(jnp.float32)

    def k_rows(owner, slot):
        return pl.ds(pl.multiple_of(owner * block + slot * rows, rows), rows)

    def kv(slot, which):
        ref = (kx, vv)[which].at[k_rows(c, slot), :]
        return remote(ref, ref, kv_s.at[which, slot], kv_r.at[which, slot], sib)

    def kv_in(slot, which):
        ref = (kx, vv)[which].at[k_rows(1 - c, slot), :]
        return remote(ref, ref, kv_s.at[which, slot], kv_r.at[which, slot], sib)

    def project(slot):
        made = nn(toks[slot], wcol[...])
        hot = jnp.where(jnp.broadcast_to(segs[slot], (IDS, rows)) == ids, 1.0, 0.0).astype(jnp.bfloat16)
        q_low = (made[:, :LANES] + bias_q).astype(jnp.bfloat16).astype(jnp.float32) * dims["scale"]
        ext_q = tn(hot, put_q)
        for h in range(heads):
            mine = (lane >= h * head_dim) & (lane < (h + 1) * head_dim)
            qx[pl.ds(pl.multiple_of(h * block + slot * rows, rows), rows), :] = (
                jnp.where(mine, q_low, 0.0) + ext_q
            ).astype(jnp.bfloat16)
        kx[k_rows(c, slot), :] = (made[:, LANES : 2 * LANES] + tn(hot, put_k)).astype(jnp.bfloat16)
        vv[k_rows(c, slot), :] = (made[:, 2 * LANES :] + bias_v).astype(jnp.bfloat16)
        kv(slot, 0).start()
        kv(slot, 1).start()

    def qkv_z(part):
        for q in zz:
            wz_in(q).wait_recv()
            for k in (1, 2, 3):
                wp(q, k).start()

    def qkv_plane(part):
        for q in zz:
            for k in (1, 2, 3):
                wp_in(q, k).wait_recv()
            wp(q, 0).start()
        wcol[pl.ds(pl.multiple_of(z * group, 16), group), :] = w_send[z]

    def qkv_core(part):
        for q in zz:
            wp_in(q, 0).wait_recv()
            seg_in(q).wait_recv()

    def forward(far):
        @pl.when(z >= far)
        def _():
            tok_copy(z - far, 1, 0).wait_recv()

            @pl.when(z + 1 < W)
            def _():
                tok_copy(z - far, 1, 0).start()

        @pl.when(z + far < W)
        def _():
            tok_copy(z + far, 1, 0).wait_recv()

            @pl.when(z > 0)
            def _():
                tok_copy(z + far, -1, 1).start()

    def near(far):
        def side(k, carry):
            slot = jnp.where(k == 0, z - far, z + far)

            @pl.when((slot >= 0) & (slot < W))
            def _():
                project(slot)

            return carry

        if far == 0:
            project(z)
        else:
            lax.fori_loop(0, 2, side, 0)

    stages.update({
        DO_QKV_Z: qkv_z, DO_QKV_PLANE: qkv_plane, DO_QKV_CORE: qkv_core, DO_FORWARD: forward, DO_NEAR: near,
    })
    for name, part in dims["seq_t"]:
        stages[name](part)
    for j in range(W):
        kv_in(j, 0).wait_recv()
        kv_in(j, 1).wait_recv()
    vt[...] = vv[...].astype(jnp.float32).T.astype(jnp.bfloat16)

    chunk = dims["chunk"]
    n_chunks = total // chunk

    def cx(b):
        return remote(ctx_send.at[b], ctx_recv.at[z], cx_s.at[b], cx_r.at[z], (s, c, b))

    def cx_in(b):
        return remote(ctx_send.at[b], ctx_recv.at[b], cx_s.at[b], cx_r.at[b], (s, c, b))

    def attend(step, carry):
        i = lax.div(step, heads)
        h = lax.rem(step, heads)
        b = lax.rem(z + 1 + i, W)
        query = qx[pl.ds(pl.multiple_of(h * block + b * rows, rows), rows), :]
        top = None
        for n in range(n_chunks):
            got = nt(kx[n * chunk : (n + 1) * chunk, :], query)
            scores[n * chunk : (n + 1) * chunk, :] = got
            high = jnp.max(got, axis=0, keepdims=True)
            top = high if top is None else jnp.maximum(top, high)
        mass = None
        out = None
        here = pl.ds(pl.multiple_of(h * head_dim, head_dim), head_dim)
        for n in range(n_chunks):
            raised = jnp.exp(scores[n * chunk : (n + 1) * chunk, :] - top)
            add = jnp.sum(raised, axis=0, keepdims=True)
            mass = add if mass is None else mass + add
            piece_out = nn(vt[here, n * chunk : (n + 1) * chunk], raised.astype(jnp.bfloat16))
            out = piece_out if out is None else out + piece_out
        att_t[here, pl.ds(pl.multiple_of(b * rows, rows), rows)] = out / mass
        lse[h, :, pl.ds(pl.multiple_of(b * rows, rows), rows)] = top + jnp.log(mass)

        @pl.when(h == heads - 1)
        def _():
            done = att_t[:, pl.ds(pl.multiple_of(b * rows, rows), rows)]
            ctx_send[b] = done.T.astype(jnp.bfloat16)

            @pl.when(i < W - 1)
            def _():
                cx(b).start()

            @pl.when(i == W - 1)
            def _():
                ctx_recv[b] = ctx_send[b]

        for when, name, part in dims["moves_a"]:
            @pl.when(step == when)
            def _():
                stages[name](part)

        return carry

    lax.fori_loop(0, W * heads, attend, 0)
    for q in zz:
        wz(q).wait_send()
    for j in range(W):
        kv(j, 0).wait_send()
        kv(j, 1).wait_send()
    for q in zz:
        cx_in(q).wait_recv()
    for j in range(W):
        ctx[:, j * group : (j + 1) * group] = ctx_recv[j]
    for q in zz:
        vec_in(q).wait_recv()

    def vcore():
        return remote(vc.at[c], vc.at[c], vp_s.at[0], vp_r.at[0], sib)

    def vplane(k):
        return remote(vs.at[s], vs.at[s], vp_s.at[k], vp_r.at[k], (s ^ k, c, z))

    def vz_out(q, t):
        return remote(vx.at[q], vz.at[z], vp_s.at[4 + t], vp_r.at[4 + z], (s, c, q))

    def vz_in(q, t):
        return remote(vx.at[q], vz.at[q], vp_s.at[4 + t], vp_r.at[4 + q], (s, c, q))

    def vec_core():
        vc[c] = grad_vec[...]
        vcore().start()

    def vec_plane():
        vcore().wait_recv()
        vs[s] = vc[0] + vc[1]
        for k in (1, 2, 3):
            vplane(k).start()

    def vec_z():
        for k in (1, 2, 3):
            vplane(k).wait_recv()
        vx[...] = (vs[0] + vs[1]) + (vs[2] + vs[3])
        vz[z] = vx[z]
        for t, q in enumerate(zz):
            vz_out(q, t).start()

    def vec_end():
        for t, q in enumerate(zz):
            vz_in(q, t).wait_recv()
        acc = vz[0]
        for j in range(1, W):
            acc = acc + vz[j]
        g_vec[...] = acc
        vcore().wait_send()
        for k in (1, 2, 3):
            vplane(k).wait_send()
        for t, q in enumerate(zz):
            vz_out(q, t).wait_send()

    kinds = (*cuts_d, *cuts_i, cuts_o, cuts_o)

    def view(ref, a, cc, ss, half=None):
        return ref.at[(slice(None),) + place(kinds[a], cc, ss, half)]

    def within(a, half):
        n, m = kinds[a]["n"], kinds[a]["m"]
        if kinds[a]["how"] == 0:
            return (slice(0, n // S), slice(0, 128) if half == 0 else slice(128, m // 2))
        if kinds[a]["how"] == 1:
            return (slice(half * (n // 2), (half + 1) * (n // 2)), slice(0, m // 8))
        return (slice(0, n // 8), slice(half * (m // 2), (half + 1) * (m // 2)))

    def core_move(a):
        return remote(view(P[a], a, 1 - c, None), CR[a], core_s.at[a], core_r.at[a], sib)

    def add_into(a, cc, ss, half, more):
        at = place(kinds[a], cc, ss, half)
        for j in range(W):
            P[a][(j,) + at] = (P[a][(j,) + at].astype(f32) + more(j).astype(f32)).astype(bf16)

    def core_add(a):
        core_move(a).wait_recv()
        add_into(a, c, None, None, lambda j: CR[a][j])

    def x1(a, half, slot):
        to = (s1, s2)[half]
        at = ((s1, s3) if half == 0 else (s2, s3))[slot]
        k = half * 2 + slot
        return remote(view(P[a], a, c, at, half), X1[a].at[(slot, slice(None)) + within(a, half)], x1_s.at[a, k],
                      x1_r.at[a, k], (to, c, z))

    def x1_send(a):
        for slot in (1, 0):
            for half in range(2):
                x1(a, half, slot).start()

    def x1_far(a):
        for half in range(2):
            x1(a, half, 1).wait_recv()
            add_into(a, c, (s2, s1)[half], half, lambda j: X1[a][(1, j) + within(a, half)])
            x2(a, half).start()

    def x1_own(a):
        for half in range(2):
            x1(a, half, 0).wait_recv()
            add_into(a, c, s, half, lambda j: X1[a][(0, j) + within(a, half)])

    def x2(a, half):
        to = (s2, s1)[half]
        return remote(view(P[a], a, c, to, half), X2[a].at[(slice(None),) + within(a, half)], x2_s.at[a, half],
                      x2_r.at[a, half], (to, c, z))

    def x2_add(a):
        for half in range(2):
            x2(a, half).wait_recv()
            add_into(a, c, s, half, lambda j: X2[a][(j,) + within(a, half)])

    def own_piece(a, q):
        return P[a].at[q].at[place(kinds[a], c, s)]

    def za(a, q, t):
        return remote(own_piece(a, q), Z[a].at[z], za_s.at[a, t], za_r.at[a, z], (s, c, q))

    def za_in(a, q, t):
        return remote(own_piece(a, q), Z[a].at[q], za_s.at[a, t], za_r.at[a, q], (s, c, q))

    def z_send(a):
        for t, q in enumerate(zz):
            za(a, q, t).start()
        Z[a][z] = own_piece(a, z)[...]

    def z_add(a):
        for t, q in enumerate(zz):
            za_in(a, q, t).wait_recv()
        at = place(kinds[a], c, s)
        if a == last:
            for j in range(W):
                G[a][(j,) + at] = Z[a][j]
        else:
            acc = Z[a][0].astype(f32)
            for j in range(1, W):
                acc = acc + Z[a][j].astype(f32)
            G[a][at] = acc.astype(bf16)

    def g_view(a, cc, ss, half=None):
        at = place(kinds[a], cc, ss, half)
        return G[a].at[((slice(None),) + at) if a == last else at]

    def ga(a, kind):
        if kind < 2:
            ref, to = g_view(a, c, s), (s1, s2)[kind]
        else:
            ref, to = g_view(a, c, (s1, s2)[kind - 2], kind - 2), (s2, s1)[kind - 2]
        return remote(ref, ref, ga_s.at[a, kind], ga_r.at[a, kind], (to, c, z))

    def ga_in(a, kind):
        ref = g_view(a, c, (s1, s2)[kind]) if kind < 2 else g_view(a, c, s3, kind - 2)
        return remote(ref, ref, ga_s.at[a, kind], ga_r.at[a, kind], (s1, c, z))

    def gc(a):
        ref = g_view(a, c, None)
        return remote(ref, ref, gc_s.at[a], gc_r.at[a], sib)

    def gc_in(a):
        ref = g_view(a, 1 - c, None)
        return remote(ref, ref, gc_s.at[a], gc_r.at[a], sib)

    def g_send(a):
        ga(a, 0).start()
        ga(a, 1).start()

    def g_forward(a):
        for kind in range(2):
            ga_in(a, kind).wait_recv()
            ga(a, 2 + kind).start()

    def g_core(a):
        for kind in range(2):
            ga_in(a, 2 + kind).wait_recv()
        gc(a).start()

    def drain(a):
        core_move(a).wait_send()
        for half in range(2):
            x1(a, half, 0).wait_send()
            x1(a, half, 1).wait_send()
            x2(a, half).wait_send()
        for t, q in enumerate(zz):
            za(a, q, t).wait_send()
        for kind in range(4):
            ga(a, kind).wait_send()
        gc(a).wait_send()

    def weight_grad(a):
        if a < 2:
            w_finish(3 + a)
            lanes = slice(a * down, (a + 1) * down)
            for k in range(W):
                full_d[k, lanes, :] = tn(active[k, :, lanes], grad_branch[...]).astype(bf16)
            core_move(a).start()
        elif a == 2:
            w_finish(1)
            w_finish(2)
            for k in range(W):
                made = tn(hidden_low[...], grad_inner[k]).astype(bf16)
                for j in range(W):
                    full_i[j, :, k * width : (k + 1) * width] = made[j * group : (j + 1) * group]
            core_move(2).start()
            core_move(3).start()
        else:
            w_finish(0)
            made = tn(ctx[...], grad_attn[...]).astype(bf16)
            for j in range(W):
                full_o[j] = made[j * group : (j + 1) * group]
            core_move(4).start()

    stages.update({
        DO_CORE_ADD: core_add, DO_X1_SEND: x1_send, DO_X1_FAR: x1_far, DO_X1_OWN: x1_own, DO_X2_ADD: x2_add,
        DO_Z_SEND: z_send, DO_Z_ADD: z_add, DO_G_SEND: g_send, DO_G_FORWARD: g_forward, DO_G_CORE: g_core,
        DO_WEIGHT_GRAD: weight_grad, DO_VEC_CORE: lambda a: vec_core(), DO_VEC_PLANE: lambda a: vec_plane(),
        DO_VEC_Z: lambda a: vec_z(), DO_VEC_END: lambda a: vec_end(),
    })

    cuts = dims["cuts"]

    def vec_of(k):
        n = (b_o, gain_1, shift_1, b_d, gain_2, shift_2, b_i)[k].shape[0]
        return jnp.concatenate([vecs[j, :, cuts[k] : cuts[k] + n] for j in range(W)], axis=1)

    def norm(values, gain, shift):
        centred = values - jnp.mean(values, axis=-1, keepdims=True)
        inverse = lax.rsqrt(jnp.mean(centred * centred, axis=-1, keepdims=True) + norm_eps)
        normed = centred * inverse
        return normed * gain + shift, normed, inverse

    def norm_back(grad, normed, inverse, gain):
        scaled = grad * gain
        return inverse * (
            scaled
            - jnp.mean(scaled, axis=-1, keepdims=True)
            - normed * jnp.mean(scaled * normed, axis=-1, keepdims=True)
        )

    def put_vec(k, values):
        n = values.shape[1] // W
        for j in range(W):
            grad_vec[j, :, cuts[k] : cuts[k] + n] = values[:, j * n : (j + 1) * n]

    def total_of(values):
        return jnp.sum(values, axis=0, keepdims=True)

    gain_a, gain_b = vec_of(1), vec_of(4)
    w_ready(0)
    summed = tokens[...].astype(f32) + (nn(ctx[...], full_o[...].reshape(width, width)) + vec_of(0))
    hidden, normed_1, inverse_1 = norm(summed, gain_a, vec_of(2))
    hidden_low[...] = hidden.astype(bf16)
    run("seq_f0")
    w_ready(1)
    spans = [slice(k * width, (k + 1) * width) for k in range(W)]
    bias_in = vec_of(6)
    for k, span in enumerate(spans):
        inner = nn(hidden_low[...], full_i[:, :, span].reshape(width, width)) + bias_in[:, span]
        cdf = 0.5 * (1.0 + lax.erf(inner * (0.5**0.5)))
        active[k] = (inner * cdf).astype(bf16)
        slope[k] = (cdf + inner * (jnp.exp(-0.5 * inner * inner) * dims["density"])).astype(slope.dtype)
    run("seq_f1")
    w_ready(2)
    branch = vec_of(3)
    for k in range(W):
        branch = branch + nn(active[k], full_d[k])
    out, normed_2, inverse_2 = norm(hidden + branch, gain_b, vec_of(5))
    result[...] = out.astype(bf16)
    grad_out = cot[0].astype(f32)
    put_vec(4, total_of(grad_out * normed_2))
    put_vec(5, total_of(grad_out))
    grad_res = norm_back(grad_out, normed_2, inverse_2, gain_b)
    grad_branch[...] = grad_res.astype(bf16)
    put_vec(3, total_of(grad_branch[...].astype(f32)))
    for k in range(W):
        low = (nt(grad_branch[...], full_d[k]) * slope[k].astype(f32)).astype(bf16)
        grad_inner[k] = low
        grad_vec[k, :, cuts[6] : cuts[6] + width] = total_of(low.astype(f32))
    run("seq_f2")
    grad_hidden = grad_res
    for k, span in enumerate(spans):
        grad_hidden = grad_hidden + nt(grad_inner[k], full_i[:, :, span].reshape(width, width))
    put_vec(1, total_of(grad_hidden * normed_1))
    put_vec(2, total_of(grad_hidden))
    grad_first = norm_back(grad_hidden, normed_1, inverse_1, gain_a)
    res[...] = grad_first
    grad_attn[...] = grad_first.astype(bf16)
    put_vec(0, total_of(grad_attn[...].astype(f32)))
    grad_ctx = nt(grad_attn[...], full_o[...].reshape(width, width)).astype(bf16)
    for q in zz:
        cx(q).wait_send()
    d_send = ctx_send
    for j in range(W):
        d_send[j] = grad_ctx[:, j * group : (j + 1) * group]

    def da(q):
        return remote(d_send.at[q], d_recv.at[z], da_s.at[q], da_r.at[z], (s, c, q))

    def da_in(q):
        return remote(d_send.at[q], d_recv.at[q], da_s.at[q], da_r.at[q], (s, c, q))

    for q in zz:
        da(q).start()
    d_recv[z] = d_send[z]

    kt[...] = kx[...].astype(f32).T.astype(bf16)
    dk[...] = jnp.zeros_like(dk)
    dv[...] = jnp.zeros_like(dv)
    run("seq_b")

    def attend_back(step, carry):
        i = lax.div(step, heads)
        h = lax.rem(step, heads)
        b = lax.rem(z + i, W)

        @pl.when((h == 0) & (i > 0))
        def _():
            da_in(b).wait_recv()

        at = pl.ds(pl.multiple_of(b * rows, rows), rows)
        here = pl.ds(pl.multiple_of(h * head_dim, head_dim), head_dim)
        got = d_recv[b].astype(f32)
        got = jnp.concatenate([got, jnp.zeros((rows, LANES - group), f32)], axis=1)
        mask = (lane >= h * head_dim) & (lane < (h + 1) * head_dim)
        grad = jnp.where(mask, got, 0.0).astype(bf16)

        @pl.when(h == 0)
        def _():
            both = got.T[:group] * att_t[:, at]
            for k in range(heads):
                deltas[k] = jnp.sum(both[k * head_dim : (k + 1) * head_dim], axis=0, keepdims=True)

        delta = deltas[h]
        query = qx[pl.ds(pl.multiple_of(h * block + b * rows, rows), rows), :]
        log_mass = lse[h, :, at]
        acc = None
        for n in range(n_chunks):
            span = slice(n * chunk, (n + 1) * chunk)
            weights = jnp.exp(nt(kx[span, :], query) - log_mass)
            grad_weights = nt(vv[span, :], grad)
            grad_scores = (weights * (grad_weights - delta)).astype(bf16)
            dv[span, :] += nn(weights.astype(bf16), grad)
            dk[span, :] += nn(grad_scores, query)
            add = nn(kt[here, span], grad_scores)
            acc = add if acc is None else acc + add
        dq_t[here, at] = acc * dims["scale"]

        for when, name, a in dims["moves_b"]:
            @pl.when(step == when)
            def _():
                stages[name](a)

        return carry

    lax.fori_loop(0, W * heads, attend_back, 0)

    def kv_move():
        return remote(kv_send, kv_recv, kb_s.at[0], kb_r.at[0], sib)

    other = pl.ds(pl.multiple_of((1 - c) * block, block), block)
    own = pl.ds(pl.multiple_of(c * block, block), block)
    kv_send[:block] = dk[other, :].astype(bf16)
    kv_send[block:] = dv[other, :].astype(bf16)
    kv_move().start()
    run("seq_k")
    pad = jnp.zeros((block, LANES - group), bf16)
    dqkv[:, :LANES] = jnp.concatenate([dq_t[...].T.astype(bf16), pad], axis=1)
    kv_move().wait_recv()
    keep = lane < group
    for m, ref in ((0, dk), (1, dv)):
        whole = ref[own, :] + kv_recv[m * block : (m + 1) * block].astype(f32)
        dqkv[:, (m + 1) * LANES : (m + 2) * LANES] = jnp.where(keep, whole, 0.0).astype(bf16)

    def rx_out(d, step, lane_):
        slot = jnp.where((lane_ == 1) & (d == z - 1 if step < 0 else d == z), W, d)
        return remote(px.at[d], rx.at[slot], rx_s.at[d], rx_r.at[slot], (s, c, z + step))

    def rx_in(slot):
        return remote(px.at[0], rx.at[slot], rx_s.at[0], rx_r.at[slot], (s, c, z))

    def make(d):
        at = pl.ds(pl.multiple_of(d * rows, rows), rows)
        return nt(dqkv[at, :], wcol[...])

    def line(k):
        far = W - 1 - k // 2
        right = jnp.where(z < W // 2, k % 2 == 0, k % 2 == 1)
        d = jnp.where(right, far, W - 1 - far)

        @pl.when(right & (d > z))
        def _():
            px[d] = make(d).astype(bf16)

            @pl.when(z > 0)
            def _():
                rx_in(d).wait_recv()
                px[d] = (px[d].astype(f32) + rx[d].astype(f32)).astype(bf16)

            rx_out(d, 1, 0).start()

        @pl.when(jnp.logical_not(right) & (d < z))
        def _():
            px[d] = make(d).astype(bf16)

            @pl.when(z < W - 1)
            def _():
                rx_in(d).wait_recv()
                px[d] = (px[d].astype(f32) + rx[d].astype(f32)).astype(bf16)

            rx_out(d, -1, 1).start()

    def grad_proj(part):
        made = None
        for j in range(W):
            add = tn(toks[j], dqkv[j * rows : (j + 1) * rows, :])
            made = add if made is None else made + add
        made = made.astype(bf16)
        for j in range(W):
            w_send[j] = made[j * group : (j + 1) * group]
        core_move(last).start()

    def bcore():
        return remote(bc.at[c], bc.at[c], bp_s.at[0], bp_r.at[0], sib)

    def bplane(k):
        return remote(bs.at[s], bs.at[s], bp_s.at[k], bp_r.at[k], (s ^ k, c, z))

    def b_core(part):
        sums = nn(jnp.ones((8, block), bf16), dqkv[...])[0:1]
        bc[c] = jnp.concatenate([sums[:, :LANES], sums[:, 2 * LANES :]], axis=1)
        bcore().start()

    def b_plane(part):
        bcore().wait_recv()
        bs[s] = bc[0] + bc[1]
        for k in (1, 2, 3):
            bplane(k).start()

    def own_rows(part):
        res[...] += make(z)

    stages.update({
        DO_GRAD_PROJ: grad_proj, DO_LINE: line, DO_B_CORE: b_core, DO_B_PLANE: b_plane, DO_OWN_ROWS: own_rows,
    })
    run("seq_l")

    @pl.when(z > 0)
    def _():
        rx_in(z).wait_recv()
        res[...] += rx[z].astype(f32)

    @pl.when(z < W - 1)
    def _():
        rx_in(W).wait_recv()
        res[...] += rx[W].astype(f32)

    g_tok[...] = res[...].astype(bf16)
    run("seq_g")
    for k in (1, 2, 3):
        bplane(k).wait_recv()
    tot = (bs[0] + bs[1]) + (bs[2] + bs[3])
    g_b[...] = tot
    bcore().wait_send()
    for k in (1, 2, 3):
        bplane(k).wait_send()
    kv_move().wait_send()
    for q in zz:
        da(q).wait_send()
    for j in range(W):
        @pl.when(j > z)
        def _():
            rx_out(j, 1, 0).wait_send()

        @pl.when(j < z)
        def _():
            rx_out(j, -1, 1).wait_send()

    for a in range(6):
        gc_in(a).wait_recv()
        drain(a)


    @pl.when(z + 1 < W)
    def _():
        for j in range(W):
            @pl.when(j <= z)
            def _():
                tok_copy(j, 1, 0).wait_send()

    @pl.when(z > 0)
    def _():
        for j in range(W):
            @pl.when(j >= z)
            def _():
                tok_copy(j, -1, 1).wait_send()

    for q in zz:
        seg_out(q).wait_send()
        vec_out(q).wait_send()
        for k in range(4):
            wp(q, k).wait_send()


def layer_call(dims, *operands):
    S, W, heads = dims["S"], dims["W"], dims["heads"]
    tokens, w_i = operands[0], operands[-2]
    rows, width = tokens.shape
    group = width // W
    block = rows * W
    total = 2 * block
    ff = w_i.shape[1]
    f32, bf16 = jnp.float32, jnp.bfloat16
    vm = pl.BlockSpec(memory_space=pltpu.VMEM)
    hb = pl.BlockSpec(memory_space=pl.ANY)
    dma = pltpu.SemaphoreType.DMA
    shape = jax.ShapeDtypeStruct
    vmem = pltpu.VMEM
    n_vec = dims["n_vec"]
    n_d, n_i = ff // W // 2, group // 2
    halves = ((n_d // 2, width),) * 2 + ((n_i, ff // 2),) * 2 + ((group, width // 2),) * 2
    pieces = ((n_d // 8, width),) * 2 + ((n_i, ff // 8),) * 2 + ((group // S, width // 2),) * 2
    return pl.pallas_call(
        partial(layer_kernel, dims),
        name="layer",
        out_shape=(
            shape((rows, width), bf16),
            shape((rows, width), bf16),
            shape((ff // W, width), bf16),
            shape((group, ff), bf16),
            shape((group, width), bf16),
            shape((W, group, 3 * LANES), bf16),
            shape((1, n_vec), f32),
            shape((1, 2 * LANES), f32),
        ),
        in_specs=[vm] * 15 + [hb] * 3,
        out_specs=tuple([vm] * 8),
        scratch_shapes=[
            vmem((W, rows, width), bf16),
            vmem((width, 3 * LANES), bf16),
            vmem((heads * block, LANES), bf16),
            vmem((total, LANES), bf16),
            vmem((total, LANES), bf16),
            vmem((group, block), f32),
            vmem((heads, 1, block), f32),
            vmem((rows, width), bf16),
            vmem((rows, width), f32),
            vmem((W, rows, width), bf16),
            vmem((rows, width), bf16),
            vmem((rows, width), bf16),
            vmem((W, rows, width), bf16),
            vmem((rows, width), bf16),
            vmem((W, 1, n_vec), f32),
            vmem((W, group, width), bf16),
            vmem((W, group, ff), bf16),
            vmem((W, ff // W, width), bf16),
            vmem((W, 1, n_vec), f32),
            vmem((W, rows, width), dims["slope"]),
            vmem((W, 1, rows), f32),
            vmem((W, group, 3 * LANES), bf16),
            vmem((LANES, total), bf16),
            vmem((total, rows), f32),
            vmem((total, rows), f32),
            vmem((W, rows, group), bf16),
            vmem((W, rows, group), bf16),
            vmem((W, rows, group), bf16),
            vmem((block, 3 * LANES), bf16),
            vmem((2 * block, LANES), bf16),
            vmem((W + 1, rows, width), bf16),
            [vmem((W,) + h, bf16) for h in halves]
            + [vmem((2, W) + p, bf16) for p in pieces]
            + [vmem((W,) + p, bf16) for p in pieces] * 2,
            vmem((heads, 1, rows), f32),
            vmem((W, 1, n_vec), f32),
            vmem((2, W, 1, n_vec), f32),
            vmem((S, W, 1, n_vec), f32),
            vmem((W, 1, n_vec), f32),
            vmem((2, 1, 2 * LANES), f32),
            vmem((S, 1, 2 * LANES), f32),
            dma((2, W)), dma((W,)), dma((2, W)), dma((2, W)), dma((W,)), dma((W,)),
            dma((W, 4)), dma((W, 4)), dma((2, W)), dma((2, W)), dma((W,)), dma((W,)),
            dma((5, W)), dma((5, W)), dma((5, W, 4)), dma((5, W, 4)), dma((5, W)), dma((5, W)),
            dma((3,)),
            dma((W,)), dma((W,)), dma((1,)), dma((1,)), dma((W,)), dma((W + 1,)),
            dma((6,)), dma((6,)), dma((6, 4)), dma((6, 4)), dma((6, 2)), dma((6, 2)),
            dma((6, W)), dma((6, W)), dma((6, 4)), dma((6, 4)), dma((6,)), dma((6,)),
            dma((4 + W,)), dma((4 + W,)), dma((4,)), dma((4,)),
        ],
        compiler_params=pltpu.CompilerParams(
            collective_id=1, has_side_effects=True, vmem_limit_bytes=VMEM_LIMIT
        ),
    )(*operands)


def finish_kernel(dims, result, g_tok, gd, gi, go, gq, vec, g_b,
                  o_res, o_tok, o_q, o_bq, o_k, o_v, o_bv, o_o, o_s0, o_s1, o_s2, o_i, o_s3, o_d, o_s4, o_s5, o_s6):
    f32 = jnp.float32
    W = dims["W"]
    group = o_bq.shape[0]
    o_res[0] = result[...]
    o_tok[0] = g_tok[...]
    o_d[...] = gd[...].astype(f32)
    o_i[...] = gi[...].astype(f32)
    o_o[...] = go[...].astype(f32)
    for j in range(W):
        for m, ref in enumerate((o_q, o_k, o_v)):
            ref[:, j * group : (j + 1) * group] = gq[j, :, m * LANES : m * LANES + group].astype(f32)
    o_bq[...] = g_b[0, :group]
    o_bv[...] = g_b[0, LANES : LANES + group]
    for ref, lo in zip((o_s0, o_s1, o_s2, o_s4, o_s5, o_s6, o_s3), dims["cuts"]):
        ref[...] = vec[0, lo : lo + ref.shape[0]]


def finish_call(dims, result, g_tok, gd, gi, go, gq, vec, g_b):
    f32, bf16 = jnp.float32, jnp.bfloat16
    W, steps = dims["W"], 4
    rows, width = result.shape
    group = width // W
    ff = gi.shape[1]
    down = gd.shape[0]
    shape = jax.ShapeDtypeStruct
    small, mat = shape((group,), f32), shape((group, width), f32)

    def cut(n, m):
        return pl.BlockSpec((n // steps, m), lambda k: (k, 0))

    def deep(d, n, m):
        return pl.BlockSpec((d, n // steps, m), lambda k: (0, k, 0))

    def flat(n):
        return pl.BlockSpec((n,), lambda k: (0,))

    def whole(a):
        return pl.BlockSpec(a.shape, lambda k: (0, 0))

    one, sheet = flat(group), cut(group, width)
    return pl.pallas_call(
        partial(finish_kernel, dims),
        name="finish",
        grid=(steps,),
        out_shape=(shape((1, rows, width), bf16), shape((1, rows, width), bf16), mat, small, mat, mat, small, mat,
                   small, small, small, shape((group, ff), f32), shape((ff // W,), f32), shape((down, width), f32),
                   small, small, small),
        in_specs=[cut(rows, width), cut(rows, width), cut(down, width), cut(group, ff), sheet,
                  deep(W, group, gq.shape[2]), whole(vec), whole(g_b)],
        out_specs=(deep(1, rows, width), deep(1, rows, width), sheet, one, sheet, sheet, one, sheet, one, one, one,
                   cut(group, ff), flat(ff // W), cut(down, width), one, one, one),
        compiler_params=pltpu.CompilerParams(vmem_limit_bytes=VMEM_LIMIT),
    )(result, g_tok, gd, gi, go, gq, vec, g_b)


def fast_device(dims, tokens, segment_ids, w_query, b_query, w_key, w_value, b_value, w_out, b_out, gain_attn,
                shift_attn, w_in, b_in, w_down, b_down, gain_ffn, shift_ffn, cotangent):
    made = layer_call(dims, tokens[0], segment_ids, w_query, w_key, w_value, b_query, b_value, b_out, gain_attn, shift_attn,
                      b_in, b_down, gain_ffn, shift_ffn, cotangent, w_out, w_in, w_down)
    return finish_call(dims, *made)


def plan(mesh):
    return dict(
        S=mesh.shape["seq"], W=mesh.shape["wsh"], heads=HEADS // mesh.shape["wsh"], scale=0.125, chunk=512,
        cuts=(0, 256, 512, 768, 1024, 1280, 1536), n_vec=2304, density=1.0 / math.sqrt(2.0 * math.pi), slope=jnp.bfloat16,
        first=[],
        seq_t=[
            (DO_START, 0), (DO_FORWARD, 1), (DO_QKV_Z, 0), (DO_START, 1), (DO_FORWARD, 2), (DO_QKV_PLANE, 0),
            (DO_QKV_CORE, 0), (DO_NEAR, 1), (DO_PLANE, 1), (DO_NEAR, 2), (DO_START, 3), (DO_CROSS, 1),
            (DO_PLANE, 0), (DO_START, 2), (DO_NEAR, 0), (DO_FORWARD, 3), (DO_NEAR, 3), (DO_CROSS, 0),
        ],
        moves_a=[
            (0, DO_PLANE, 3), (1, DO_START, 4), (2, DO_PLANE, 2), (2, DO_CORE, 1), (4, DO_CROSS, 3),
            (5, DO_CORE, 0), (6, DO_PLANE, 4), (7, DO_CROSS, 2), (10, DO_CORE, 3), (11, DO_CROSS, 4),
            (11, DO_CORE, 2),
        ],
        seq_f0=[
            (DO_CORE, 4),
        ],
        seq_f1=[],
        seq_f2=[
            (DO_WEIGHT_GRAD, 1), (DO_WEIGHT_GRAD, 0),
        ],
        seq_b=[
            (DO_VEC_CORE, 0), (DO_CORE_ADD, 1), (DO_X1_SEND, 1),
        ],
        moves_b=[
            (0, DO_WEIGHT_GRAD, 2), (0, DO_CORE_ADD, 0), (0, DO_X1_SEND, 0), (1, DO_WEIGHT_GRAD, 3),
            (2, DO_X1_FAR, 0), (2, DO_CORE_ADD, 4), (3, DO_X1_OWN, 0), (3, DO_CORE_ADD, 2), (3, DO_X1_SEND, 4),
            (5, DO_X2_ADD, 0), (5, DO_Z_SEND, 0), (5, DO_X1_FAR, 4), (5, DO_X1_FAR, 1), (5, DO_VEC_PLANE, 0),
            (6, DO_X1_OWN, 4), (6, DO_X1_SEND, 2), (6, DO_X2_ADD, 4), (7, DO_Z_SEND, 4), (8, DO_CORE_ADD, 3),
            (8, DO_X1_OWN, 1), (8, DO_X2_ADD, 1), (10, DO_Z_SEND, 1), (10, DO_Z_ADD, 0), (10, DO_VEC_Z, 0),
        ],
        seq_k=[
            (DO_X1_FAR, 2), (DO_X1_SEND, 3), (DO_G_SEND, 0), (DO_Z_ADD, 4),
        ],
        seq_l=[
            (DO_LINE, 0), (DO_X1_OWN, 2), (DO_GRAD_PROJ, 0), (DO_B_CORE, 0), (DO_CORE_ADD, 5), (DO_X1_SEND, 5),
            (DO_X1_FAR, 3), (DO_B_PLANE, 0), (DO_X2_ADD, 2), (DO_OWN_ROWS, 0), (DO_X1_OWN, 3), (DO_Z_SEND, 2),
            (DO_LINE, 1), (DO_Z_ADD, 1), (DO_X1_FAR, 5), (DO_LINE, 2), (DO_X1_OWN, 5), (DO_G_FORWARD, 0),
            (DO_X2_ADD, 5), (DO_G_SEND, 1), (DO_Z_SEND, 5), (DO_G_FORWARD, 1), (DO_G_SEND, 4), (DO_LINE, 3),
            (DO_X2_ADD, 3), (DO_LINE, 4), (DO_G_FORWARD, 4), (DO_VEC_END, 0), (DO_LINE, 5), (DO_Z_SEND, 3),
        ],
        seq_g=[
            (DO_Z_ADD, 2), (DO_G_CORE, 0), (DO_G_CORE, 1), (DO_G_SEND, 2), (DO_G_CORE, 4), (DO_Z_ADD, 5),
            (DO_G_SEND, 5), (DO_G_FORWARD, 2), (DO_G_FORWARD, 5), (DO_Z_ADD, 3), (DO_G_SEND, 3), (DO_G_CORE, 2),
            (DO_G_CORE, 5), (DO_G_FORWARD, 3), (DO_G_CORE, 3),
        ],
    )


def solution(mesh):
    fast = mesh.shape["seq"] == 4 and mesh.shape["ctx"] == 2 and HEADS % mesh.shape["wsh"] == 0
    return jax.shard_map(
        partial(fast_device, plan(mesh)) if fast else per_device,
        mesh=mesh,
        in_specs=(
            P("seq", ("ctx", "wsh"), None),
            P("seq", ("ctx", "wsh")),
            P("wsh", None),
            P("wsh"),
            P("wsh", None),
            P("wsh", None),
            P("wsh"),
            P("wsh", None),
            P("wsh"),
            P("wsh"),
            P("wsh"),
            P("wsh", None),
            P("wsh"),
            P("wsh", None),
            P("wsh"),
            P("wsh"),
            P("wsh"),
            P("seq", ("ctx", "wsh"), None),
        ),
        out_specs=(
            P("seq", ("ctx", "wsh"), None),
            P("seq", ("ctx", "wsh"), None),
            P("wsh", None),
            P("wsh"),
            P("wsh", None),
            P("wsh", None),
            P("wsh"),
            P("wsh", None),
            P("wsh"),
            P("wsh"),
            P("wsh"),
            P("wsh", None),
            P("wsh"),
            P("wsh", None),
            P("wsh"),
            P("wsh"),
            P("wsh"),
        ),
        check_vma=False,
    )
```
